32 devices in a mesh: dp: 8 (over z, x), fsdp: 4 (over y, core).
Axes of the slice: x: 2, y: 2, z: 4, core: 2. Of those that a mesh axis runs over, the one named last changes fastest.
Arguments:
- acts: bfloat16 [1024, 3072], P('dp'), may hold values from -6 to 6
- weight: bfloat16 [3072, 3072], P('dp', 'fsdp'), may hold values from -0.15625 to 0.15625
- block_mask: int32 [4, 12, 12], replicated, may hold values 0 or 1
- out_grad: bfloat16 [4, 1024, 3072], P(None, 'dp', 'fsdp'), may hold values from -6 to 6
Outputs:
- outputs: bfloat16 [4, 1024, 3072], P(None, 'dp', 'fsdp')
- grad_w: float32 [3072, 3072], P('dp', 'fsdp')
- grad_x: bfloat16 [1024, 3072], P('dp', 'fsdp')
The draws below stay inside these ranges and needn't reach their ends.
All inputs are finite; a program needn't handle non-finite values.
Results may differ from the reference program's by a relative error of at most 0.001.
Values may be sent and summed in bfloat16 or wider, within the bound.
No kernel may reach another device: no remote copies, remote signals or barrier semaphores. Data moves between devices by JAX's collectives and lax.ppermute only.
A program may use at most 128 MiB of HBM per device.

```python
import jax
import jax.numpy as jnp

D = 3072
DO = 3072
BS = 256
NSUB = 4
TOK_G = 128
TOKENS = 1024
KB = 12
OB = 12


def plant(values, stream_key, low, largest):
    shape = values.shape
    place = [jax.random.randint(jax.random.fold_in(stream_key, axis), (), 0, shape[axis]) for axis in range(len(shape))]
    values = values.at[tuple(place)].set(low)
    longest = shape.index(max(shape))
    place[longest] = (place[longest] + 1) % shape[longest]
    return values.at[tuple(place)].set(largest)


def with_spikes(entries, stream_key, source, target, parts, factor):
    def block_of(dim):
        return (jnp.arange(entries.shape[dim]) // (entries.shape[dim] // parts)).reshape((-1,) + (1,) * (entries.ndim - 1 - dim))

    near = jax.random.permutation(stream_key, parts)[block_of(target)]
    other_side = (block_of(target) + parts // 2) % parts
    return jnp.where((block_of(source) == near) | (block_of(source) == other_side), factor * entries, entries)


def levels(key, shape, shards, low, largest):
    factor_of, own = 1.0, jax.random.fold_in(key, 6)
    for axis_at, blocks in shards:
        steps = jnp.exp(jax.random.uniform(jax.random.fold_in(own, axis_at), (blocks,), jnp.float32, low / len(shards), largest / len(shards)))
        factor_of = factor_of * jnp.repeat(steps, shape[axis_at] // blocks).reshape([-1 if axis == axis_at else 1 for axis in range(len(shape))])
    return factor_of


def scatter_about(key, extent, width, limit, pieces=(), held_as=jnp.bfloat16):
    result = width * jax.random.normal(key, extent, jnp.float32)
    if pieces:
        result = result * levels(key, extent, pieces, -0.22, 0.18)
    return jnp.clip(result, -limit, limit).astype(held_as)


def bell_draw_with(stream_key, shape, scale, limit, shards, heavy, kind=jnp.bfloat16):
    entries = scale * jax.random.normal(stream_key, shape, jnp.float32)
    if shards:
        entries = entries * levels(stream_key, shape, shards, -0.22, 0.18)
    return jnp.clip(with_spikes(entries, jax.random.fold_in(stream_key, 3), *heavy), -limit, limit).astype(kind)


def setup_inputs(seed: int = 0) -> dict:
    seeds = jax.random.split(jax.random.key(seed), 5)
    acts = bell_draw_with(seeds[0], (TOKENS, D), 1.0, 6.0, ((0, 8),), (0, 1, 8, 2.0))
    weight = bell_draw_with(seeds[1], (D, DO), D ** -0.5, 0.15625, ((0, 8), (1, 4)), (1, 0, 8, 2.0))
    block_mask = plant((jax.random.randint(seeds[2], (NSUB, KB, OB), 0, 3) < 2).astype(jnp.int32), jax.random.fold_in(seeds[2], 1), 0, 1)
    out_grad = scatter_about(seeds[3], (NSUB, TOKENS, DO), 1.0, 6.0, ((1, 8), (2, 4)))
    return {"acts": acts, "weight": weight, "block_mask": block_mask, "out_grad": out_grad}


def expand(block_mask):
    grown = jnp.repeat(jnp.repeat(block_mask, BS, axis=1), BS, axis=2)
    return grown.astype(jnp.float32)


def reference(acts, weight, block_mask, out_grad):
    element_mask = expand(block_mask)
    masked = (element_mask * weight.astype(jnp.float32)[None]).astype(jnp.bfloat16)
    outputs = jnp.stack([jnp.dot(acts, masked[s], preferred_element_type=jnp.float32) for s in range(NSUB)]).astype(jnp.bfloat16)

    grad_w = jnp.zeros((D, DO), jnp.float32)
    for s in range(NSUB):
        grad_w = grad_w + element_mask[s] * jnp.dot(acts.T, out_grad[s], preferred_element_type=jnp.float32)
    grad_w = grad_w * (1.0 / TOK_G)

    grad_x = jnp.zeros((TOKENS, D), jnp.float32)
    for s in range(NSUB):
        grad_x = grad_x + jnp.dot(out_grad[s], masked[s].T, preferred_element_type=jnp.float32)
    return outputs, grad_w, grad_x.astype(jnp.bfloat16)
```

```python
import math

import jax
import jax.numpy as jnp
from jax import lax
from jax.sharding import PartitionSpec as P

BS = 256
TOK_G = 128
F32 = jnp.float32
BF16 = jnp.bfloat16


def on_device(acts, weight, block_mask, out_grad):
    nsub = block_mask.shape[0]
    rows, width = weight.shape
    tokens, depth = acts.shape
    dp = lax.axis_size("dp")
    nx = 2 if dp % 2 == 0 else 1
    nz = dp // nx
    me = lax.axis_index("dp")
    z, x = me // nx, me % nx
    first_col = lax.axis_index("fsdp") * width
    cw = math.gcd(width, BS)
    nch = width // cw

    def swap_x(a):
        return lax.ppermute(a, "dp", [(d, d ^ 1) for d in range(dp)])

    def shift_z(a, step, senders):
        pairs = [(i * nx + j, (i + step) * nx + j) for i in senders for j in range(nx)]
        return lax.ppermute(a, "dp", pairs)

    acts_by = acts.reshape(tokens, nz, nx, rows)
    mine = lax.dynamic_index_in_dim(acts_by, x, 2, keepdims=False)
    other = lax.dynamic_index_in_dim(acts_by, 1 - x, 2, keepdims=False)

    col_blocks = (first_col + jnp.arange(nch, dtype=jnp.int32) * cw) // BS
    chunk_mask = jnp.take(block_mask, col_blocks, axis=2)
    row_mask = jnp.repeat(chunk_mask, BS, axis=1).reshape(nsub, nz, nx, rows, nch).astype(BF16)
    row_mask_mine = lax.dynamic_index_in_dim(row_mask, x, 2, keepdims=False)
    row_mask_other = lax.dynamic_index_in_dim(row_mask, 1 - x, 2, keepdims=False)

    groups = [[i * nx + j for i in range(nz)] for j in range(nx)]
    halves = 2
    hr = rows // halves
    weight_own = [
        lax.all_gather(weight[h * hr : (h + 1) * hr], "dp", axis_index_groups=groups, axis=0)
        for h in range(halves)
    ]

    acts_pair = jnp.concatenate([mine, swap_x(other)], axis=0).reshape(2 * tokens, nz * rows)
    grads = []
    for j in range(nch):
        og = out_grad[:, :, j * cw : (j + 1) * cw]
        og_pair = jnp.concatenate([og, swap_x(og)], axis=1)
        lhs = acts_pair[None] * row_mask_mine[..., j].reshape(nsub, 1, nz * rows)
        part = jnp.einsum("stn,stc->nc", lhs, og_pair, preferred_element_type=F32)
        part = part.reshape(nz, rows, cw)
        up = None
        down = None
        for i in range(1, nz):
            send = lax.dynamic_index_in_dim(part, jnp.minimum(z + nz - i, nz - 1), 0, keepdims=False)
            up = shift_z(send if up is None else send + up, 1, range(0, i))
            send = lax.dynamic_index_in_dim(part, jnp.maximum(z - nz + i, 0), 0, keepdims=False)
            down = shift_z(send if down is None else send + down, -1, range(nz - i, nz))
        own = lax.dynamic_index_in_dim(part, z, 0, keepdims=False)
        if nz > 1:
            own = own + up + down
        grads.append(own * (1.0 / TOK_G))
    grad_w = jnp.concatenate(grads, axis=1)

    forward = jnp.zeros((nsub, tokens, width), F32)
    parts = []
    for h in range(halves):
        own = weight_own[h]
        peer = swap_x(own)
        pair = []
        for w, a, m in ((own, mine, row_mask_mine), (peer, other, row_mask_other)):
            m_h = m[:, :, h * hr : (h + 1) * hr]
            full = jnp.repeat(m_h, cw, axis=3)
            masked = (full * w[None]).reshape(nsub, nz * hr, width)
            a_h = a[:, :, h * hr : (h + 1) * hr].reshape(tokens, nz * hr)
            forward = forward + jnp.einsum("tn,snc->stc", a_h, masked, preferred_element_type=F32)
            pair.append(
                jnp.einsum("stc,snc->tn", out_grad, masked, preferred_element_type=F32).reshape(
                    tokens, nz, hr
                )
            )
        lo = jnp.where(x == 0, pair[0], pair[1])
        hi = jnp.where(x == 0, pair[1], pair[0])
        parts.append(jnp.stack([lo, hi], axis=2))
    outputs = forward.astype(BF16)
    input_part = jnp.stack(parts, axis=3).reshape(tokens, depth)
    grad_x = lax.psum_scatter(input_part, "fsdp", scatter_dimension=1, tiled=True).astype(BF16)
    return (outputs, grad_w, grad_x)


def solution(mesh):
    in_specs = (P("dp", None), P("dp", "fsdp"), P(), P(None, "dp", "fsdp"))
    out_specs = (P(None, "dp", "fsdp"), P("dp", "fsdp"), P("dp", "fsdp"))
    return jax.shard_map(
        on_device, mesh=mesh, in_specs=in_specs, out_specs=out_specs, check_vma=False
    )
```

```python
import math

import jax
import jax.numpy as jnp
from jax import lax
from jax.experimental import pallas as pl
from jax.experimental.pallas import tpu as pltpu
from jax.sharding import PartitionSpec as P

BS = 256
TOK_G = 128
LANES = 128
F32 = jnp.float32
BF16 = jnp.bfloat16
VMEM_BYTES = 40 * 1024 * 1024


def plain(acts, weight, block_mask, out_grad):
    width = weight.shape[1]
    kblocks = block_mask.shape[1]
    oblocks = block_mask.shape[2]
    first_col = lax.axis_index("fsdp") * width
    col_ids = (first_col + jnp.arange(width, dtype=jnp.int32)) // BS
    col_select = (col_ids[None, :] == jnp.arange(oblocks, dtype=jnp.int32)[:, None]).astype(F32)
    col_mask = jnp.einsum("skb,bc->skc", block_mask.astype(F32), col_select)
    full = lax.all_gather(weight, "dp", axis=0, tiled=True)
    row_ids = jnp.arange(full.shape[0], dtype=jnp.int32) // BS
    row_select = (row_ids[:, None] == jnp.arange(kblocks, dtype=jnp.int32)[None, :]).astype(F32)
    mask = jnp.einsum("nk,skc->snc", row_select, col_mask)
    masked = mask.astype(BF16) * full[None]
    forward = jnp.einsum("tn,snc->stc", acts, masked, preferred_element_type=F32)
    input_part = jnp.einsum("stc,snc->tn", out_grad, masked, preferred_element_type=F32)
    products = jnp.einsum("tn,stc->snc", acts, out_grad, preferred_element_type=F32)
    grad_w = lax.psum_scatter(
        jnp.sum(mask * products, axis=0) * (1.0 / TOK_G), "dp", scatter_dimension=0, tiled=True
    )
    grad_x = lax.psum_scatter(input_part, "fsdp", scatter_dimension=1, tiled=True).astype(BF16)
    return (forward.astype(BF16), grad_w, grad_x)


def weight_grad_part(acts_mine, acts_peer, og_mine, og_peer, block_mask, where, nx, rows, chunk):
    nsub, tokens, cw = og_mine.shape
    total = acts_mine.shape[1]

    def kernel(where_ref, mask_ref, am_ref, ap_ref, om_ref, op_ref, out_ref):
        x = where_ref[0]
        col = where_ref[1] + chunk
        rhs_m = om_ref[...].reshape(nsub * tokens, cw)
        rhs_p = op_ref[...].reshape(nsub * tokens, cw)
        for g in range(total // LANES):
            piece, inside = divmod(g * LANES, rows)
            block = ((piece * nx + x) * rows + inside) // BS
            at = slice(g * LANES, (g + 1) * LANES)
            tm = am_ref[:, at].T
            tp = ap_ref[:, at].T
            keep = [mask_ref[s, block, col].astype(F32) for s in range(nsub)]
            keep = [jnp.full(tm.shape, k).astype(BF16) for k in keep]
            lhs_m = jnp.concatenate([tm * k for k in keep], axis=1)
            lhs_p = jnp.concatenate([tp * k for k in keep], axis=1)
            out_ref[at, :] = jnp.dot(lhs_m, rhs_m, preferred_element_type=F32) + jnp.dot(
                lhs_p, rhs_p, preferred_element_type=F32
            )

    smem = pl.BlockSpec(memory_space=pltpu.SMEM)
    vmem = pl.BlockSpec(memory_space=pltpu.VMEM)
    return pl.pallas_call(
        kernel,
        out_shape=jax.ShapeDtypeStruct((total, cw), F32),
        in_specs=[smem, smem, vmem, vmem, vmem, vmem],
        out_specs=vmem,
        compiler_params=pltpu.CompilerParams(vmem_limit_bytes=VMEM_BYTES),
        cost_estimate=pl.CostEstimate(
            flops=4 * total * cw * nsub * tokens, bytes_accessed=6 * total * cw, transcendentals=0
        ),
        name="weight_grad_part",
    )(where, block_mask, acts_mine, acts_peer, og_mine, og_peer)


def forward_and_input(acts, w_mine, w_peer, og, so_far, block_mask, where, nx, chunk):
    nsub, tokens, cw = og.shape
    depth = acts.shape[1]
    nz, rows, _ = w_mine.shape
    per = rows // LANES

    def kernel(where_ref, mask_ref, acts_ref, wm_ref, wp_ref, og_ref, *rest):
        prev_ref = rest[0] if so_far is not None else None
        out_ref, gx_ref, acc, hilo = rest[-4:]
        x = where_ref[0]
        col = where_ref[1] + chunk
        acc[...] = jnp.zeros_like(acc)
        for b in range(depth // BS):
            total = jnp.zeros((tokens, cw), F32)
            for s in range(nsub):
                total = total + mask_ref[s, b, col].astype(F32) * og_ref[s].astype(F32)
            hi = total.astype(BF16)
            hilo[b, :tokens] = hi
            hilo[b, tokens:] = (total - hi.astype(F32)).astype(BF16)

        for side in range(2):
            w_ref = wm_ref if side == 0 else wp_ref
            xs = x if side == 0 else 1 - x
            for piece in range(nz):
                for g in range(per):
                    start = (piece * nx + xs) * rows + g * LANES
                    block = start // BS
                    at = pl.ds(pl.multiple_of(start, LANES), LANES)
                    w = w_ref[piece, g * LANES : (g + 1) * LANES, :]
                    prod = jnp.dot(acts_ref[:, at], w, preferred_element_type=F32)
                    for s in range(nsub):
                        acc[s] += mask_ref[s, block, col].astype(F32) * prod
                    two = lax.dot_general(
                        hilo[block], w, (((1,), (1,)), ((), ())), preferred_element_type=F32
                    )
                    gx = two[:tokens] + two[tokens:]
                    if prev_ref is not None:
                        gx = gx + prev_ref[:, at]
                    gx_ref[:, at] = gx
        out_ref[...] = acc[...].astype(BF16)

    smem = pl.BlockSpec(memory_space=pltpu.SMEM)
    vmem = pl.BlockSpec(memory_space=pltpu.VMEM)
    args = [where, block_mask, acts, w_mine, w_peer, og]
    if so_far is not None:
        args.append(so_far)
    return pl.pallas_call(
        kernel,
        out_shape=(
            jax.ShapeDtypeStruct((nsub, tokens, cw), BF16),
            jax.ShapeDtypeStruct((tokens, depth), F32),
        ),
        in_specs=[smem, smem] + [vmem] * (len(args) - 2),
        out_specs=(vmem, vmem),
        scratch_shapes=[
            pltpu.VMEM((nsub, tokens, cw), F32),
            pltpu.VMEM((depth // BS, 2 * tokens, cw), BF16),
        ],
        compiler_params=pltpu.CompilerParams(vmem_limit_bytes=VMEM_BYTES),
        cost_estimate=pl.CostEstimate(
            flops=6 * tokens * depth * cw, bytes_accessed=4 * depth * cw, transcendentals=0
        ),
        name="forward_and_input",
    )(*args)


def on_device(acts, weight, block_mask, out_grad):
    rows, width = weight.shape
    tokens, depth = acts.shape
    dp = lax.axis_size("dp")
    fsdp = lax.axis_size("fsdp")
    if rows % LANES or width % BS or dp % 2 or fsdp != 4 or tokens % LANES:
        return plain(acts, weight, block_mask, out_grad)
    nx = 2
    nz = dp // nx
    me = lax.axis_index("dp")
    z, x = me // nx, me % nx
    col0 = lax.axis_index("fsdp") * (width // BS)
    cw = BS
    nch = width // cw
    where = jnp.stack([x, col0]).astype(jnp.int32)

    def swap_x(a):
        return lax.ppermute(a, "dp", [(d, d ^ 1) for d in range(dp)])

    def swap_f(a, bit):
        return lax.ppermute(a, "fsdp", [(d, d ^ bit) for d in range(fsdp)])

    def shift_z(a, step, senders):
        pairs = [(i * nx + j, (i + step) * nx + j) for i in senders for j in range(nx)]
        return lax.ppermute(a, "dp", pairs)

    groups = [[i * nx + j for i in range(nz)] for j in range(nx)]
    weight_mine = [
        lax.all_gather(weight[:, j * cw : (j + 1) * cw], "dp", axis_index_groups=groups, axis=0)
        for j in range(nch)
    ]

    acts_by = acts.reshape(tokens, nz, nx, rows)
    mine = lax.dynamic_index_in_dim(acts_by, x, 2, keepdims=False).reshape(tokens, nz * rows)
    other = lax.dynamic_index_in_dim(acts_by, 1 - x, 2, keepdims=False).reshape(tokens, nz * rows)
    peer = swap_x(other)
    grads = []
    for j in range(nch):
        og = out_grad[:, :, j * cw : (j + 1) * cw]
        part = weight_grad_part(mine, peer, og, swap_x(og), block_mask, where, nx, rows, j)
        part = part.reshape(nz, rows, cw)
        up = None
        down = None
        for i in range(1, nz):
            send = lax.dynamic_index_in_dim(part, jnp.minimum(z + nz - i, nz - 1), 0, keepdims=False)
            up = shift_z(send if up is None else send + up, 1, range(0, i))
            send = lax.dynamic_index_in_dim(part, jnp.maximum(z - nz + i, 0), 0, keepdims=False)
            down = shift_z(send if down is None else send + down, -1, range(nz - i, nz))
        own = lax.dynamic_index_in_dim(part, z, 0, keepdims=False)
        if nz > 1:
            own = own + up + down
        grads.append(own * (1.0 / TOK_G))
    grad_w = jnp.concatenate(grads, axis=1)

    outs = []
    gx = None
    for j in range(nch):
        og = out_grad[:, :, j * cw : (j + 1) * cw]
        out, gx = forward_and_input(
            acts, weight_mine[j], swap_x(weight_mine[j]), og, gx, block_mask, where, nx, j
        )
        outs.append(out)
    outputs = jnp.concatenate(outs, axis=2)

    f = lax.axis_index("fsdp")
    y, c = f // 2, f % 2
    by = gx.reshape(tokens, 2, 2, depth // 4)
    half = lax.dynamic_index_in_dim(by, c, 2, keepdims=False) + swap_f(
        lax.dynamic_index_in_dim(by, 1 - c, 2, keepdims=False), 1
    )
    grad_x = lax.dynamic_index_in_dim(half, y, 1, keepdims=False) + swap_f(
        lax.dynamic_index_in_dim(half, 1 - y, 1, keepdims=False), 2
    )
    return (outputs, grad_w, grad_x.astype(BF16))


def solution(mesh):
    in_specs = (P("dp", None), P("dp", "fsdp"), P(), P(None, "dp", "fsdp"))
    out_specs = (P(None, "dp", "fsdp"), P("dp", "fsdp"), P("dp", "fsdp"))
    return jax.shard_map(
        on_device, mesh=mesh, in_specs=in_specs, out_specs=out_specs, check_vma=False
    )
```

```python
import jax
import jax.numpy as jnp
from jax import lax
from jax.experimental import pallas as pl
from jax.experimental.pallas import tpu as pltpu
from jax.sharding import PartitionSpec as P

BS = 256
TOK_G = 128
LANES = 128
F32 = jnp.float32
BF16 = jnp.bfloat16
VMEM_BYTES = 40 * 1024 * 1024


def plain(acts, weight, block_mask, out_grad):
    width = weight.shape[1]
    kblocks = block_mask.shape[1]
    oblocks = block_mask.shape[2]
    first_col = lax.axis_index("fsdp") * width
    col_ids = (first_col + jnp.arange(width, dtype=jnp.int32)) // BS
    col_select = (col_ids[None, :] == jnp.arange(oblocks, dtype=jnp.int32)[:, None]).astype(F32)
    col_mask = jnp.einsum("skb,bc->skc", block_mask.astype(F32), col_select)
    full = lax.all_gather(weight, "dp", axis=0, tiled=True)
    row_ids = jnp.arange(full.shape[0], dtype=jnp.int32) // BS
    row_select = (row_ids[:, None] == jnp.arange(kblocks, dtype=jnp.int32)[None, :]).astype(F32)
    mask = jnp.einsum("nk,skc->snc", row_select, col_mask)
    masked = mask.astype(BF16) * full[None]
    forward = jnp.einsum("tn,snc->stc", acts, masked, preferred_element_type=F32)
    input_part = jnp.einsum("stc,snc->tn", out_grad, masked, preferred_element_type=F32)
    products = jnp.einsum("tn,stc->snc", acts, out_grad, preferred_element_type=F32)
    grad_w = lax.psum_scatter(
        jnp.sum(mask * products, axis=0) * (1.0 / TOK_G), "dp", scatter_dimension=0, tiled=True
    )
    grad_x = lax.psum_scatter(input_part, "fsdp", scatter_dimension=1, tiled=True).astype(BF16)
    return (forward.astype(BF16), grad_w, grad_x)


def weight_grad_part(acts_own, acts_got, og_own, og_got, block_mask, where, rows, chunk):
    nsub, tokens, cw = og_own.shape
    cols = where_chunk(chunk, cw)
    got = len(og_got)

    def kernel(where_ref, mask_ref, *refs):
        acts_refs, og_refs = refs[: got + 1], refs[got + 1 : 2 * got + 2]
        outs = refs[2 * got + 2 :]
        z, x = where_ref[0], where_ref[1]
        col = where_ref[2] + cols
        rhs = [r[...].reshape(nsub * tokens, cw) for r in og_refs]
        for side in range(2):
            xs = x if side == 0 else 1 - x
            for g in range(rows // LANES):
                inside = xs * rows + g * LANES
                block = (z * 2 * rows + inside) // BS
                at = pl.ds(pl.multiple_of(inside, LANES), LANES)
                keep = [mask_ref[s, block, col].astype(F32) for s in range(nsub)]
                keep = [jnp.full((LANES, tokens), k).astype(BF16) for k in keep]
                total = None
                for a_ref, r in zip(acts_refs, rhs):
                    t = a_ref[:, at].T
                    lhs = jnp.concatenate([t * k for k in keep], axis=1)
                    term = jnp.dot(lhs, r, preferred_element_type=F32)
                    total = term if total is None else total + term
                outs[side][g * LANES : (g + 1) * LANES, :] = total * (1.0 / TOK_G)

    smem = pl.BlockSpec(memory_space=pltpu.SMEM)
    vmem = pl.BlockSpec(memory_space=pltpu.VMEM)
    shape = jax.ShapeDtypeStruct((rows, cw), F32)
    return pl.pallas_call(
        kernel,
        out_shape=(shape, shape),
        in_specs=[smem, smem] + [vmem] * (2 * got + 2),
        out_specs=(vmem, vmem),
        compiler_params=pltpu.CompilerParams(vmem_limit_bytes=VMEM_BYTES),
        cost_estimate=pl.CostEstimate(
            flops=4 * (got + 1) * rows * cw * nsub * tokens,
            bytes_accessed=8 * rows * cw,
            transcendentals=0,
        ),
        name="weight_grad_part",
    )(where, block_mask, acts_own, *acts_got, og_own, *og_got)


def where_chunk(first, cw):
    assert first // BS == (first + cw - 1) // BS
    return first // BS


def forward_and_input(acts, w_mine, w_peer, og, block_mask, where):
    nsub, tokens, width = og.shape
    depth = acts.shape[1]
    nz = len(w_mine)
    rows = w_mine[0].shape[0]
    per = rows // LANES

    def kernel(where_ref, mask_ref, acts_ref, og_ref, *rest):
        w_refs, (out_ref, gx_ref, acc, hilo) = rest[: 2 * nz], rest[2 * nz :]
        z, x = where_ref[0], where_ref[1]
        step = pl.program_id(0)
        col = where_ref[2] + step

        @pl.when(step == 0)
        def _():
            gx_ref[...] = jnp.zeros_like(gx_ref)

        acc[...] = jnp.zeros_like(acc)
        for b in range(depth // BS):
            total = jnp.zeros((tokens, BS), F32)
            for s in range(nsub):
                total = total + mask_ref[s, b, col].astype(F32) * og_ref[s].astype(F32)
            hi = total.astype(BF16)
            hilo[b, :tokens] = hi
            hilo[b, tokens:] = (total - hi.astype(F32)).astype(BF16)

        for i, w_ref in enumerate(w_refs):
            xs = x if i < nz else 1 - x
            owner = z ^ (i % nz)
            for g in range(per):
                start = (owner * 2 + xs) * rows + g * LANES
                block = start // BS
                at = pl.ds(pl.multiple_of(start, LANES), LANES)
                w = w_ref[g * LANES : (g + 1) * LANES, :]
                prod = jnp.dot(acts_ref[:, at], w, preferred_element_type=F32)
                for s in range(nsub):
                    acc[s] += mask_ref[s, block, col].astype(F32) * prod
                two = lax.dot_general(
                    hilo[block], w, (((1,), (1,)), ((), ())), preferred_element_type=F32
                )
                gx_ref[:, at] += two[:tokens] + two[tokens:]
        out_ref[...] = acc[...].astype(BF16)

    smem = pl.BlockSpec(memory_space=pltpu.SMEM)
    by_col = pl.BlockSpec((nsub, tokens, BS), lambda j: (0, 0, j))
    whole = pl.BlockSpec((tokens, depth), lambda j: (0, 0))
    return pl.pallas_call(
        kernel,
        grid=(width // BS,),
        out_shape=(
            jax.ShapeDtypeStruct((nsub, tokens, width), BF16),
            jax.ShapeDtypeStruct((tokens, depth), F32),
        ),
        in_specs=[smem, smem, whole, by_col]
        + [pl.BlockSpec((rows, BS), lambda j: (0, j))] * (2 * nz),
        out_specs=(by_col, whole),
        scratch_shapes=[
            pltpu.VMEM((nsub, tokens, BS), F32),
            pltpu.VMEM((depth // BS, 2 * tokens, BS), BF16),
        ],
        compiler_params=pltpu.CompilerParams(vmem_limit_bytes=VMEM_BYTES),
        cost_estimate=pl.CostEstimate(
            flops=6 * tokens * depth * width, bytes_accessed=4 * depth * width, transcendentals=0
        ),
        name="forward_and_input",
    )(where, block_mask, acts, og, *w_mine, *w_peer)


def on_device(acts, weight, block_mask, out_grad):
    rows, width = weight.shape
    tokens, depth = acts.shape
    dp = lax.axis_size("dp")
    fsdp = lax.axis_size("fsdp")
    if rows % LANES or width % BS or dp != 8 or fsdp != 4 or tokens % LANES:
        return plain(acts, weight, block_mask, out_grad)
    nx = 2
    me = lax.axis_index("dp")
    z, x = me // nx, me % nx
    f = lax.axis_index("fsdp")
    y, c = f // 2, f % 2
    where = jnp.stack([z, x, f * (width // BS)]).astype(jnp.int32)

    def swap_dp(a, bits):
        return lax.ppermute(a, "dp", [(d, d ^ bits) for d in range(dp)])

    def swap_x(a):
        return swap_dp(a, 1)

    def swap_z(a, k):
        return swap_dp(a, k * nx)

    def swap_f(a, bit):
        return lax.ppermute(a, "fsdp", [(d, d ^ bit) for d in range(fsdp)])

    def gather_z(a):
        two = swap_z(a, 2)
        one = swap_z(a, 1)
        return [a, one, two, swap_z(two, 1)]

    w_mine = gather_z(weight)
    w_peer = [swap_x(w) for w in w_mine]

    def acts_of(k):
        return lax.dynamic_slice_in_dim(acts, (z ^ k) * nx * rows, nx * rows, 1)

    acts_own = acts_of(0)
    acts_got = [swap_z(acts_of(k), k) for k in range(1, 4)]

    grads = []
    for first, cw in [(i * BS, BS) for i in range(width // BS)]:
        og = gather_z(out_grad[:, :, first : first + cw])
        keep, send = weight_grad_part(
            acts_own, acts_got, og[0], og[1:], block_mask, where, rows, first
        )
        grads.append(keep + swap_x(send))
    grad_w = jnp.concatenate(grads, axis=1)

    outputs, gx = forward_and_input(acts, w_mine, w_peer, out_grad, block_mask, where)

    by = gx.reshape(tokens, 2, 2, depth // 4)
    half = lax.dynamic_index_in_dim(by, c, 2, keepdims=False) + swap_f(
        lax.dynamic_index_in_dim(by, 1 - c, 2, keepdims=False), 1
    )
    grad_x = lax.dynamic_index_in_dim(half, y, 1, keepdims=False) + swap_f(
        lax.dynamic_index_in_dim(half, 1 - y, 1, keepdims=False), 2
    )
    return (outputs, grad_w, grad_x.astype(BF16))


def solution(mesh):
    in_specs = (P("dp", None), P("dp", "fsdp"), P(), P(None, "dp", "fsdp"))
    out_specs = (P(None, "dp", "fsdp"), P("dp", "fsdp"), P("dp", "fsdp"))
    return jax.shard_map(
        on_device, mesh=mesh, in_specs=in_specs, out_specs=out_specs, check_vma=False
    )
```

```python
import jax
import jax.numpy as jnp
from jax import lax
from jax.experimental import pallas as pl
from jax.experimental.pallas import tpu as pltpu
from jax.sharding import PartitionSpec as P

BS = 256
TOK_G = 128
LANES = 128
F32 = jnp.float32
BF16 = jnp.bfloat16
VMEM_BYTES = 40 * 1024 * 1024


def plain(acts, weight, block_mask, out_grad):
    width = weight.shape[1]
    kblocks = block_mask.shape[1]
    oblocks = block_mask.shape[2]
    first_col = lax.axis_index("fsdp") * width
    col_ids = (first_col + jnp.arange(width, dtype=jnp.int32)) // BS
    col_select = (col_ids[None, :] == jnp.arange(oblocks, dtype=jnp.int32)[:, None]).astype(F32)
    col_mask = jnp.einsum("skb,bc->skc", block_mask.astype(F32), col_select)
    full = lax.all_gather(weight, "dp", axis=0, tiled=True)
    row_ids = jnp.arange(full.shape[0], dtype=jnp.int32) // BS
    row_select = (row_ids[:, None] == jnp.arange(kblocks, dtype=jnp.int32)[None, :]).astype(F32)
    mask = jnp.einsum("nk,skc->snc", row_select, col_mask)
    masked = mask.astype(BF16) * full[None]
    forward = jnp.einsum("tn,snc->stc", acts, masked, preferred_element_type=F32)
    input_part = jnp.einsum("stc,snc->tn", out_grad, masked, preferred_element_type=F32)
    products = jnp.einsum("tn,stc->snc", acts, out_grad, preferred_element_type=F32)
    grad_w = lax.psum_scatter(
        jnp.sum(mask * products, axis=0) * (1.0 / TOK_G), "dp", scatter_dimension=0, tiled=True
    )
    grad_x = lax.psum_scatter(input_part, "fsdp", scatter_dimension=1, tiled=True).astype(BF16)
    return (forward.astype(BF16), grad_w, grad_x)


def pack_acts(a, lanes):
    t = a.shape[0]
    rest = a[:, lanes:].reshape(2, t // 2, 2, LANES)
    return jnp.concatenate(
        [a[:, :lanes]] + [jnp.concatenate([rest[h, :, i] for i in range(2) for h in range(2)], axis=1)]
    )


def unpack_acts(ref, first, t, g):
    if g < 4:
        return ref[first : first + t, g * LANES : (g + 1) * LANES]
    at = 2 * (g - 4)
    return jnp.concatenate(
        [
            ref[first + t : first + t + t // 2, (at + h) * LANES : (at + h + 1) * LANES]
            for h in range(2)
        ]
    )


def weight_grad_part(acts_own, acts_got, acts_swap, og, og_first, block_mask, where, rows, first):
    nsub = block_mask.shape[0]
    tokens = acts_own.shape[0]
    half = tokens // 2
    packed = half + half // 2
    cw = og[0].shape[-1]
    ng = len(og)

    def kernel(where_ref, mask_ref, own_ref, swap_ref, *refs):
        got_refs, og_refs = refs[: ng - 1], refs[ng - 1 : 2 * ng - 1]
        keep_ref, send_ref = refs[2 * ng - 1 :]
        z, x, core = where_ref[0], where_ref[1], where_ref[3]
        for g in range(2 * rows // LANES):
            side, inside = divmod(g * LANES, rows)
            block = (z * 2 * rows + g * LANES) // BS
            tiles = [own_ref[:, g * LANES : (g + 1) * LANES].T]
            for k, r in enumerate(got_refs):
                mine = unpack_acts(r, acts_first[k], half, g)
                other = unpack_acts(swap_ref, k * packed, half, g)
                low = jnp.where(core == 0, mine, other)
                high = jnp.where(core == 0, other, mine)
                tiles.append(jnp.concatenate([low, high]).T)
            for b in range(cw // BS):
                col = where_ref[2] + first // BS + b
                lanes = slice(b * BS, (b + 1) * BS)
                keep = [mask_ref[s, block, col].astype(F32) for s in range(nsub)]
                keep = [jnp.full((LANES, tokens), k).astype(BF16) for k in keep]
                total = None
                for t, r, r0 in zip(tiles, og_refs, og_first):
                    lhs = jnp.concatenate([t * k for k in keep], axis=1)
                    term = jnp.dot(
                        lhs, r[r0 : r0 + nsub * tokens, lanes], preferred_element_type=F32
                    )
                    total = term if total is None else total + term
                total = total * (1.0 / TOK_G)

                @pl.when(x == side)
                def _():
                    keep_ref[inside : inside + LANES, lanes] = total

                @pl.when(x != side)
                def _():
                    send_ref[inside : inside + LANES, lanes] = total

    acts_first = [nsub * tokens, 0, nsub * tokens]
    smem = pl.BlockSpec(memory_space=pltpu.SMEM)
    vmem = pl.BlockSpec(memory_space=pltpu.VMEM)
    shape = jax.ShapeDtypeStruct((rows, cw), F32)
    return pl.pallas_call(
        kernel,
        out_shape=(shape, shape),
        in_specs=[smem, smem] + [vmem] * (2 * ng + 1),
        out_specs=(vmem, vmem),
        compiler_params=pltpu.CompilerParams(vmem_limit_bytes=VMEM_BYTES),
        cost_estimate=pl.CostEstimate(
            flops=4 * ng * rows * cw * nsub * tokens,
            bytes_accessed=8 * rows * cw,
            transcendentals=0,
        ),
        name="weight_grad_part",
    )(where, block_mask, acts_own, acts_swap, *acts_got, *og)


def forward_and_input(acts, w_mine, w_peer, og, block_mask, where):
    nsub, tokens, width = og.shape
    depth = acts.shape[1]
    nz = len(w_mine)
    rows = w_mine[0].shape[0]
    per = rows // LANES

    def kernel(where_ref, mask_ref, acts_ref, og_ref, *rest):
        w_refs, (out_ref, gx_ref, acc, hilo) = rest[: 2 * nz], rest[2 * nz :]
        z, x = where_ref[0], where_ref[1]
        step = pl.program_id(0)
        col = where_ref[2] + step

        @pl.when(step == 0)
        def _():
            gx_ref[...] = jnp.zeros_like(gx_ref)

        acc[...] = jnp.zeros_like(acc)
        for b in range(depth // BS):
            total = jnp.zeros((tokens, BS), F32)
            for s in range(nsub):
                total = total + mask_ref[s, b, col].astype(F32) * og_ref[s].astype(F32)
            hi = total.astype(BF16)
            hilo[b, :tokens] = hi
            hilo[b, tokens:] = (total - hi.astype(F32)).astype(BF16)

        for i, w_ref in enumerate(w_refs):
            xs = x if i < nz else 1 - x
            owner = z ^ (i % nz)
            for g in range(per):
                start = (owner * 2 + xs) * rows + g * LANES
                block = start // BS
                at = pl.ds(pl.multiple_of(start, LANES), LANES)
                w = w_ref[g * LANES : (g + 1) * LANES, :]
                prod = jnp.dot(acts_ref[:, at], w, preferred_element_type=F32)
                for s in range(nsub):
                    acc[s] += mask_ref[s, block, col].astype(F32) * prod
                two = lax.dot_general(
                    hilo[block], w, (((1,), (1,)), ((), ())), preferred_element_type=F32
                )
                gx_ref[:, at] += two[:tokens] + two[tokens:]
        out_ref[...] = acc[...].astype(BF16)

    smem = pl.BlockSpec(memory_space=pltpu.SMEM)
    by_col = pl.BlockSpec((nsub, tokens, BS), lambda j: (0, 0, j))
    whole = pl.BlockSpec((tokens, depth), lambda j: (0, 0))
    return pl.pallas_call(
        kernel,
        grid=(width // BS,),
        out_shape=(
            jax.ShapeDtypeStruct((nsub, tokens, width), BF16),
            jax.ShapeDtypeStruct((tokens, depth), F32),
        ),
        in_specs=[smem, smem, whole, by_col]
        + [pl.BlockSpec((rows, BS), lambda j: (0, j))] * (2 * nz),
        out_specs=(by_col, whole),
        scratch_shapes=[
            pltpu.VMEM((nsub, tokens, BS), F32),
            pltpu.VMEM((depth // BS, 2 * tokens, BS), BF16),
        ],
        compiler_params=pltpu.CompilerParams(vmem_limit_bytes=VMEM_BYTES),
        cost_estimate=pl.CostEstimate(
            flops=6 * tokens * depth * width, bytes_accessed=4 * depth * width, transcendentals=0
        ),
        name="forward_and_input",
    )(where, block_mask, acts, og, *w_mine, *w_peer)


def on_device(acts, weight, block_mask, out_grad):
    rows, width = weight.shape
    tokens, depth = acts.shape
    dp = lax.axis_size("dp")
    fsdp = lax.axis_size("fsdp")
    if rows != 3 * LANES or width != 3 * BS or dp != 8 or fsdp != 4 or tokens != LANES:
        return plain(acts, weight, block_mask, out_grad)
    nx = 2
    me = lax.axis_index("dp")
    z, x = me // nx, me % nx
    f = lax.axis_index("fsdp")
    y, c = f // 2, f % 2
    where = jnp.stack([z, x, f * (width // BS), c]).astype(jnp.int32)

    def swap_dp(a, bits):
        return lax.ppermute(a, "dp", [(d, d ^ bits) for d in range(dp)])

    def swap_x(a):
        return swap_dp(a, 1)

    def swap_z(a, k):
        return swap_dp(a, k * nx)

    def swap_f(a, bit):
        return lax.ppermute(a, "fsdp", [(d, d ^ bit) for d in range(fsdp)])

    def gather_z(a):
        two = swap_z(a, 2)
        one = swap_z(a, 1)
        return [a, one, two, swap_z(two, 1)]

    w_mine = gather_z(weight)
    w_peer = [swap_x(w) for w in w_mine]

    def acts_of(k):
        return lax.dynamic_slice_in_dim(acts, (z ^ k) * nx * rows, nx * rows, 1)

    half = tokens // 2
    nsub = out_grad.shape[0]
    flat = nsub * tokens
    packed = half + half // 2
    wide = 2 * BS
    a1, a2, a3 = [
        pack_acts(lax.dynamic_slice_in_dim(acts_of(k), c * half, half, 0), wide) for k in (1, 2, 3)
    ]
    og_a = out_grad[:, :, :wide].reshape(flat, wide)
    og_b = out_grad[:, :, wide:].reshape(flat, width - wide)
    two_a = swap_z(jnp.concatenate([a2, og_a, a3]), 2)
    one_a = swap_z(jnp.concatenate([og_a, a1]), 1)
    three_a = swap_z(two_a[packed:], 1)
    b_own, b_one, b_two, b_three = gather_z(og_b)
    acts_swap = swap_f(
        jnp.concatenate([one_a[flat:], two_a[:packed], three_a[flat:]]), 1
    )
    acts_own = acts_of(0)
    acts_got = [one_a, two_a, three_a]
    grads = []
    for first, og, og_first in (
        (0, [og_a, one_a, two_a, three_a], [0, 0, packed, 0]),
        (wide, [b_own, b_one, b_two, b_three], [0, 0, 0, 0]),
    ):
        keep, send = weight_grad_part(
            acts_own, acts_got, acts_swap, og, og_first, block_mask, where, rows, first
        )
        grads.append(keep + swap_x(send))
    grad_w = jnp.concatenate(grads, axis=1)

    outputs, gx = forward_and_input(acts, w_mine, w_peer, out_grad, block_mask, where)

    by = gx.reshape(tokens, 2, 2, depth // 4)
    half = lax.dynamic_index_in_dim(by, c, 2, keepdims=False) + swap_f(
        lax.dynamic_index_in_dim(by, 1 - c, 2, keepdims=False), 1
    )
    grad_x = lax.dynamic_index_in_dim(half, y, 1, keepdims=False) + swap_f(
        lax.dynamic_index_in_dim(half, 1 - y, 1, keepdims=False), 2
    )
    return (outputs, grad_w, grad_x.astype(BF16))


def solution(mesh):
    in_specs = (P("dp", None), P("dp", "fsdp"), P(), P(None, "dp", "fsdp"))
    out_specs = (P(None, "dp", "fsdp"), P("dp", "fsdp"), P("dp", "fsdp"))
    return jax.shard_map(
        on_device, mesh=mesh, in_specs=in_specs, out_specs=out_specs, check_vma=False
    )
```

```python
import jax
import jax.numpy as jnp
from jax import lax
from jax.experimental import pallas as pl
from jax.experimental.pallas import tpu as pltpu
from jax.sharding import PartitionSpec as P

BS = 256
TOK_G = 128
LANES = 128
F32 = jnp.float32
BF16 = jnp.bfloat16
VMEM_BYTES = 40 * 1024 * 1024


def plain(acts, weight, block_mask, out_grad):
    width = weight.shape[1]
    kblocks = block_mask.shape[1]
    oblocks = block_mask.shape[2]
    first_col = lax.axis_index("fsdp") * width
    col_ids = (first_col + jnp.arange(width, dtype=jnp.int32)) // BS
    col_select = (col_ids[None, :] == jnp.arange(oblocks, dtype=jnp.int32)[:, None]).astype(F32)
    col_mask = jnp.einsum("skb,bc->skc", block_mask.astype(F32), col_select)
    full = lax.all_gather(weight, "dp", axis=0, tiled=True)
    row_ids = jnp.arange(full.shape[0], dtype=jnp.int32) // BS
    row_select = (row_ids[:, None] == jnp.arange(kblocks, dtype=jnp.int32)[None, :]).astype(F32)
    mask = jnp.einsum("nk,skc->snc", row_select, col_mask)
    masked = mask.astype(BF16) * full[None]
    forward = jnp.einsum("tn,snc->stc", acts, masked, preferred_element_type=F32)
    input_part = jnp.einsum("stc,snc->tn", out_grad, masked, preferred_element_type=F32)
    products = jnp.einsum("tn,stc->snc", acts, out_grad, preferred_element_type=F32)
    grad_w = lax.psum_scatter(
        jnp.sum(mask * products, axis=0) * (1.0 / TOK_G), "dp", scatter_dimension=0, tiled=True
    )
    grad_x = lax.psum_scatter(input_part, "fsdp", scatter_dimension=1, tiled=True).astype(BF16)
    return (forward.astype(BF16), grad_w, grad_x)


def pack_acts(a, lanes):
    t = a.shape[0]
    rest = a[:, lanes:].reshape(2, t // 2, 2, LANES)
    return jnp.concatenate(
        [a[:, :lanes]] + [jnp.concatenate([rest[h, :, i] for i in range(2) for h in range(2)], axis=1)]
    )


def unpack_acts(ref, first, t, g):
    if g < 4:
        return ref[first : first + t, g * LANES : (g + 1) * LANES]
    at = 2 * (g - 4)
    return jnp.concatenate(
        [
            ref[first + t : first + t + t // 2, (at + h) * LANES : (at + h + 1) * LANES]
            for h in range(2)
        ]
    )


def weight_grad_part(acts_in, og, og_first, block_mask, where, rows, first, acts_first):
    nsub = block_mask.shape[0]
    fresh = acts_first is not None
    tokens = acts_in[0].shape[0] if fresh else acts_in[0].shape[2]
    half = tokens // 2
    packed = half + half // 2
    cw = og[0].shape[-1]
    ng = len(og)

    def kernel(where_ref, mask_ref, *refs):
        acts_refs, og_refs = refs[: len(acts_in)], refs[len(acts_in) : len(acts_in) + ng]
        outs = refs[len(acts_in) + ng :]
        keep_ref, send_ref = outs[:2]
        z, x, core = where_ref[0], where_ref[1], where_ref[3]
        for g in range(2 * rows // LANES):
            side, inside = divmod(g * LANES, rows)
            block = (z * 2 * rows + g * LANES) // BS
            at = slice(g * LANES, (g + 1) * LANES)
            if fresh:
                own_ref, swap_ref, *got_refs = acts_refs
                tiles = [own_ref[:, at].T]
                for k, r in enumerate(got_refs):
                    mine = unpack_acts(r, acts_first[k], half, g)
                    other = unpack_acts(swap_ref, k * packed, half, g)
                    low = jnp.where(core == 0, mine, other)
                    high = jnp.where(core == 0, other, mine)
                    tiles.append(jnp.concatenate([low, high]).T)
                for k, t in enumerate(tiles):
                    outs[2][k, at, :] = t
            else:
                tiles = [acts_refs[0][k, at, :] for k in range(ng)]
            for b in range(cw // BS):
                col = where_ref[2] + first // BS + b
                lanes = slice(b * BS, (b + 1) * BS)
                keep = [mask_ref[s, block, col].astype(F32) for s in range(nsub)]
                keep = [jnp.full((LANES, tokens), k).astype(BF16) for k in keep]
                total = None
                for t, r, r0 in zip(tiles, og_refs, og_first):
                    lhs = jnp.concatenate([t * k for k in keep], axis=1)
                    term = jnp.dot(
                        lhs, r[r0 : r0 + nsub * tokens, lanes], preferred_element_type=F32
                    )
                    total = term if total is None else total + term
                total = total * (1.0 / TOK_G)

                @pl.when(x == side)
                def _():
                    keep_ref[inside : inside + LANES, lanes] = total

                @pl.when(x != side)
                def _():
                    send_ref[inside : inside + LANES, lanes] = total

    smem = pl.BlockSpec(memory_space=pltpu.SMEM)
    vmem = pl.BlockSpec(memory_space=pltpu.VMEM)
    shapes = [jax.ShapeDtypeStruct((rows, cw), F32)] * 2
    if fresh:
        shapes.append(jax.ShapeDtypeStruct((ng, 2 * rows, tokens), BF16))
    return pl.pallas_call(
        kernel,
        out_shape=tuple(shapes),
        in_specs=[smem, smem] + [vmem] * (len(acts_in) + ng),
        out_specs=(vmem,) * len(shapes),
        compiler_params=pltpu.CompilerParams(vmem_limit_bytes=VMEM_BYTES),
        cost_estimate=pl.CostEstimate(
            flops=4 * ng * rows * cw * nsub * tokens,
            bytes_accessed=8 * rows * cw,
            transcendentals=0,
        ),
        name="weight_grad_part",
    )(where, block_mask, *acts_in, *og)


def forward_and_input(acts, w_mine, w_peer, og, block_mask, where):
    nsub, tokens, width = og.shape
    depth = acts.shape[1]
    nz = len(w_mine)
    rows = w_mine[0].shape[0]
    per = rows // LANES
    two = BS // LANES

    def kernel(where_ref, mask_ref, acts_ref, og_ref, *rest):
        w_refs, (out_ref, gx_ref, acc, hilo) = rest[: 2 * nz], rest[2 * nz :]
        z, x = where_ref[0], where_ref[1]
        step = pl.program_id(0)
        col = where_ref[2] + step

        @pl.when(step == 0)
        def _():
            gx_ref[...] = jnp.zeros_like(gx_ref)

        acc[...] = jnp.zeros_like(acc)
        for b in range(depth // BS):
            total = jnp.zeros((tokens, BS), F32)
            for s in range(nsub):
                total = total + mask_ref[s, b, col].astype(F32) * og_ref[s].astype(F32)
            hi = total.astype(BF16)
            hilo[b, :tokens] = hi
            hilo[b, tokens:] = (total - hi.astype(F32)).astype(BF16)

        for k in range(nz):
            owner = z ^ k
            tiles = []
            for side in range(2):
                for g in range(per):
                    at = slice(g * LANES, (g + 1) * LANES)
                    tiles.append(jnp.where(x == side, w_refs[k][at, :], w_refs[nz + k][at, :]))
            for b in range(2 * per // two):
                block = owner * (2 * per // two) + b
                w = jnp.concatenate(tiles[b * two : (b + 1) * two])
                cols = pl.ds(pl.multiple_of(block * BS, BS), BS)
                prod = jnp.dot(acts_ref[:, cols], w, preferred_element_type=F32)
                for s in range(nsub):
                    acc[s] += mask_ref[s, block, col].astype(F32) * prod
                both = lax.dot_general(
                    hilo[block], w, (((1,), (1,)), ((), ())), preferred_element_type=F32
                )
                gx_ref[owner, :, b * BS : (b + 1) * BS] += both[:tokens] + both[tokens:]
        out_ref[...] = acc[...].astype(BF16)

    smem = pl.BlockSpec(memory_space=pltpu.SMEM)
    by_col = pl.BlockSpec((nsub, tokens, BS), lambda j: (0, 0, j))
    whole = pl.BlockSpec((tokens, depth), lambda j: (0, 0))
    by_owner = (nz, tokens, depth // nz)
    return pl.pallas_call(
        kernel,
        grid=(width // BS,),
        out_shape=(
            jax.ShapeDtypeStruct((nsub, tokens, width), BF16),
            jax.ShapeDtypeStruct(by_owner, F32),
        ),
        in_specs=[smem, smem, whole, by_col]
        + [pl.BlockSpec((rows, BS), lambda j: (0, j))] * (2 * nz),
        out_specs=(by_col, pl.BlockSpec(by_owner, lambda j: (0, 0, 0))),
        scratch_shapes=[
            pltpu.VMEM((nsub, tokens, BS), F32),
            pltpu.VMEM((depth // BS, 2 * tokens, BS), BF16),
        ],
        compiler_params=pltpu.CompilerParams(vmem_limit_bytes=VMEM_BYTES),
        cost_estimate=pl.CostEstimate(
            flops=36 * tokens * depth * width, bytes_accessed=4 * depth * width, transcendentals=0
        ),
        name="forward_and_input",
    )(where, block_mask, acts, og, *w_mine, *w_peer)


def on_device(acts, weight, block_mask, out_grad):
    rows, width = weight.shape
    tokens, depth = acts.shape
    dp = lax.axis_size("dp")
    fsdp = lax.axis_size("fsdp")
    if rows != 3 * LANES or width != 3 * BS or dp != 8 or fsdp != 4 or tokens != LANES:
        return plain(acts, weight, block_mask, out_grad)
    nx = 2
    me = lax.axis_index("dp")
    z, x = me // nx, me % nx
    f = lax.axis_index("fsdp")
    y, c = f // 2, f % 2
    where = jnp.stack([z, x, f * (width // BS), c]).astype(jnp.int32)

    def swap_dp(a, bits):
        return lax.ppermute(a, "dp", [(d, d ^ bits) for d in range(dp)])

    def swap_x(a):
        return swap_dp(a, 1)

    def swap_z(a, k):
        return swap_dp(a, k * nx)

    def swap_f(a, bit):
        return lax.ppermute(a, "fsdp", [(d, d ^ bit) for d in range(fsdp)])

    def after(a, *others):
        return lax.optimization_barrier((a, *others))[0]

    def acts_of(k):
        return lax.dynamic_slice_in_dim(acts, (z ^ k) * nx * rows, nx * rows, 1)

    half = tokens // 2
    nsub = out_grad.shape[0]
    flat = nsub * tokens
    packed = half + half // 2
    wide = 2 * BS

    w_two = swap_z(weight, 2)
    w_one = swap_z(weight, 1)
    a1, a2, a3 = [
        pack_acts(lax.dynamic_slice_in_dim(acts_of(k), c * half, half, 0), wide) for k in (1, 2, 3)
    ]
    og_a = out_grad[:, :, :wide].reshape(flat, wide)
    og_b = out_grad[:, :, wide:].reshape(flat, width - wide)
    two_a = swap_z(jnp.concatenate([a2, og_a, a3]), 2)
    one_a = swap_z(jnp.concatenate([og_a, a1]), 1)
    x_own = swap_x(weight)
    w_three = swap_z(after(w_two, one_a, x_own), 1)
    w_mine = [weight, w_one, w_two, w_three]
    w_peer = [x_own] + [swap_x(w) for w in w_mine[1:]]

    three_a = swap_z(two_a[packed:], 1)
    b_two = swap_z(og_b, 2)
    b_one = swap_z(og_b, 1)
    b_three = swap_z(b_two, 1)
    acts_swap = swap_f(
        jnp.concatenate([one_a[flat:], two_a[:packed], three_a[flat:]]), 1
    )
    keep_a, send_a, acts_t = weight_grad_part(
        [acts_of(0), acts_swap, one_a, two_a, three_a],
        [og_a, one_a, two_a, three_a],
        [0, 0, packed, 0],
        block_mask,
        where,
        rows,
        0,
        [flat, 0, flat],
    )
    got_a = swap_x(send_a)

    outputs, gx = forward_and_input(
        acts, w_mine, w_peer, after(out_grad, keep_a, b_two, b_one), block_mask, where
    )

    keep_b, send_b = weight_grad_part(
        [acts_t], [og_b, b_one, b_two, b_three], [0, 0, 0, 0], block_mask, where, rows, wide, None
    )
    grad_w = jnp.concatenate([keep_a + got_a, keep_b + swap_x(send_b)], axis=1)

    by = gx.reshape(2, 2, tokens, depth // 4)
    both = lax.dynamic_index_in_dim(by, c, 1, keepdims=False) + swap_f(
        lax.dynamic_index_in_dim(by, 1 - c, 1, keepdims=False), 1
    )
    grad_x = lax.dynamic_index_in_dim(both, y, 0, keepdims=False) + swap_f(
        lax.dynamic_index_in_dim(both, 1 - y, 0, keepdims=False), 2
    )
    return (outputs, grad_w, grad_x.astype(BF16))


def solution(mesh):
    in_specs = (P("dp", None), P("dp", "fsdp"), P(), P(None, "dp", "fsdp"))
    out_specs = (P(None, "dp", "fsdp"), P("dp", "fsdp"), P("dp", "fsdp"))
    return jax.shard_map(
        on_device, mesh=mesh, in_specs=in_specs, out_specs=out_specs, check_vma=False
    )
```

```python
import jax
import jax.numpy as jnp
from jax import lax
from jax.experimental import pallas as pl
from jax.experimental.pallas import tpu as pltpu
from jax.sharding import PartitionSpec as P

BS = 256
TOK_G = 128
LANES = 128
F32 = jnp.float32
BF16 = jnp.bfloat16
VMEM_BYTES = 40 * 1024 * 1024


def plain(acts, weight, block_mask, out_grad):
    width = weight.shape[1]
    kblocks = block_mask.shape[1]
    oblocks = block_mask.shape[2]
    first_col = lax.axis_index("fsdp") * width
    col_ids = (first_col + jnp.arange(width, dtype=jnp.int32)) // BS
    col_select = (col_ids[None, :] == jnp.arange(oblocks, dtype=jnp.int32)[:, None]).astype(F32)
    col_mask = jnp.einsum("skb,bc->skc", block_mask.astype(F32), col_select)
    full = lax.all_gather(weight, "dp", axis=0, tiled=True)
    row_ids = jnp.arange(full.shape[0], dtype=jnp.int32) // BS
    row_select = (row_ids[:, None] == jnp.arange(kblocks, dtype=jnp.int32)[None, :]).astype(F32)
    mask = jnp.einsum("nk,skc->snc", row_select, col_mask)
    masked = mask.astype(BF16) * full[None]
    forward = jnp.einsum("tn,snc->stc", acts, masked, preferred_element_type=F32)
    input_part = jnp.einsum("stc,snc->tn", out_grad, masked, preferred_element_type=F32)
    products = jnp.einsum("tn,stc->snc", acts, out_grad, preferred_element_type=F32)
    grad_w = lax.psum_scatter(
        jnp.sum(mask * products, axis=0) * (1.0 / TOK_G), "dp", scatter_dimension=0, tiled=True
    )
    grad_x = lax.psum_scatter(input_part, "fsdp", scatter_dimension=1, tiled=True).astype(BF16)
    return (forward.astype(BF16), grad_w, grad_x)


def weight_grad_part(acts_in, og, block_mask, where, rows, chunk):
    nsub = block_mask.shape[0]
    fresh = acts_in.ndim == 2
    tokens = acts_in.shape[0] if fresh else acts_in.shape[2]
    flat = nsub * tokens
    ng = len(og)
    per = rows // LANES

    def kernel(where_ref, mask_ref, acts_ref, *refs):
        og_refs, outs = refs[:ng], refs[ng:]
        z, x = where_ref[0], where_ref[1]
        for r in range(2):
            zz = z ^ (2 * r)
            for g in range(per):
                start = (zz * 2 + x) * rows + g * LANES
                block = start // BS
                at = slice(g * LANES, (g + 1) * LANES)
                dst = slice((r * per + g) * LANES, (r * per + g + 1) * LANES)
                if fresh:
                    here = pl.ds(pl.multiple_of(start, LANES), LANES)
                    there = pl.ds(pl.multiple_of(x * rows + g * LANES, LANES), LANES)
                    own_ref, one_ref, side_ref, both_ref = og_refs
                    tiles = [
                        acts_ref[:, here].T,
                        one_ref[flat + r * tokens : flat + (r + 1) * tokens, there].T,
                        side_ref[flat : flat + tokens, dst].T,
                        both_ref[flat : flat + tokens, dst].T,
                    ]
                    for k, t in enumerate(tiles):
                        outs[2][k, dst, :] = t
                else:
                    tiles = [acts_ref[k, dst, :] for k in range(ng)]
                col = where_ref[2] + chunk
                keep = [mask_ref[s, block, col].astype(F32) for s in range(nsub)]
                keep = [jnp.full((LANES, tokens), k).astype(BF16) for k in keep]
                total = None
                for t, o_ref in zip(tiles, og_refs):
                    lhs = jnp.concatenate([t * k for k in keep], axis=1)
                    rhs = o_ref[:flat, chunk * BS : (chunk + 1) * BS]
                    term = jnp.dot(lhs, rhs, preferred_element_type=F32)
                    total = term if total is None else total + term
                outs[r][at, :] = total * (1.0 / TOK_G)

    smem = pl.BlockSpec(memory_space=pltpu.SMEM)
    vmem = pl.BlockSpec(memory_space=pltpu.VMEM)
    shapes = [jax.ShapeDtypeStruct((rows, BS), F32)] * 2
    if fresh:
        shapes.append(jax.ShapeDtypeStruct((ng, 2 * rows, tokens), BF16))
    return pl.pallas_call(
        kernel,
        out_shape=tuple(shapes),
        in_specs=[smem, smem] + [vmem] * (1 + ng),
        out_specs=(vmem,) * len(shapes),
        compiler_params=pltpu.CompilerParams(vmem_limit_bytes=VMEM_BYTES),
        cost_estimate=pl.CostEstimate(
            flops=4 * ng * rows * BS * flat, bytes_accessed=8 * rows * BS, transcendentals=0
        ),
        name="weight_grad_part",
    )(where, block_mask, acts_in, *og)


def forward_and_input(acts, w_mine, w_peer, og, block_mask, where):
    nsub, tokens, width = og.shape
    depth = acts.shape[1]
    nz = len(w_mine)
    rows = w_mine[0].shape[0]
    per = rows // LANES
    two = BS // LANES

    def kernel(where_ref, mask_ref, acts_ref, og_ref, *rest):
        w_refs, (out_ref, gx_ref, acc, hilo) = rest[: 2 * nz], rest[2 * nz :]
        z, x = where_ref[0], where_ref[1]
        step = pl.program_id(0)
        col = where_ref[2] + step

        @pl.when(step == 0)
        def _():
            gx_ref[...] = jnp.zeros_like(gx_ref)

        acc[...] = jnp.zeros_like(acc)
        for b in range(depth // BS):
            total = jnp.zeros((tokens, BS), F32)
            for s in range(nsub):
                total = total + mask_ref[s, b, col].astype(F32) * og_ref[s].astype(F32)
            hi = total.astype(BF16)
            hilo[b, :tokens] = hi
            hilo[b, tokens:] = (total - hi.astype(F32)).astype(BF16)

        for k in range(nz):
            owner = z ^ k
            tiles = []
            for side in range(2):
                for g in range(per):
                    at = slice(g * LANES, (g + 1) * LANES)
                    tiles.append(jnp.where(x == side, w_refs[k][at, :], w_refs[nz + k][at, :]))
            for b in range(2 * per // two):
                block = owner * (2 * per // two) + b
                w = jnp.concatenate(tiles[b * two : (b + 1) * two])
                cols = pl.ds(pl.multiple_of(block * BS, BS), BS)
                prod = jnp.dot(acts_ref[:, cols], w, preferred_element_type=F32)
                for s in range(nsub):
                    acc[s] += mask_ref[s, block, col].astype(F32) * prod
                both = lax.dot_general(
                    hilo[block], w, (((1,), (1,)), ((), ())), preferred_element_type=F32
                )
                gx_ref[owner, :, b * BS : (b + 1) * BS] += both[:tokens] + both[tokens:]
        out_ref[...] = acc[...].astype(BF16)

    smem = pl.BlockSpec(memory_space=pltpu.SMEM)
    by_col = pl.BlockSpec((nsub, tokens, BS), lambda j: (0, 0, j))
    whole = pl.BlockSpec((tokens, depth), lambda j: (0, 0))
    by_owner = (nz, tokens, depth // nz)
    return pl.pallas_call(
        kernel,
        grid=(width // BS,),
        out_shape=(
            jax.ShapeDtypeStruct((nsub, tokens, width), BF16),
            jax.ShapeDtypeStruct(by_owner, F32),
        ),
        in_specs=[smem, smem, whole, by_col]
        + [pl.BlockSpec((rows, BS), lambda j: (0, j))] * (2 * nz),
        out_specs=(by_col, pl.BlockSpec(by_owner, lambda j: (0, 0, 0))),
        scratch_shapes=[
            pltpu.VMEM((nsub, tokens, BS), F32),
            pltpu.VMEM((depth // BS, 2 * tokens, BS), BF16),
        ],
        compiler_params=pltpu.CompilerParams(vmem_limit_bytes=VMEM_BYTES),
        cost_estimate=pl.CostEstimate(
            flops=36 * tokens * depth * width, bytes_accessed=4 * depth * width, transcendentals=0
        ),
        name="forward_and_input",
    )(where, block_mask, acts, og, *w_mine, *w_peer)


def on_device(acts, weight, block_mask, out_grad):
    rows, width = weight.shape
    tokens, depth = acts.shape
    dp = lax.axis_size("dp")
    fsdp = lax.axis_size("fsdp")
    if rows != 3 * LANES or width != 3 * BS or dp != 8 or fsdp != 4 or tokens != LANES:
        return plain(acts, weight, block_mask, out_grad)
    nx = 2
    me = lax.axis_index("dp")
    z, x = me // nx, me % nx
    f = lax.axis_index("fsdp")
    y, c = f // 2, f % 2
    where = jnp.stack([z, x, f * (width // BS), c]).astype(jnp.int32)

    def swap_dp(a, bits):
        return lax.ppermute(a, "dp", [(d, d ^ bits) for d in range(dp)])

    def swap_x(a):
        return swap_dp(a, 1)

    def swap_z(a, k):
        return swap_dp(a, k * nx)

    def swap_f(a, bit):
        return lax.ppermute(a, "fsdp", [(d, d ^ bit) for d in range(fsdp)])

    def after(a, *others):
        return lax.optimization_barrier((a, *others))[0]

    nsub = out_grad.shape[0]
    flat = nsub * tokens
    own = out_grad.reshape(flat, width)
    by_z = acts.reshape(tokens, dp // nx, nx * rows)

    def acts_of(k):
        return lax.dynamic_index_in_dim(by_z, z ^ k, 1, keepdims=False)

    def of_x(a, side):
        return lax.dynamic_slice_in_dim(a, side * rows, rows, 1)

    one = swap_z(jnp.concatenate([own, acts_of(1), acts_of(3)]), 1)
    side = swap_x(
        jnp.concatenate(
            [own, jnp.concatenate([of_x(acts_of(0), 1 - x), of_x(acts_of(2), 1 - x)], axis=1)]
        )
    )
    one = after(one, side)
    passed = [
        of_x(one[flat + r * tokens : flat + (r + 1) * tokens], 1 - x) for r in range(2)
    ]
    both = swap_x(jnp.concatenate([one[:flat], jnp.concatenate(passed, axis=1)]))

    w_two = swap_z(weight, 2)
    w_one = swap_z(weight, 1)
    w_three = swap_z(w_two, 1)
    w_mine = [weight, w_one, w_two, w_three]
    w_peer = [swap_x(after(weight, both))]

    og = [own, one, side, both]
    acts_in = acts
    grads = []
    for j in range(width // BS):
        ready = ((w_two,), (w_peer[0],), (w_peer[0], *[got for _, got in grads[:1]]))[j]
        keep, send, *made = weight_grad_part(
            acts_in, og, block_mask, after(where, *ready), rows, j
        )
        if made:
            acts_in = made[0]
        grads.append((keep, swap_z(send, 2)))
        w_peer.append(swap_x(after(w_mine[j + 1], keep)))
    grad_w = jnp.concatenate([keep + got for keep, got in grads], axis=1)

    outputs, gx = forward_and_input(
        acts, w_mine, w_peer, after(out_grad, grads[1][1], grads[2][1]), block_mask, where
    )

    by = gx.reshape(2, 2, tokens, depth // 4)
    pair = lax.dynamic_index_in_dim(by, c, 1, keepdims=False) + swap_f(
        lax.dynamic_index_in_dim(by, 1 - c, 1, keepdims=False), 1
    )
    grad_x = lax.dynamic_index_in_dim(pair, y, 0, keepdims=False) + swap_f(
        lax.dynamic_index_in_dim(pair, 1 - y, 0, keepdims=False), 2
    )
    return (outputs, grad_w, grad_x.astype(BF16))


def solution(mesh):
    in_specs = (P("dp", None), P("dp", "fsdp"), P(), P(None, "dp", "fsdp"))
    out_specs = (P(None, "dp", "fsdp"), P("dp", "fsdp"), P("dp", "fsdp"))
    return jax.shard_map(
        on_device, mesh=mesh, in_specs=in_specs, out_specs=out_specs, check_vma=False
    )
```

```python
import jax
import jax.numpy as jnp
from jax import lax
from jax.experimental import pallas as pl
from jax.experimental.pallas import tpu as pltpu
from jax.sharding import PartitionSpec as P

BS = 256
TOK_G = 128
LANES = 128
F32 = jnp.float32
BF16 = jnp.bfloat16
VMEM_BYTES = 40 * 1024 * 1024


def plain(acts, weight, block_mask, out_grad):
    width = weight.shape[1]
    kblocks = block_mask.shape[1]
    oblocks = block_mask.shape[2]
    first_col = lax.axis_index("fsdp") * width
    col_ids = (first_col + jnp.arange(width, dtype=jnp.int32)) // BS
    col_select = (col_ids[None, :] == jnp.arange(oblocks, dtype=jnp.int32)[:, None]).astype(F32)
    col_mask = jnp.einsum("skb,bc->skc", block_mask.astype(F32), col_select)
    full = lax.all_gather(weight, "dp", axis=0, tiled=True)
    row_ids = jnp.arange(full.shape[0], dtype=jnp.int32) // BS
    row_select = (row_ids[:, None] == jnp.arange(kblocks, dtype=jnp.int32)[None, :]).astype(F32)
    mask = jnp.einsum("nk,skc->snc", row_select, col_mask)
    masked = mask.astype(BF16) * full[None]
    forward = jnp.einsum("tn,snc->stc", acts, masked, preferred_element_type=F32)
    input_part = jnp.einsum("stc,snc->tn", out_grad, masked, preferred_element_type=F32)
    products = jnp.einsum("tn,stc->snc", acts, out_grad, preferred_element_type=F32)
    grad_w = lax.psum_scatter(
        jnp.sum(mask * products, axis=0) * (1.0 / TOK_G), "dp", scatter_dimension=0, tiled=True
    )
    grad_x = lax.psum_scatter(input_part, "fsdp", scatter_dimension=1, tiled=True).astype(BF16)
    return (forward.astype(BF16), grad_w, grad_x)


def weight_grad_part(acts, og, block_mask, where, rows, chunk, chunks):
    nsub = block_mask.shape[0]
    tokens = acts.shape[0]
    flat = nsub * tokens
    ng = len(og)
    per = rows // LANES
    width = og[0].shape[1]
    made = chunks * BS

    def kernel(where_ref, mask_ref, acts_ref, *refs):
        extra, og_refs, outs, tiles = refs[:3], refs[3 : 3 + ng], refs[3 + ng : -1], refs[-1]
        z, x = where_ref[0], where_ref[1]
        step = pl.program_id(0)
        col = where_ref[2] + chunk + step

        @pl.when(step == 0)
        def _():
            one_ref, side_ref, both_ref = extra
            for r in range(2):
                for g in range(per):
                    start = ((z ^ (2 * r)) * 2 + x) * rows + g * LANES
                    here = pl.ds(pl.multiple_of(start, LANES), LANES)
                    there = pl.ds(pl.multiple_of(x * rows + g * LANES, LANES), LANES)
                    dst = slice((r * per + g) * LANES, (r * per + g + 1) * LANES)
                    tiles[0, dst, :] = acts_ref[:, here].T
                    tiles[1, dst, :] = one_ref[r * tokens : (r + 1) * tokens, there].T
                    tiles[2, dst, :] = side_ref[:, dst].T
                    tiles[3, dst, :] = both_ref[:, dst].T

        for r in range(2):
            for g in range(per):
                block = (((z ^ (2 * r)) * 2 + x) * rows + g * LANES) // BS
                dst = slice((r * per + g) * LANES, (r * per + g + 1) * LANES)
                keep = [mask_ref[s, block, col].astype(F32) for s in range(nsub)]
                keep = [jnp.full((LANES, tokens), k).astype(BF16) for k in keep]
                total = None
                for k in range(ng):
                    t = tiles[k, dst, :]
                    lhs = jnp.concatenate([t * m for m in keep], axis=1)
                    term = jnp.dot(lhs, og_refs[k][...], preferred_element_type=F32)
                    total = term if total is None else total + term
                outs[r][g * LANES : (g + 1) * LANES, :] = total * (1.0 / TOK_G)

    smem = pl.BlockSpec(memory_space=pltpu.SMEM)
    out = pl.BlockSpec((rows, BS), lambda j: (0, j))
    return pl.pallas_call(
        kernel,
        grid=(chunks,),
        out_shape=(jax.ShapeDtypeStruct((rows, made), F32),) * 2,
        in_specs=[smem, smem, pl.BlockSpec(acts.shape, lambda j: (0, 0))]
        + [
            pl.BlockSpec((2 * tokens, width), lambda j: (flat // (2 * tokens), 0)),
            pl.BlockSpec((tokens, width), lambda j: (flat // tokens, 0)),
            pl.BlockSpec((tokens, width), lambda j: (flat // tokens, 0)),
        ]
        + [pl.BlockSpec((flat, BS), lambda j: (0, chunk + j))] * ng,
        out_specs=(out, out),
        scratch_shapes=[pltpu.VMEM((ng, 2 * rows, tokens), BF16)],
        compiler_params=pltpu.CompilerParams(vmem_limit_bytes=VMEM_BYTES),
        cost_estimate=pl.CostEstimate(
            flops=4 * ng * rows * made * flat, bytes_accessed=8 * rows * made, transcendentals=0
        ),
        name="weight_grad_part",
    )(where, block_mask, acts, *og[1:], *og)


def forward_and_input(acts, side, og, weights, block_mask, where):
    nsub, tokens, width = og.shape
    flat = nsub * tokens
    nz = len(weights)
    rows = weights[0].shape[0]
    per = rows // LANES

    def kernel(where_ref, mask_ref, acts_ref, sacts_ref, og_ref, sog_ref, *rest):
        w_refs, (keep_ref, send_ref, gx_ref, acc, hilo) = rest[:nz], rest[nz:]
        z, x = where_ref[0], where_ref[1]
        step = pl.program_id(0)
        col = where_ref[2] + step
        first = step == 0
        near = (1 - x).astype(F32)
        far = x.astype(F32)

        def keep_of(block):
            return [mask_ref[s, block, col].astype(F32) for s in range(nsub)]

        for k in range(nz):
            start = ((z ^ k) * 2 + x) * rows
            blocks = [start // BS, (start + rows - LANES) // BS]
            keeps = [keep_of(block) for block in blocks]
            for i in range(2):
                for t, ref in enumerate((og_ref, sog_ref)):
                    total = jnp.zeros((tokens, BS), F32)
                    for s in range(nsub):
                        if t == 0:
                            piece = ref[s]
                        else:
                            piece = ref[s * tokens : (s + 1) * tokens, :]
                        total = total + keeps[i][s] * piece.astype(F32)
                    hi = total.astype(BF16)
                    hilo[k, i, t * tokens : (t + 1) * tokens] = hi
                    hilo[k, i, (t + 2) * tokens : (t + 3) * tokens] = (
                        total - hi.astype(F32)
                    ).astype(BF16)
            prods = []
            for g in range(per):
                here = pl.ds(pl.multiple_of(start + g * LANES, LANES), LANES)
                there = slice((k // 2) * rows + g * LANES, (k // 2) * rows + (g + 1) * LANES)
                both = jnp.concatenate(
                    [acts_ref[:, here], sacts_ref[(k % 2) * tokens : (k % 2 + 1) * tokens, there]]
                )
                at = slice(g * LANES, (g + 1) * LANES)
                w = w_refs[k][at, :]
                prods.append(jnp.dot(both, w, preferred_element_type=F32))
                i = (0, x, 1)[g]
                four = lax.dot_general(
                    hilo[k, i], w, (((1,), (1,)), ((), ())), preferred_element_type=F32
                )
                term = four[: 2 * tokens] + four[2 * tokens :]
                gx_ref[z ^ k, :, at] = jnp.where(first, term, gx_ref[z ^ k, :, at] + term)
            low = prods[0] + near * prods[1]
            high = prods[2] + far * prods[1]
            for s in range(nsub):
                term = keeps[0][s] * low + keeps[1][s] * high
                acc[s] = term if k == 0 else acc[s] + term
        for s in range(nsub):
            keep_ref[s] = acc[s, :tokens]
            send_ref[0, s] = acc[s, tokens:]

    smem = pl.BlockSpec(memory_space=pltpu.SMEM)
    by_col = pl.BlockSpec((nsub, tokens, BS), lambda j: (0, 0, j))
    gx_shape = (nz, 2 * tokens, rows)
    assert per == 3
    return pl.pallas_call(
        kernel,
        grid=(width // BS,),
        out_shape=(
            jax.ShapeDtypeStruct((nsub, tokens, width), F32),
            jax.ShapeDtypeStruct((width // BS, nsub, tokens, BS), F32),
            jax.ShapeDtypeStruct(gx_shape, F32),
        ),
        in_specs=[
            smem,
            smem,
            pl.BlockSpec(acts.shape, lambda j: (0, 0)),
            pl.BlockSpec((2 * tokens, width), lambda j: (flat // (2 * tokens), 0)),
            by_col,
            pl.BlockSpec((flat, BS), lambda j: (0, j)),
        ]
        + [pl.BlockSpec((rows, BS), lambda j: (0, j))] * nz,
        out_specs=(
            by_col,
            pl.BlockSpec((1, nsub, tokens, BS), lambda j: (j, 0, 0, 0)),
            pl.BlockSpec(gx_shape, lambda j: (0, 0, 0)),
        ),
        scratch_shapes=[
            pltpu.VMEM((nsub, 2 * tokens, BS), F32),
            pltpu.VMEM((nz, 2, 4 * tokens, BS), BF16),
        ],
        compiler_params=pltpu.CompilerParams(vmem_limit_bytes=VMEM_BYTES),
        cost_estimate=pl.CostEstimate(
            flops=36 * tokens * nz * 2 * rows * width,
            bytes_accessed=4 * nz * 2 * rows * width,
            transcendentals=0,
        ),
        name="forward_and_input",
    )(where, block_mask, acts, side, og, side, *weights)


def on_device(acts, weight, block_mask, out_grad):
    rows, width = weight.shape
    tokens, depth = acts.shape
    dp = lax.axis_size("dp")
    fsdp = lax.axis_size("fsdp")
    if rows != 3 * LANES or width != 3 * BS or dp != 8 or fsdp != 4 or tokens != LANES:
        return plain(acts, weight, block_mask, out_grad)
    nx = 2
    me = lax.axis_index("dp")
    z, x = me // nx, me % nx
    f = lax.axis_index("fsdp")
    y, c = f // 2, f % 2
    where = jnp.stack([z, x, f * (width // BS), c]).astype(jnp.int32)

    def swap_dp(a, bits):
        return lax.ppermute(a, "dp", [(d, d ^ bits) for d in range(dp)])

    def swap_x(a):
        return swap_dp(a, 1)

    def swap_z(a, k):
        return swap_dp(a, k * nx)

    def swap_f(a, bit):
        return lax.ppermute(a, "fsdp", [(d, d ^ bit) for d in range(fsdp)])

    def after(a, *others):
        return lax.optimization_barrier((a, *others))[0]

    nsub = out_grad.shape[0]
    flat = nsub * tokens
    own = out_grad.reshape(flat, width)
    by_z = acts.reshape(tokens, dp // nx, nx * rows)

    def acts_of(k):
        return lax.dynamic_index_in_dim(by_z, z ^ k, 1, keepdims=False)

    def of_x(a, side):
        return lax.dynamic_slice_in_dim(a, side * rows, rows, 1)

    def for_other(k):
        return of_x(acts_of(k), 1 - x)

    one = swap_z(jnp.concatenate([own, acts_of(1), acts_of(3)]), 1)
    side = swap_x(
        jnp.concatenate(
            [own]
            + [jnp.concatenate([for_other(k), for_other(k + 2)], axis=1) for k in range(2)]
        )
    )
    one = after(one, side)
    passed = [
        of_x(one[flat + r * tokens : flat + (r + 1) * tokens], 1 - x) for r in range(2)
    ]
    both = swap_x(jnp.concatenate([one[:flat], jnp.concatenate(passed, axis=1)]))

    w_two = swap_z(weight, 2)
    w_one = swap_z(weight, 1)
    w_three = swap_z(w_two, 1)

    og = [own, one, side, both]
    keep_0, send = weight_grad_part(acts, og, block_mask, where, rows, 0, 1)
    got_0 = swap_z(send, 2)
    keep_1, send = weight_grad_part(acts, og, block_mask, where, rows, 1, width // BS - 1)
    got_1 = swap_z(send, 2)
    grad_w = jnp.concatenate([keep_0 + got_0, keep_1 + got_1], axis=1)

    mine, theirs, gx = forward_and_input(
        acts, side, after(out_grad, got_0, keep_1), [weight, w_one, w_two, w_three], block_mask, where
    )
    got = jnp.concatenate([swap_x(t) for t in theirs], axis=2)
    outputs = (mine + got).astype(BF16)

    by = gx.reshape(2, 2, 2 * tokens, rows)
    pair = lax.dynamic_index_in_dim(by, c, 1, keepdims=False) + swap_f(
        lax.dynamic_index_in_dim(by, 1 - c, 1, keepdims=False), 1
    )
    done = lax.dynamic_index_in_dim(pair, y, 0, keepdims=False) + swap_f(
        lax.dynamic_index_in_dim(pair, 1 - y, 0, keepdims=False), 2
    )
    done = done.astype(BF16)
    mine, got = done[:tokens], swap_x(done[tokens:])
    low, high = jnp.where(x == 0, mine, got), jnp.where(x == 0, got, mine)
    return (outputs, grad_w, jnp.concatenate([low, high], axis=1))


def solution(mesh):
    in_specs = (P("dp", None), P("dp", "fsdp"), P(), P(None, "dp", "fsdp"))
    out_specs = (P(None, "dp", "fsdp"), P("dp", "fsdp"), P("dp", "fsdp"))
    return jax.shard_map(
        on_device, mesh=mesh, in_specs=in_specs, out_specs=out_specs, check_vma=False
    )
```

```python
import jax
import jax.numpy as jnp
from jax import lax
from jax.experimental import pallas as pl
from jax.experimental.pallas import tpu as pltpu
from jax.sharding import PartitionSpec as P

BS = 256
TOK_G = 128
LANES = 128
F32 = jnp.float32
BF16 = jnp.bfloat16
PART_VMEM = 16 * 1024 * 1024
FORWARD_VMEM = 28 * 1024 * 1024


def plain(acts, weight, block_mask, out_grad):
    width = weight.shape[1]
    kblocks = block_mask.shape[1]
    oblocks = block_mask.shape[2]
    first_col = lax.axis_index("fsdp") * width
    col_ids = (first_col + jnp.arange(width, dtype=jnp.int32)) // BS
    col_select = (col_ids[None, :] == jnp.arange(oblocks, dtype=jnp.int32)[:, None]).astype(F32)
    col_mask = jnp.einsum("skb,bc->skc", block_mask.astype(F32), col_select)
    full = lax.all_gather(weight, "dp", axis=0, tiled=True)
    row_ids = jnp.arange(full.shape[0], dtype=jnp.int32) // BS
    row_select = (row_ids[:, None] == jnp.arange(kblocks, dtype=jnp.int32)[None, :]).astype(F32)
    mask = jnp.einsum("nk,skc->snc", row_select, col_mask)
    masked = mask.astype(BF16) * full[None]
    forward = jnp.einsum("tn,snc->stc", acts, masked, preferred_element_type=F32)
    input_part = jnp.einsum("stc,snc->tn", out_grad, masked, preferred_element_type=F32)
    products = jnp.einsum("tn,stc->snc", acts, out_grad, preferred_element_type=F32)
    grad_w = lax.psum_scatter(
        jnp.sum(mask * products, axis=0) * (1.0 / TOK_G), "dp", scatter_dimension=0, tiled=True
    )
    grad_x = lax.psum_scatter(input_part, "fsdp", scatter_dimension=1, tiled=True).astype(BF16)
    return (forward.astype(BF16), grad_w, grad_x)


def weight_grad_part(acts, og, block_mask, where, rows, chunk, chunks):
    nsub = block_mask.shape[0]
    tokens = acts.shape[0]
    flat = nsub * tokens
    ng = len(og)
    per = rows // LANES
    width = og[0].shape[1]
    made = chunks * BS

    def kernel(where_ref, mask_ref, acts_ref, *refs):
        extra, og_refs, outs, tiles = refs[:3], refs[3 : 3 + ng], refs[3 + ng : -1], refs[-1]
        z, x = where_ref[0], where_ref[1]
        step = pl.program_id(0)
        col = where_ref[2] + chunk + step

        @pl.when(step == 0)
        def _():
            one_ref, side_ref, both_ref = extra
            for r in range(2):
                for g in range(per):
                    start = ((z ^ (2 * r)) * 2 + x) * rows + g * LANES
                    here = pl.ds(pl.multiple_of(start, LANES), LANES)
                    there = pl.ds(pl.multiple_of(x * rows + g * LANES, LANES), LANES)
                    dst = slice((r * per + g) * LANES, (r * per + g + 1) * LANES)
                    tiles[0, dst, :] = acts_ref[:, here].T
                    tiles[1, dst, :] = one_ref[r * tokens : (r + 1) * tokens, there].T
                    tiles[2, dst, :] = side_ref[:, dst].T
                    tiles[3, dst, :] = both_ref[:, dst].T

        for r in range(2):
            for g in range(per):
                block = (((z ^ (2 * r)) * 2 + x) * rows + g * LANES) // BS
                dst = slice((r * per + g) * LANES, (r * per + g + 1) * LANES)
                keep = [mask_ref[s, block, col].astype(F32) for s in range(nsub)]
                keep = [jnp.full((LANES, tokens), k).astype(BF16) for k in keep]
                total = None
                for k in range(ng):
                    t = tiles[k, dst, :]
                    lhs = jnp.concatenate([t * m for m in keep], axis=1)
                    term = jnp.dot(lhs, og_refs[k][...], preferred_element_type=F32)
                    total = term if total is None else total + term
                outs[r][g * LANES : (g + 1) * LANES, :] = total * (1.0 / TOK_G)

    smem = pl.BlockSpec(memory_space=pltpu.SMEM)
    out = pl.BlockSpec((rows, BS), lambda j: (0, j))
    return pl.pallas_call(
        kernel,
        grid=(chunks,),
        out_shape=(jax.ShapeDtypeStruct((rows, made), F32),) * 2,
        in_specs=[smem, smem, pl.BlockSpec(acts.shape, lambda j: (0, 0))]
        + [
            pl.BlockSpec((2 * tokens, width), lambda j: (flat // (2 * tokens), 0)),
            pl.BlockSpec((tokens, width), lambda j: (flat // tokens, 0)),
            pl.BlockSpec((tokens, width), lambda j: (flat // tokens, 0)),
        ]
        + [pl.BlockSpec((flat, BS), lambda j: (0, chunk + j))] * ng,
        out_specs=(out, out),
        scratch_shapes=[pltpu.VMEM((ng, 2 * rows, tokens), BF16)],
        compiler_params=pltpu.CompilerParams(vmem_limit_bytes=PART_VMEM),
        cost_estimate=pl.CostEstimate(
            flops=4 * ng * rows * made * flat, bytes_accessed=8 * rows * made, transcendentals=0
        ),
        name="weight_grad_part",
    )(where, block_mask, acts, *og[1:], *og)


def forward_and_input(acts, side, og, weights, block_mask, where):
    nsub, tokens, width = og.shape
    flat = nsub * tokens
    nz = len(weights)
    rows = weights[0].shape[0]
    per = rows // LANES

    def kernel(where_ref, mask_ref, acts_ref, sacts_ref, og_ref, sog_ref, *rest):
        w_refs, (keep_ref, send_ref, rest_ref, gx_ref, acc, hilo) = rest[:nz], rest[nz:]
        z, x = where_ref[0], where_ref[1]
        step = pl.program_id(0)
        col = where_ref[2] + step
        first = step == 0
        near = (1 - x).astype(F32)
        far = x.astype(F32)

        def keep_of(block):
            return [mask_ref[s, block, col].astype(F32) for s in range(nsub)]

        for k in range(nz):
            start = ((z ^ k) * 2 + x) * rows
            blocks = [start // BS, (start + rows - LANES) // BS]
            keeps = [keep_of(block) for block in blocks]
            for i in range(2):
                for t, ref in enumerate((og_ref, sog_ref)):
                    total = jnp.zeros((tokens, BS), F32)
                    for s in range(nsub):
                        if t == 0:
                            piece = ref[s]
                        else:
                            piece = ref[s * tokens : (s + 1) * tokens, :]
                        total = total + keeps[i][s] * piece.astype(F32)
                    hi = total.astype(BF16)
                    hilo[k, i, t * tokens : (t + 1) * tokens] = hi
                    hilo[k, i, (t + 2) * tokens : (t + 3) * tokens] = (
                        total - hi.astype(F32)
                    ).astype(BF16)
            prods = []
            for g in range(per):
                here = pl.ds(pl.multiple_of(start + g * LANES, LANES), LANES)
                there = slice((k // 2) * rows + g * LANES, (k // 2) * rows + (g + 1) * LANES)
                both = jnp.concatenate(
                    [acts_ref[:, here], sacts_ref[(k % 2) * tokens : (k % 2 + 1) * tokens, there]]
                )
                at = slice(g * LANES, (g + 1) * LANES)
                w = w_refs[k][at, :]
                prods.append(jnp.dot(both, w, preferred_element_type=F32))
                i = (0, x, 1)[g]
                four = lax.dot_general(
                    hilo[k, i], w, (((1,), (1,)), ((), ())), preferred_element_type=F32
                )
                term = four[: 2 * tokens] + four[2 * tokens :]
                gx_ref[z ^ k, :, at] = jnp.where(first, term, gx_ref[z ^ k, :, at] + term)
            low = prods[0] + near * prods[1]
            high = prods[2] + far * prods[1]
            for s in range(nsub):
                term = keeps[0][s] * low + keeps[1][s] * high
                acc[s] = term if k == 0 else acc[s] + term
        for s in range(nsub):
            keep_ref[s] = acc[s, :tokens]

        @pl.when(first)
        def _():
            for s in range(nsub):
                send_ref[s] = acc[s, tokens:]

        @pl.when(step > 0)
        def _():
            for s in range(nsub):
                rest_ref[0, s] = acc[s, tokens:]

    smem = pl.BlockSpec(memory_space=pltpu.SMEM)
    by_col = pl.BlockSpec((nsub, tokens, BS), lambda j: (0, 0, j))
    gx_shape = (nz, 2 * tokens, rows)
    assert per == 3
    return pl.pallas_call(
        kernel,
        grid=(width // BS,),
        out_shape=(
            jax.ShapeDtypeStruct((nsub, tokens, width), F32),
            jax.ShapeDtypeStruct((nsub, tokens, BS), F32),
            jax.ShapeDtypeStruct((width // BS - 1, nsub, tokens, BS), F32),
            jax.ShapeDtypeStruct(gx_shape, F32),
        ),
        in_specs=[
            smem,
            smem,
            pl.BlockSpec(acts.shape, lambda j: (0, 0)),
            pl.BlockSpec((2 * tokens, width), lambda j: (flat // (2 * tokens), 0)),
            by_col,
            pl.BlockSpec((flat, BS), lambda j: (0, j)),
        ]
        + [pl.BlockSpec((rows, BS), lambda j: (0, j))] * nz,
        out_specs=(
            by_col,
            pl.BlockSpec((nsub, tokens, BS), lambda j: (0, 0, 0)),
            pl.BlockSpec((1, nsub, tokens, BS), lambda j: (jnp.maximum(j - 1, 0), 0, 0, 0)),
            pl.BlockSpec(gx_shape, lambda j: (0, 0, 0)),
        ),
        scratch_shapes=[
            pltpu.VMEM((nsub, 2 * tokens, BS), F32),
            pltpu.VMEM((nz, 2, 4 * tokens, BS), BF16),
        ],
        compiler_params=pltpu.CompilerParams(vmem_limit_bytes=FORWARD_VMEM),
        cost_estimate=pl.CostEstimate(
            flops=36 * tokens * nz * 2 * rows * width,
            bytes_accessed=4 * nz * 2 * rows * width,
            transcendentals=0,
        ),
        name="forward_and_input",
    )(where, block_mask, acts, side, og, side, *weights)


def on_device(acts, weight, block_mask, out_grad):
    rows, width = weight.shape
    tokens, depth = acts.shape
    dp = lax.axis_size("dp")
    fsdp = lax.axis_size("fsdp")
    if rows != 3 * LANES or width != 3 * BS or dp != 8 or fsdp != 4 or tokens != LANES:
        return plain(acts, weight, block_mask, out_grad)
    nx = 2
    me = lax.axis_index("dp")
    z, x = me // nx, me % nx
    f = lax.axis_index("fsdp")
    y, c = f // 2, f % 2
    where = jnp.stack([z, x, f * (width // BS), c]).astype(jnp.int32)

    def swap_dp(a, bits):
        return lax.ppermute(a, "dp", [(d, d ^ bits) for d in range(dp)])

    def swap_x(a):
        return swap_dp(a, 1)

    def swap_z(a, k):
        return swap_dp(a, k * nx)

    def swap_f(a, bit):
        return lax.ppermute(a, "fsdp", [(d, d ^ bit) for d in range(fsdp)])

    def after(a, *others):
        return lax.optimization_barrier((a, *others))[0]

    nsub = out_grad.shape[0]
    flat = nsub * tokens
    own = out_grad.reshape(flat, width)
    by_z = acts.reshape(tokens, dp // nx, nx * rows)

    def acts_of(k):
        return lax.dynamic_index_in_dim(by_z, z ^ k, 1, keepdims=False)

    def of_x(a, side):
        return lax.dynamic_slice_in_dim(a, side * rows, rows, 1)

    def for_other(k):
        return of_x(acts_of(k), 1 - x)

    one = swap_z(jnp.concatenate([own, acts_of(1), acts_of(3)]), 1)
    side = swap_x(
        jnp.concatenate(
            [own]
            + [jnp.concatenate([for_other(k), for_other(k + 2)], axis=1) for k in range(2)]
        )
    )
    one = after(one, side)
    passed = [
        of_x(one[flat + r * tokens : flat + (r + 1) * tokens], 1 - x) for r in range(2)
    ]
    both = swap_x(jnp.concatenate([one[:flat], jnp.concatenate(passed, axis=1)]))

    w_two = swap_z(weight, 2)
    w_one = swap_z(weight, 1)

    og = [own, one, side, both]
    keeps, gots = [], []
    for j in range(width // BS):
        keep, send = weight_grad_part(acts, og, block_mask, where, rows, j, 1)
        keeps.append(keep)
        gots.append(swap_z(send, 2))
    grad_w = jnp.concatenate([k + g for k, g in zip(keeps, gots)], axis=1)
    w_three = swap_z(after(w_two, keeps[0]), 1)

    mine_out, first, rest, gx = forward_and_input(
        acts,
        side,
        after(out_grad, gots[0], *keeps[1:]),
        [weight, w_one, w_two, w_three],
        block_mask,
        where,
    )

    by = after(gx, gots[1]).reshape(2, 2, 2 * tokens, rows)
    pair = swap_f(lax.dynamic_index_in_dim(by, 1 - c, 1, keepdims=False), 1)
    first = swap_x(first)
    rest = swap_x(after(rest, pair))
    pair = after(pair, first) + lax.dynamic_index_in_dim(by, c, 1, keepdims=False)
    done = lax.dynamic_index_in_dim(pair, y, 0, keepdims=False) + swap_f(
        lax.dynamic_index_in_dim(pair, 1 - y, 0, keepdims=False), 2
    )
    done = done.astype(BF16)
    mine, got = done[:tokens], swap_x(done[tokens:])
    low, high = jnp.where(x == 0, mine, got), jnp.where(x == 0, got, mine)
    got = jnp.concatenate([first] + [rest[j] for j in range(rest.shape[0])], axis=2)
    outputs = (mine_out + got).astype(BF16)
    return (outputs, grad_w, jnp.concatenate([low, high], axis=1))


def solution(mesh):
    in_specs = (P("dp", None), P("dp", "fsdp"), P(), P(None, "dp", "fsdp"))
    out_specs = (P(None, "dp", "fsdp"), P("dp", "fsdp"), P("dp", "fsdp"))
    return jax.shard_map(
        on_device, mesh=mesh, in_specs=in_specs, out_specs=out_specs, check_vma=False
    )
```

```python
import jax
import jax.numpy as jnp
from jax import lax
from jax.experimental import pallas as pl
from jax.experimental.pallas import tpu as pltpu
from jax.sharding import PartitionSpec as P

BS = 256
TOK_G = 128
LANES = 128
F32 = jnp.float32
BF16 = jnp.bfloat16
PART_VMEM = 16 * 1024 * 1024
FORWARD_VMEM = 28 * 1024 * 1024


def plain(acts, weight, block_mask, out_grad):
    width = weight.shape[1]
    kblocks = block_mask.shape[1]
    oblocks = block_mask.shape[2]
    first_col = lax.axis_index("fsdp") * width
    col_ids = (first_col + jnp.arange(width, dtype=jnp.int32)) // BS
    col_select = (col_ids[None, :] == jnp.arange(oblocks, dtype=jnp.int32)[:, None]).astype(F32)
    col_mask = jnp.einsum("skb,bc->skc", block_mask.astype(F32), col_select)
    full = lax.all_gather(weight, "dp", axis=0, tiled=True)
    row_ids = jnp.arange(full.shape[0], dtype=jnp.int32) // BS
    row_select = (row_ids[:, None] == jnp.arange(kblocks, dtype=jnp.int32)[None, :]).astype(F32)
    mask = jnp.einsum("nk,skc->snc", row_select, col_mask)
    masked = mask.astype(BF16) * full[None]
    forward = jnp.einsum("tn,snc->stc", acts, masked, preferred_element_type=F32)
    input_part = jnp.einsum("stc,snc->tn", out_grad, masked, preferred_element_type=F32)
    products = jnp.einsum("tn,stc->snc", acts, out_grad, preferred_element_type=F32)
    grad_w = lax.psum_scatter(
        jnp.sum(mask * products, axis=0) * (1.0 / TOK_G), "dp", scatter_dimension=0, tiled=True
    )
    grad_x = lax.psum_scatter(input_part, "fsdp", scatter_dimension=1, tiled=True).astype(BF16)
    return (forward.astype(BF16), grad_w, grad_x)


def weight_grad_part(acts, og, block_mask, where, rows, chunk, chunks):
    nsub = block_mask.shape[0]
    tokens = acts.shape[0]
    flat = nsub * tokens
    ng = len(og)
    per = rows // LANES
    width = og[0].shape[1]
    made = chunks * BS

    def kernel(where_ref, mask_ref, acts_ref, *refs):
        extra, og_refs, outs, tiles = refs[:3], refs[3 : 3 + ng], refs[3 + ng : -1], refs[-1]
        z, x = where_ref[0], where_ref[1]
        step = pl.program_id(0)
        col = where_ref[2] + chunk + step

        @pl.when(step == 0)
        def _():
            one_ref, side_ref, both_ref = extra
            for r in range(2):
                for g in range(per):
                    start = ((z ^ (2 * r)) * 2 + x) * rows + g * LANES
                    here = pl.ds(pl.multiple_of(start, LANES), LANES)
                    there = pl.ds(pl.multiple_of(x * rows + g * LANES, LANES), LANES)
                    dst = slice((r * per + g) * LANES, (r * per + g + 1) * LANES)
                    tiles[0, dst, :] = acts_ref[:, here].T
                    tiles[1, dst, :] = one_ref[r * tokens : (r + 1) * tokens, there].T
                    tiles[2, dst, :] = side_ref[:, dst].T
                    tiles[3, dst, :] = both_ref[:, dst].T

        for r in range(2):
            for g in range(per):
                block = (((z ^ (2 * r)) * 2 + x) * rows + g * LANES) // BS
                dst = slice((r * per + g) * LANES, (r * per + g + 1) * LANES)
                keep = [mask_ref[s, block, col].astype(F32) for s in range(nsub)]
                keep = [jnp.full((LANES, tokens), k).astype(BF16) for k in keep]
                total = None
                for k in range(ng):
                    t = tiles[k, dst, :]
                    lhs = jnp.concatenate([t * m for m in keep], axis=1)
                    term = jnp.dot(lhs, og_refs[k][...], preferred_element_type=F32)
                    total = term if total is None else total + term
                outs[r][g * LANES : (g + 1) * LANES, :] = total * (1.0 / TOK_G)

    smem = pl.BlockSpec(memory_space=pltpu.SMEM)
    out = pl.BlockSpec((rows, BS), lambda j: (0, j))
    return pl.pallas_call(
        kernel,
        grid=(chunks,),
        out_shape=(jax.ShapeDtypeStruct((rows, made), F32),) * 2,
        in_specs=[smem, smem, pl.BlockSpec(acts.shape, lambda j: (0, 0))]
        + [
            pl.BlockSpec((2 * tokens, width), lambda j: (flat // (2 * tokens), 0)),
            pl.BlockSpec((tokens, width), lambda j: (flat // tokens, 0)),
            pl.BlockSpec((tokens, width), lambda j: (flat // tokens, 0)),
        ]
        + [pl.BlockSpec((flat, BS), lambda j: (0, chunk + j))] * ng,
        out_specs=(out, out),
        scratch_shapes=[pltpu.VMEM((ng, 2 * rows, tokens), BF16)],
        compiler_params=pltpu.CompilerParams(vmem_limit_bytes=PART_VMEM),
        cost_estimate=pl.CostEstimate(
            flops=4 * ng * rows * made * flat, bytes_accessed=8 * rows * made, transcendentals=0
        ),
        name="weight_grad_part",
    )(where, block_mask, acts, *og[1:], *og)


def forward_and_input(acts, w_mine, w_peer, og, block_mask, where):
    nsub, tokens, width = og.shape
    depth = acts.shape[1]
    nz = len(w_mine)
    rows = w_mine[0].shape[0]
    per = rows // LANES
    two = BS // LANES

    def kernel(where_ref, mask_ref, acts_ref, og_ref, *rest):
        w_refs, (out_ref, gx_ref, acc, hilo) = rest[: 2 * nz], rest[2 * nz :]
        z, x = where_ref[0], where_ref[1]
        step = pl.program_id(0)
        col = where_ref[2] + step

        @pl.when(step == 0)
        def _():
            gx_ref[...] = jnp.zeros_like(gx_ref)

        acc[...] = jnp.zeros_like(acc)
        for b in range(depth // BS):
            total = jnp.zeros((tokens, BS), F32)
            for s in range(nsub):
                total = total + mask_ref[s, b, col].astype(F32) * og_ref[s].astype(F32)
            hi = total.astype(BF16)
            hilo[b, :tokens] = hi
            hilo[b, tokens:] = (total - hi.astype(F32)).astype(BF16)

        for k in range(nz):
            owner = z ^ k
            tiles = []
            for side in range(2):
                for g in range(per):
                    at = slice(g * LANES, (g + 1) * LANES)
                    tiles.append(jnp.where(x == side, w_refs[k][at, :], w_refs[nz + k][at, :]))
            for b in range(2 * per // two):
                block = owner * (2 * per // two) + b
                w = jnp.concatenate(tiles[b * two : (b + 1) * two])
                cols = pl.ds(pl.multiple_of(block * BS, BS), BS)
                prod = jnp.dot(acts_ref[:, cols], w, preferred_element_type=F32)
                for s in range(nsub):
                    acc[s] += mask_ref[s, block, col].astype(F32) * prod
                both = lax.dot_general(
                    hilo[block], w, (((1,), (1,)), ((), ())), preferred_element_type=F32
                )
                gx_ref[owner, :, b * BS : (b + 1) * BS] += both[:tokens] + both[tokens:]
        out_ref[...] = acc[...].astype(BF16)

    smem = pl.BlockSpec(memory_space=pltpu.SMEM)
    by_col = pl.BlockSpec((nsub, tokens, BS), lambda j: (0, 0, j))
    whole = pl.BlockSpec((tokens, depth), lambda j: (0, 0))
    by_owner = (nz, tokens, depth // nz)
    return pl.pallas_call(
        kernel,
        grid=(width // BS,),
        out_shape=(
            jax.ShapeDtypeStruct((nsub, tokens, width), BF16),
            jax.ShapeDtypeStruct(by_owner, F32),
        ),
        in_specs=[smem, smem, whole, by_col]
        + [pl.BlockSpec((rows, BS), lambda j: (0, j))] * (2 * nz),
        out_specs=(by_col, pl.BlockSpec(by_owner, lambda j: (0, 0, 0))),
        scratch_shapes=[
            pltpu.VMEM((nsub, tokens, BS), F32),
            pltpu.VMEM((depth // BS, 2 * tokens, BS), BF16),
        ],
        compiler_params=pltpu.CompilerParams(vmem_limit_bytes=FORWARD_VMEM),
        cost_estimate=pl.CostEstimate(
            flops=36 * tokens * depth * width, bytes_accessed=4 * depth * width, transcendentals=0
        ),
        name="forward_and_input",
    )(where, block_mask, acts, og, *w_mine, *w_peer)


def on_device(acts, weight, block_mask, out_grad):
    rows, width = weight.shape
    tokens, depth = acts.shape
    dp = lax.axis_size("dp")
    fsdp = lax.axis_size("fsdp")
    if rows != 3 * LANES or width != 3 * BS or dp != 8 or fsdp != 4 or tokens != LANES:
        return plain(acts, weight, block_mask, out_grad)
    nx = 2
    me = lax.axis_index("dp")
    z, x = me // nx, me % nx
    f = lax.axis_index("fsdp")
    y, c = f // 2, f % 2
    where = jnp.stack([z, x, f * (width // BS), c]).astype(jnp.int32)

    def swap_dp(a, bits):
        return lax.ppermute(a, "dp", [(d, d ^ bits) for d in range(dp)])

    def swap_x(a):
        return swap_dp(a, 1)

    def swap_z(a, k):
        return swap_dp(a, k * nx)

    def swap_f(a, bit):
        return lax.ppermute(a, "fsdp", [(d, d ^ bit) for d in range(fsdp)])

    def after(a, *others):
        return lax.optimization_barrier((a, *others))[0]

    nsub = out_grad.shape[0]
    flat = nsub * tokens
    own = out_grad.reshape(flat, width)
    by_z = acts.reshape(tokens, dp // nx, nx * rows)

    def acts_of(k):
        return lax.dynamic_index_in_dim(by_z, z ^ k, 1, keepdims=False)

    def of_x(a, side):
        return lax.dynamic_slice_in_dim(a, side * rows, rows, 1)

    one = swap_z(jnp.concatenate([own, acts_of(1), acts_of(3)]), 1)
    side = swap_x(
        jnp.concatenate(
            [own, jnp.concatenate([of_x(acts_of(0), 1 - x), of_x(acts_of(2), 1 - x)], axis=1)]
        )
    )
    w_peer = [swap_x(weight)]
    one = after(one, side, w_peer[0])
    passed = [
        of_x(one[flat + r * tokens : flat + (r + 1) * tokens], 1 - x) for r in range(2)
    ]
    both = swap_x(jnp.concatenate([one[:flat], jnp.concatenate(passed, axis=1)]))

    w_two = swap_z(weight, 2)
    w_one = swap_z(weight, 1)
    w_peer += [swap_x(w_one), swap_x(w_two)]
    og = [own, one, side, both]
    keeps, gots = [], []
    for j in range(width // BS):
        keep, send = weight_grad_part(acts, og, block_mask, where, rows, j, 1)
        keeps.append(keep)
        gots.append(swap_z(send, 2))
    w_three = swap_z(after(w_two, keeps[0]), 1)
    w_mine = [weight, w_one, w_two, w_three]
    w_peer.append(swap_x(after(w_three, *w_peer[1:], gots[0], keeps[1])))
    grad_w = jnp.concatenate([k + g for k, g in zip(keeps, gots)], axis=1)

    outputs, gx = forward_and_input(
        acts, w_mine, w_peer, after(out_grad, gots[1], keeps[2]), block_mask, where
    )

    by = gx.reshape(2, 2, tokens, depth // 4)
    pair = lax.dynamic_index_in_dim(by, c, 1, keepdims=False) + swap_f(
        lax.dynamic_index_in_dim(by, 1 - c, 1, keepdims=False), 1
    )
    grad_x = lax.dynamic_index_in_dim(pair, y, 0, keepdims=False) + swap_f(
        lax.dynamic_index_in_dim(pair, 1 - y, 0, keepdims=False), 2
    )
    return (outputs, grad_w, grad_x.astype(BF16))


def solution(mesh):
    in_specs = (P("dp", None), P("dp", "fsdp"), P(), P(None, "dp", "fsdp"))
    out_specs = (P(None, "dp", "fsdp"), P("dp", "fsdp"), P("dp", "fsdp"))
    return jax.shard_map(
        on_device, mesh=mesh, in_specs=in_specs, out_specs=out_specs, check_vma=False
    )
```

```python
import jax
import jax.numpy as jnp
from jax import lax
from jax.experimental import pallas as pl
from jax.experimental.pallas import tpu as pltpu
from jax.sharding import PartitionSpec as P

BS = 256
TOK_G = 128
LANES = 128
F32 = jnp.float32
BF16 = jnp.bfloat16
PART_VMEM = 16 * 1024 * 1024
FORWARD_VMEM = 28 * 1024 * 1024


def plain(acts, weight, block_mask, out_grad):
    width = weight.shape[1]
    kblocks = block_mask.shape[1]
    oblocks = block_mask.shape[2]
    first_col = lax.axis_index("fsdp") * width
    col_ids = (first_col + jnp.arange(width, dtype=jnp.int32)) // BS
    col_select = (col_ids[None, :] == jnp.arange(oblocks, dtype=jnp.int32)[:, None]).astype(F32)
    col_mask = jnp.einsum("skb,bc->skc", block_mask.astype(F32), col_select)
    full = lax.all_gather(weight, "dp", axis=0, tiled=True)
    row_ids = jnp.arange(full.shape[0], dtype=jnp.int32) // BS
    row_select = (row_ids[:, None] == jnp.arange(kblocks, dtype=jnp.int32)[None, :]).astype(F32)
    mask = jnp.einsum("nk,skc->snc", row_select, col_mask)
    masked = mask.astype(BF16) * full[None]
    forward = jnp.einsum("tn,snc->stc", acts, masked, preferred_element_type=F32)
    input_part = jnp.einsum("stc,snc->tn", out_grad, masked, preferred_element_type=F32)
    products = jnp.einsum("tn,stc->snc", acts, out_grad, preferred_element_type=F32)
    grad_w = lax.psum_scatter(
        jnp.sum(mask * products, axis=0) * (1.0 / TOK_G), "dp", scatter_dimension=0, tiled=True
    )
    grad_x = lax.psum_scatter(input_part, "fsdp", scatter_dimension=1, tiled=True).astype(BF16)
    return (forward.astype(BF16), grad_w, grad_x)


def weight_grad_part(acts, og, block_mask, where, rows, chunk, chunks):
    nsub = block_mask.shape[0]
    tokens = acts.shape[0]
    flat = nsub * tokens
    ng = len(og)
    per = rows // LANES
    width = og[0].shape[1]
    made = chunks * BS

    def kernel(where_ref, mask_ref, acts_ref, *refs):
        extra, og_refs, outs, tiles = refs[:3], refs[3 : 3 + ng], refs[3 + ng : -1], refs[-1]
        z, x = where_ref[0], where_ref[1]
        step = pl.program_id(0)
        col = where_ref[2] + chunk + step

        @pl.when(step == 0)
        def _():
            one_ref, side_ref, both_ref = extra
            for r in range(2):
                for g in range(per):
                    start = ((z ^ (2 * r)) * 2 + x) * rows + g * LANES
                    here = pl.ds(pl.multiple_of(start, LANES), LANES)
                    there = pl.ds(pl.multiple_of(x * rows + g * LANES, LANES), LANES)
                    dst = slice((r * per + g) * LANES, (r * per + g + 1) * LANES)
                    tiles[0, dst, :] = acts_ref[:, here].T
                    tiles[1, dst, :] = one_ref[r * tokens : (r + 1) * tokens, there].T
                    tiles[2, dst, :] = side_ref[:, dst].T
                    tiles[3, dst, :] = both_ref[:, dst].T

        for r in range(2):
            for g in range(per):
                block = (((z ^ (2 * r)) * 2 + x) * rows + g * LANES) // BS
                dst = slice((r * per + g) * LANES, (r * per + g + 1) * LANES)
                keep = [mask_ref[s, block, col].astype(F32) for s in range(nsub)]
                keep = [jnp.full((LANES, tokens), k).astype(BF16) for k in keep]
                total = None
                for k in range(ng):
                    t = tiles[k, dst, :]
                    lhs = jnp.concatenate([t * m for m in keep], axis=1)
                    term = jnp.dot(lhs, og_refs[k][...], preferred_element_type=F32)
                    total = term if total is None else total + term
                outs[r][g * LANES : (g + 1) * LANES, :] = total * (1.0 / TOK_G)

    smem = pl.BlockSpec(memory_space=pltpu.SMEM)
    out = pl.BlockSpec((rows, BS), lambda j: (0, j))
    return pl.pallas_call(
        kernel,
        grid=(chunks,),
        out_shape=(jax.ShapeDtypeStruct((rows, made), F32),) * 2,
        in_specs=[smem, smem, pl.BlockSpec(acts.shape, lambda j: (0, 0))]
        + [
            pl.BlockSpec((2 * tokens, width), lambda j: (flat // (2 * tokens), 0)),
            pl.BlockSpec((tokens, width), lambda j: (flat // tokens, 0)),
            pl.BlockSpec((tokens, width), lambda j: (flat // tokens, 0)),
        ]
        + [pl.BlockSpec((flat, BS), lambda j: (0, chunk + j))] * ng,
        out_specs=(out, out),
        scratch_shapes=[pltpu.VMEM((ng, 2 * rows, tokens), BF16)],
        compiler_params=pltpu.CompilerParams(vmem_limit_bytes=PART_VMEM),
        cost_estimate=pl.CostEstimate(
            flops=4 * ng * rows * made * flat, bytes_accessed=8 * rows * made, transcendentals=0
        ),
        name="weight_grad_part",
    )(where, block_mask, acts, *og[1:], *og)


def forward_and_input(acts, w_mine, w_peer, og, block_mask, where):
    nsub, tokens, width = og.shape
    depth = acts.shape[1]
    nz = len(w_mine)
    rows = w_mine[0].shape[0]
    per = rows // LANES
    two = BS // LANES

    def kernel(where_ref, mask_ref, acts_ref, og_ref, *rest):
        w_refs, (out_ref, gx_ref, acc, hilo) = rest[: 2 * nz], rest[2 * nz :]
        z, x = where_ref[0], where_ref[1]
        step = pl.program_id(0)
        col = where_ref[2] + step

        @pl.when(step == 0)
        def _():
            gx_ref[...] = jnp.zeros_like(gx_ref)

        acc[...] = jnp.zeros_like(acc)
        for b in range(depth // BS):
            total = jnp.zeros((tokens, BS), F32)
            for s in range(nsub):
                total = total + mask_ref[s, b, col].astype(F32) * og_ref[s].astype(F32)
            hi = total.astype(BF16)
            hilo[b, :tokens] = hi
            hilo[b, tokens:] = (total - hi.astype(F32)).astype(BF16)

        for k in range(nz):
            owner = z ^ k
            tiles = []
            for side in range(2):
                for g in range(per):
                    at = slice(g * LANES, (g + 1) * LANES)
                    tiles.append(jnp.where(x == side, w_refs[k][at, :], w_refs[nz + k][at, :]))
            for b in range(2 * per // two):
                block = owner * (2 * per // two) + b
                w = jnp.concatenate(tiles[b * two : (b + 1) * two])
                cols = pl.ds(pl.multiple_of(block * BS, BS), BS)
                prod = jnp.dot(acts_ref[:, cols], w, preferred_element_type=F32)
                for s in range(nsub):
                    acc[s] += mask_ref[s, block, col].astype(F32) * prod
                both = lax.dot_general(
                    hilo[block], w, (((1,), (1,)), ((), ())), preferred_element_type=F32
                )
                gx_ref[owner, :, b * BS : (b + 1) * BS] += both[:tokens] + both[tokens:]
        out_ref[...] = acc[...].astype(BF16)

    smem = pl.BlockSpec(memory_space=pltpu.SMEM)
    by_col = pl.BlockSpec((nsub, tokens, BS), lambda j: (0, 0, j))
    whole = pl.BlockSpec((tokens, depth), lambda j: (0, 0))
    by_owner = (nz, tokens, depth // nz)
    return pl.pallas_call(
        kernel,
        grid=(width // BS,),
        out_shape=(
            jax.ShapeDtypeStruct((nsub, tokens, width), BF16),
            jax.ShapeDtypeStruct(by_owner, F32),
        ),
        in_specs=[smem, smem, whole, by_col]
        + [pl.BlockSpec((rows, BS), lambda j: (0, j))] * (2 * nz),
        out_specs=(by_col, pl.BlockSpec(by_owner, lambda j: (0, 0, 0))),
        scratch_shapes=[
            pltpu.VMEM((nsub, tokens, BS), F32),
            pltpu.VMEM((depth // BS, 2 * tokens, BS), BF16),
        ],
        compiler_params=pltpu.CompilerParams(vmem_limit_bytes=FORWARD_VMEM),
        cost_estimate=pl.CostEstimate(
            flops=36 * tokens * depth * width, bytes_accessed=4 * depth * width, transcendentals=0
        ),
        name="forward_and_input",
    )(where, block_mask, acts, og, *w_mine, *w_peer)


def on_device(acts, weight, block_mask, out_grad):
    rows, width = weight.shape
    tokens, depth = acts.shape
    dp = lax.axis_size("dp")
    fsdp = lax.axis_size("fsdp")
    if rows != 3 * LANES or width != 3 * BS or dp != 8 or fsdp != 4 or tokens != LANES:
        return plain(acts, weight, block_mask, out_grad)
    nx = 2
    me = lax.axis_index("dp")
    z, x = me // nx, me % nx
    f = lax.axis_index("fsdp")
    y, c = f // 2, f % 2
    where = jnp.stack([z, x, f * (width // BS), c]).astype(jnp.int32)

    def swap_dp(a, bits):
        return lax.ppermute(a, "dp", [(d, d ^ bits) for d in range(dp)])

    def swap_x(a):
        return swap_dp(a, 1)

    def swap_z(a, k):
        return swap_dp(a, k * nx)

    def swap_f(a, bit):
        return lax.ppermute(a, "fsdp", [(d, d ^ bit) for d in range(fsdp)])

    def after(a, *others):
        return lax.optimization_barrier((a, *others))[0]

    nsub = out_grad.shape[0]
    flat = nsub * tokens
    own = out_grad.reshape(flat, width)
    by_z = acts.reshape(tokens, dp // nx, nx * rows)

    def acts_of(k):
        return lax.dynamic_index_in_dim(by_z, z ^ k, 1, keepdims=False)

    def of_x(a, side):
        return lax.dynamic_slice_in_dim(a, side * rows, rows, 1)

    one = swap_z(jnp.concatenate([own, acts_of(1), acts_of(3)]), 1)
    side = swap_x(
        jnp.concatenate(
            [own, jnp.concatenate([of_x(acts_of(0), 1 - x), of_x(acts_of(2), 1 - x)], axis=1)]
        )
    )
    w_peer = [swap_x(weight)]
    one = after(one, side)
    passed = [
        of_x(one[flat + r * tokens : flat + (r + 1) * tokens], 1 - x) for r in range(2)
    ]
    both = swap_x(jnp.concatenate([one[:flat], jnp.concatenate(passed, axis=1)]))

    w_two = swap_z(after(weight, w_peer[0]), 2)
    w_one = swap_z(after(weight, w_peer[0]), 1)
    og = [own, one, side, both]
    keep_0, send_0 = weight_grad_part(acts, og, block_mask, where, rows, 0, 2)
    got_0 = swap_z(send_0, 2)
    keep_1, send_1 = weight_grad_part(acts, og, block_mask, where, rows, 2, width // BS - 2)
    got_1 = swap_z(send_1, 2)
    grad_w = jnp.concatenate([keep_0 + got_0, keep_1 + got_1], axis=1)
    w_three = swap_z(after(w_two, keep_0), 1)
    w_mine = [weight, w_one, w_two, w_three]
    w_peer += [swap_x(after(w_one, keep_0)), swap_x(after(w_two, keep_0))]
    w_peer.append(swap_x(after(w_three, *w_peer[1:], got_0, keep_1)))

    outputs, gx = forward_and_input(
        acts, w_mine, w_peer, out_grad, block_mask, where
    )

    by = after(gx, got_1).reshape(2, 2, tokens, depth // 4)
    pair = lax.dynamic_index_in_dim(by, c, 1, keepdims=False) + swap_f(
        lax.dynamic_index_in_dim(by, 1 - c, 1, keepdims=False), 1
    )
    grad_x = lax.dynamic_index_in_dim(pair, y, 0, keepdims=False) + swap_f(
        lax.dynamic_index_in_dim(pair, 1 - y, 0, keepdims=False), 2
    )
    return (outputs, grad_w, grad_x.astype(BF16))


def solution(mesh):
    in_specs = (P("dp", None), P("dp", "fsdp"), P(), P(None, "dp", "fsdp"))
    out_specs = (P(None, "dp", "fsdp"), P("dp", "fsdp"), P("dp", "fsdp"))
    return jax.shard_map(
        on_device, mesh=mesh, in_specs=in_specs, out_specs=out_specs, check_vma=False
    )
```

```python
import jax
import jax.numpy as jnp
from jax import lax
from jax.experimental import pallas as pl
from jax.experimental.pallas import tpu as pltpu
from jax.sharding import PartitionSpec as P

BS = 256
TOK_G = 128
LANES = 128
F32 = jnp.float32
BF16 = jnp.bfloat16
PART_VMEM = 16 * 1024 * 1024
FORWARD_VMEM = 28 * 1024 * 1024


def plain(acts, weight, block_mask, out_grad):
    width = weight.shape[1]
    kblocks = block_mask.shape[1]
    oblocks = block_mask.shape[2]
    first_col = lax.axis_index("fsdp") * width
    col_ids = (first_col + jnp.arange(width, dtype=jnp.int32)) // BS
    col_select = (col_ids[None, :] == jnp.arange(oblocks, dtype=jnp.int32)[:, None]).astype(F32)
    col_mask = jnp.einsum("skb,bc->skc", block_mask.astype(F32), col_select)
    full = lax.all_gather(weight, "dp", axis=0, tiled=True)
    row_ids = jnp.arange(full.shape[0], dtype=jnp.int32) // BS
    row_select = (row_ids[:, None] == jnp.arange(kblocks, dtype=jnp.int32)[None, :]).astype(F32)
    mask = jnp.einsum("nk,skc->snc", row_select, col_mask)
    masked = mask.astype(BF16) * full[None]
    forward = jnp.einsum("tn,snc->stc", acts, masked, preferred_element_type=F32)
    input_part = jnp.einsum("stc,snc->tn", out_grad, masked, preferred_element_type=F32)
    products = jnp.einsum("tn,stc->snc", acts, out_grad, preferred_element_type=F32)
    grad_w = lax.psum_scatter(
        jnp.sum(mask * products, axis=0) * (1.0 / TOK_G), "dp", scatter_dimension=0, tiled=True
    )
    grad_x = lax.psum_scatter(input_part, "fsdp", scatter_dimension=1, tiled=True).astype(BF16)
    return (forward.astype(BF16), grad_w, grad_x)


def weight_grad_part(acts, og, block_mask, where, rows, chunk, chunks):
    nsub, tokens, width = og[0].shape
    flat = nsub * tokens
    ng = len(og)
    per = rows // LANES
    made = chunks * BS

    def kernel(where_ref, mask_ref, *refs):
        og_refs, outs, tiles = refs[ng : 2 * ng], refs[2 * ng : -1], refs[-1]
        z, x = where_ref[0], where_ref[1]
        step = pl.program_id(0)
        col = where_ref[2] + chunk + step

        @pl.when(step == 0)
        def _():
            acts_ref, one_ref, side_ref, both_ref = refs[:ng]
            for r in range(2):
                for g in range(per):
                    start = ((z ^ (2 * r)) * 2 + x) * rows + g * LANES
                    here = pl.ds(pl.multiple_of(start, LANES), LANES)
                    there = pl.ds(pl.multiple_of(x * rows + g * LANES, LANES), LANES)
                    dst = slice((r * per + g) * LANES, (r * per + g + 1) * LANES)
                    tiles[0, dst, :] = acts_ref[:, here].T
                    tiles[1, dst, :] = one_ref[r, :, there].T
                    tiles[2, dst, :] = side_ref[:, dst].T
                    tiles[3, dst, :] = both_ref[:, dst].T

        rhs = [ref[...].reshape(flat, BS) for ref in og_refs]
        for r in range(2):
            for g in range(per):
                block = (((z ^ (2 * r)) * 2 + x) * rows + g * LANES) // BS
                dst = slice((r * per + g) * LANES, (r * per + g + 1) * LANES)
                keep = [mask_ref[s, block, col].astype(F32) for s in range(nsub)]
                keep = [jnp.full((LANES, tokens), k).astype(BF16) for k in keep]
                total = None
                for k in range(ng):
                    t = tiles[k, dst, :]
                    lhs = jnp.concatenate([t * m for m in keep], axis=1)
                    term = jnp.dot(lhs, rhs[k], preferred_element_type=F32)
                    total = term if total is None else total + term
                outs[r][g * LANES : (g + 1) * LANES, :] = total * (1.0 / TOK_G)

    smem = pl.BlockSpec(memory_space=pltpu.SMEM)
    out = pl.BlockSpec((rows, BS), lambda j: (0, j))
    return pl.pallas_call(
        kernel,
        grid=(chunks,),
        out_shape=(jax.ShapeDtypeStruct((rows, made), F32),) * 2,
        in_specs=[smem, smem]
        + [pl.BlockSpec(a.shape, lambda j, n=a.ndim: (0,) * n) for a in acts]
        + [pl.BlockSpec((nsub, tokens, BS), lambda j: (0, 0, chunk + j))] * ng,
        out_specs=(out, out),
        scratch_shapes=[pltpu.VMEM((ng, 2 * rows, tokens), BF16)],
        compiler_params=pltpu.CompilerParams(vmem_limit_bytes=PART_VMEM),
        cost_estimate=pl.CostEstimate(
            flops=4 * ng * rows * made * flat, bytes_accessed=8 * rows * made, transcendentals=0
        ),
        name="weight_grad_part",
    )(where, block_mask, *acts, *og)


def forward_and_input(acts, w_mine, w_peer, og, block_mask, where):
    nsub, tokens, width = og.shape
    depth = acts.shape[1]
    nz = len(w_mine)
    rows = w_mine[0].shape[0]
    per = rows // LANES
    two = BS // LANES

    def kernel(where_ref, mask_ref, acts_ref, og_ref, *rest):
        w_refs, (out_ref, gx_ref, acc, hilo) = rest[: 2 * nz], rest[2 * nz :]
        z, x = where_ref[0], where_ref[1]
        step = pl.program_id(0)
        col = where_ref[2] + step

        @pl.when(step == 0)
        def _():
            gx_ref[...] = jnp.zeros_like(gx_ref)

        acc[...] = jnp.zeros_like(acc)
        for b in range(depth // BS):
            total = jnp.zeros((tokens, BS), F32)
            for s in range(nsub):
                total = total + mask_ref[s, b, col].astype(F32) * og_ref[s].astype(F32)
            hi = total.astype(BF16)
            hilo[b, :tokens] = hi
            hilo[b, tokens:] = (total - hi.astype(F32)).astype(BF16)

        for k in range(nz):
            owner = z ^ k
            tiles = []
            for side in range(2):
                for g in range(per):
                    at = slice(g * LANES, (g + 1) * LANES)
                    tiles.append(jnp.where(x == side, w_refs[k][at, :], w_refs[nz + k][at, :]))
            for b in range(2 * per // two):
                block = owner * (2 * per // two) + b
                w = jnp.concatenate(tiles[b * two : (b + 1) * two])
                cols = pl.ds(pl.multiple_of(block * BS, BS), BS)
                prod = jnp.dot(acts_ref[:, cols], w, preferred_element_type=F32)
                for s in range(nsub):
                    acc[s] += mask_ref[s, block, col].astype(F32) * prod
                both = lax.dot_general(
                    hilo[block], w, (((1,), (1,)), ((), ())), preferred_element_type=F32
                )
                gx_ref[owner, :, b * BS : (b + 1) * BS] += both[:tokens] + both[tokens:]
        out_ref[...] = acc[...].astype(BF16)

    smem = pl.BlockSpec(memory_space=pltpu.SMEM)
    by_col = pl.BlockSpec((nsub, tokens, BS), lambda j: (0, 0, j))
    whole = pl.BlockSpec((tokens, depth), lambda j: (0, 0))
    by_owner = (nz, tokens, depth // nz)
    return pl.pallas_call(
        kernel,
        grid=(width // BS,),
        out_shape=(
            jax.ShapeDtypeStruct((nsub, tokens, width), BF16),
            jax.ShapeDtypeStruct(by_owner, F32),
        ),
        in_specs=[smem, smem, whole, by_col]
        + [pl.BlockSpec((rows, BS), lambda j: (0, j))] * (2 * nz),
        out_specs=(by_col, pl.BlockSpec(by_owner, lambda j: (0, 0, 0))),
        scratch_shapes=[
            pltpu.VMEM((nsub, tokens, BS), F32),
            pltpu.VMEM((depth // BS, 2 * tokens, BS), BF16),
        ],
        compiler_params=pltpu.CompilerParams(vmem_limit_bytes=FORWARD_VMEM),
        cost_estimate=pl.CostEstimate(
            flops=36 * tokens * depth * width, bytes_accessed=4 * depth * width, transcendentals=0
        ),
        name="forward_and_input",
    )(where, block_mask, acts, og, *w_mine, *w_peer)


def on_device(acts, weight, block_mask, out_grad):
    rows, width = weight.shape
    tokens, depth = acts.shape
    dp = lax.axis_size("dp")
    fsdp = lax.axis_size("fsdp")
    if rows != 3 * LANES or width != 3 * BS or dp != 8 or fsdp != 4 or tokens != LANES:
        return plain(acts, weight, block_mask, out_grad)
    nx = 2
    me = lax.axis_index("dp")
    z, x = me // nx, me % nx
    f = lax.axis_index("fsdp")
    y, c = f // 2, f % 2
    where = jnp.stack([z, x, f * (width // BS), c]).astype(jnp.int32)

    def swap_dp(a, bits):
        return lax.ppermute(a, "dp", [(d, d ^ bits) for d in range(dp)])

    def swap_x(a):
        return swap_dp(a, 1)

    def swap_z(a, k):
        return swap_dp(a, k * nx)

    def swap_f(a, bit):
        return lax.ppermute(a, "fsdp", [(d, d ^ bit) for d in range(fsdp)])

    def after(a, *others):
        return lax.optimization_barrier((a, *others))[0]

    og_one = swap_z(out_grad, 1)
    og_side = swap_x(out_grad)
    og_both = swap_x(after(og_one, og_side))

    def acts_of(a, first, count):
        return lax.dynamic_slice_in_dim(a, first * rows, count * rows, 1)

    acts_one = swap_z(jnp.stack([acts_of(acts, (z ^ k) * nx, nx) for k in (1, 3)]), 1)
    acts_side = swap_x(
        jnp.concatenate([acts_of(acts, (z ^ k) * nx + 1 - x, 1) for k in (0, 2)], axis=1)
    )
    passed = after(acts_one, acts_side)
    acts_both = swap_x(jnp.concatenate([acts_of(passed[r], 1 - x, 1) for r in range(2)], axis=1))

    w_two = swap_z(weight, 2)
    w_one = swap_z(weight, 1)
    og = [out_grad, og_one, og_side, og_both]
    acts_all = [acts, acts_one, acts_side, acts_both]
    keep_0, send_0 = weight_grad_part(acts_all, og, block_mask, where, rows, 0, 1)
    got_0 = swap_z(send_0, 2)
    keep_1, send_1 = weight_grad_part(acts_all, og, block_mask, where, rows, 1, width // BS - 1)
    got_1 = swap_z(send_1, 2)
    grad_w = jnp.concatenate([keep_0 + got_0, keep_1 + got_1], axis=1)
    w_three = swap_z(after(w_two, keep_0), 1)
    w_mine = [weight, w_one, w_two, w_three]
    w_peer = [swap_x(after(w, keep_0)) for w in w_mine[:3]]
    w_peer.append(swap_x(after(w_three, got_0, keep_1)))

    outputs, gx = forward_and_input(
        acts, w_mine, w_peer, out_grad, block_mask, where
    )

    by = after(gx, got_1).reshape(2, 2, tokens, depth // 4)
    pair = lax.dynamic_index_in_dim(by, c, 1, keepdims=False) + swap_f(
        lax.dynamic_index_in_dim(by, 1 - c, 1, keepdims=False), 1
    )
    grad_x = lax.dynamic_index_in_dim(pair, y, 0, keepdims=False) + swap_f(
        lax.dynamic_index_in_dim(pair, 1 - y, 0, keepdims=False), 2
    )
    return (outputs, grad_w, grad_x.astype(BF16))


def solution(mesh):
    in_specs = (P("dp", None), P("dp", "fsdp"), P(), P(None, "dp", "fsdp"))
    out_specs = (P(None, "dp", "fsdp"), P("dp", "fsdp"), P("dp", "fsdp"))
    return jax.shard_map(
        on_device, mesh=mesh, in_specs=in_specs, out_specs=out_specs, check_vma=False
    )
```

```python
import jax
import jax.numpy as jnp
from jax import lax
from jax.experimental import pallas as pl
from jax.experimental.pallas import tpu as pltpu
from jax.sharding import PartitionSpec as P

BS = 256
TOK_G = 128
LANES = 128
F32 = jnp.float32
BF16 = jnp.bfloat16
PART_VMEM = 16 * 1024 * 1024
FORWARD_VMEM = 28 * 1024 * 1024


def plain(acts, weight, block_mask, out_grad):
    width = weight.shape[1]
    kblocks = block_mask.shape[1]
    oblocks = block_mask.shape[2]
    first_col = lax.axis_index("fsdp") * width
    col_ids = (first_col + jnp.arange(width, dtype=jnp.int32)) // BS
    col_select = (col_ids[None, :] == jnp.arange(oblocks, dtype=jnp.int32)[:, None]).astype(F32)
    col_mask = jnp.einsum("skb,bc->skc", block_mask.astype(F32), col_select)
    full = lax.all_gather(weight, "dp", axis=0, tiled=True)
    row_ids = jnp.arange(full.shape[0], dtype=jnp.int32) // BS
    row_select = (row_ids[:, None] == jnp.arange(kblocks, dtype=jnp.int32)[None, :]).astype(F32)
    mask = jnp.einsum("nk,skc->snc", row_select, col_mask)
    masked = mask.astype(BF16) * full[None]
    forward = jnp.einsum("tn,snc->stc", acts, masked, preferred_element_type=F32)
    input_part = jnp.einsum("stc,snc->tn", out_grad, masked, preferred_element_type=F32)
    products = jnp.einsum("tn,stc->snc", acts, out_grad, preferred_element_type=F32)
    grad_w = lax.psum_scatter(
        jnp.sum(mask * products, axis=0) * (1.0 / TOK_G), "dp", scatter_dimension=0, tiled=True
    )
    grad_x = lax.psum_scatter(input_part, "fsdp", scatter_dimension=1, tiled=True).astype(BF16)
    return (forward.astype(BF16), grad_w, grad_x)


def weight_grad_part(acts, og, block_mask, where, rows, chunk, chunks):
    nsub, tokens, width = og[0].shape
    flat = nsub * tokens
    ng = len(og)
    per = rows // LANES
    made = chunks * BS

    def kernel(where_ref, mask_ref, *refs):
        og_refs, outs, tiles = refs[ng : 2 * ng], refs[2 * ng : -1], refs[-1]
        z, x = where_ref[0], where_ref[1]
        step = pl.program_id(0)
        col = where_ref[2] + chunk + step

        @pl.when(step == 0)
        def _():
            acts_ref, one_ref, side_ref, both_ref = refs[:ng]
            for r in range(2):
                for g in range(per):
                    start = ((z ^ (2 * r)) * 2 + x) * rows + g * LANES
                    here = pl.ds(pl.multiple_of(start, LANES), LANES)
                    there = pl.ds(pl.multiple_of(x * rows + g * LANES, LANES), LANES)
                    dst = slice((r * per + g) * LANES, (r * per + g + 1) * LANES)
                    tiles[0, dst, :] = acts_ref[:, here].T
                    tiles[1, dst, :] = one_ref[r, :, there].T
                    tiles[2, dst, :] = side_ref[:, dst].T
                    tiles[3, dst, :] = both_ref[:, dst].T

        rhs = [ref[...].reshape(flat, BS) for ref in og_refs]
        for r in range(2):
            for g in range(per):
                block = (((z ^ (2 * r)) * 2 + x) * rows + g * LANES) // BS
                dst = slice((r * per + g) * LANES, (r * per + g + 1) * LANES)
                keep = [mask_ref[s, block, col].astype(F32) for s in range(nsub)]
                keep = [jnp.full((LANES, tokens), k).astype(BF16) for k in keep]
                total = None
                for k in range(ng):
                    t = tiles[k, dst, :]
                    lhs = jnp.concatenate([t * m for m in keep], axis=1)
                    term = jnp.dot(lhs, rhs[k], preferred_element_type=F32)
                    total = term if total is None else total + term
                outs[r][g * LANES : (g + 1) * LANES, :] = total * (1.0 / TOK_G)

    smem = pl.BlockSpec(memory_space=pltpu.SMEM)
    out = pl.BlockSpec((rows, BS), lambda j: (0, j))
    return pl.pallas_call(
        kernel,
        grid=(chunks,),
        out_shape=(jax.ShapeDtypeStruct((rows, made), F32),) * 2,
        in_specs=[smem, smem]
        + [pl.BlockSpec(a.shape, lambda j, n=a.ndim: (0,) * n) for a in acts]
        + [pl.BlockSpec((nsub, tokens, BS), lambda j: (0, 0, chunk + j))] * ng,
        out_specs=(out, out),
        scratch_shapes=[pltpu.VMEM((ng, 2 * rows, tokens), BF16)],
        compiler_params=pltpu.CompilerParams(vmem_limit_bytes=PART_VMEM),
        cost_estimate=pl.CostEstimate(
            flops=4 * ng * rows * made * flat, bytes_accessed=8 * rows * made, transcendentals=0
        ),
        name="weight_grad_part",
    )(where, block_mask, *acts, *og)


def forward_and_input(acts, w_mine, w_peer, og, block_mask, where, first, before):
    nsub, tokens, width = og.shape
    depth = acts.shape[1]
    nz = len(w_mine)
    owners = depth // (2 * w_mine[0].shape[0])
    rows = w_mine[0].shape[0]
    per = rows // LANES
    two = BS // LANES

    def kernel(where_ref, mask_ref, acts_ref, og_ref, *rest):
        w_refs, rest = rest[: 2 * nz], rest[2 * nz :]
        out_ref, gx_ref, acc, hilo = rest[-4:]
        z, x = where_ref[0], where_ref[1]
        step = pl.program_id(0)
        col = where_ref[2] + step

        @pl.when(step == 0)
        def _():
            gx_ref[...] = rest[1][...] if before else jnp.zeros_like(gx_ref)

        acc[...] = rest[0][...] if before else jnp.zeros_like(acc)
        for k in range(nz):
            owner = z ^ (first + k)
            tiles = []
            for side in range(2):
                for g in range(per):
                    at = slice(g * LANES, (g + 1) * LANES)
                    tiles.append(jnp.where(x == side, w_refs[k][at, :], w_refs[nz + k][at, :]))
            for b in range(2 * per // two):
                block = owner * (2 * per // two) + b
                w = jnp.concatenate(tiles[b * two : (b + 1) * two])
                cols = pl.ds(pl.multiple_of(block * BS, BS), BS)
                total = jnp.zeros((tokens, BS), F32)
                for s in range(nsub):
                    total = total + mask_ref[s, block, col].astype(F32) * og_ref[s].astype(F32)
                hi = total.astype(BF16)
                hilo[:tokens] = hi
                hilo[tokens:] = (total - hi.astype(F32)).astype(BF16)
                prod = jnp.dot(acts_ref[:, cols], w, preferred_element_type=F32)
                for s in range(nsub):
                    acc[s] += mask_ref[s, block, col].astype(F32) * prod
                both = lax.dot_general(
                    hilo[...], w, (((1,), (1,)), ((), ())), preferred_element_type=F32
                )
                gx_ref[owner, :, b * BS : (b + 1) * BS] += both[:tokens] + both[tokens:]
        out_ref[...] = acc[...].astype(out_ref.dtype)

    smem = pl.BlockSpec(memory_space=pltpu.SMEM)
    by_col = pl.BlockSpec((nsub, tokens, BS), lambda j: (0, 0, j))
    whole = pl.BlockSpec((tokens, depth), lambda j: (0, 0))
    by_owner = (owners, tokens, depth // owners)
    gx_spec = pl.BlockSpec(by_owner, lambda j: (0, 0, 0))
    return pl.pallas_call(
        kernel,
        grid=(width // BS,),
        out_shape=(
            jax.ShapeDtypeStruct((nsub, tokens, width), BF16 if before else F32),
            jax.ShapeDtypeStruct(by_owner, F32),
        ),
        in_specs=[smem, smem, whole, by_col]
        + [pl.BlockSpec((rows, BS), lambda j: (0, j))] * (2 * nz)
        + ([by_col, gx_spec] if before else []),
        out_specs=(by_col, gx_spec),
        scratch_shapes=[
            pltpu.VMEM((nsub, tokens, BS), F32),
            pltpu.VMEM((2 * tokens, BS), BF16),
        ],
        compiler_params=pltpu.CompilerParams(vmem_limit_bytes=FORWARD_VMEM),
        cost_estimate=pl.CostEstimate(
            flops=72 * tokens * nz * rows * width,
            bytes_accessed=8 * nz * rows * width,
            transcendentals=0,
        ),
        name="forward_and_input",
    )(where, block_mask, acts, og, *w_mine, *w_peer, *(before or ()))


def on_device(acts, weight, block_mask, out_grad):
    rows, width = weight.shape
    tokens, depth = acts.shape
    dp = lax.axis_size("dp")
    fsdp = lax.axis_size("fsdp")
    if rows != 3 * LANES or width != 3 * BS or dp != 8 or fsdp != 4 or tokens != LANES:
        return plain(acts, weight, block_mask, out_grad)
    nx = 2
    me = lax.axis_index("dp")
    z, x = me // nx, me % nx
    f = lax.axis_index("fsdp")
    y, c = f // 2, f % 2
    where = jnp.stack([z, x, f * (width // BS), c]).astype(jnp.int32)

    def swap_dp(a, bits):
        return lax.ppermute(a, "dp", [(d, d ^ bits) for d in range(dp)])

    def swap_x(a):
        return swap_dp(a, 1)

    def swap_z(a, k):
        return swap_dp(a, k * nx)

    def swap_f(a, bit):
        return lax.ppermute(a, "fsdp", [(d, d ^ bit) for d in range(fsdp)])

    def after(a, *others):
        return lax.optimization_barrier((a, *others))[0]

    og_one = swap_z(out_grad, 1)
    og_side = swap_x(out_grad)
    og_both = swap_x(after(og_one, og_side))

    def acts_of(a, first, count):
        return lax.dynamic_slice_in_dim(a, first * rows, count * rows, 1)

    acts_one = swap_z(jnp.stack([acts_of(acts, (z ^ k) * nx, nx) for k in (1, 3)]), 1)
    acts_side = swap_x(
        jnp.concatenate([acts_of(acts, (z ^ k) * nx + 1 - x, 1) for k in (0, 2)], axis=1)
    )
    passed = after(acts_one, acts_side)
    acts_both = swap_x(jnp.concatenate([acts_of(passed[r], 1 - x, 1) for r in range(2)], axis=1))

    w_two = swap_z(weight, 2)
    w_one = swap_z(weight, 1)
    og = [out_grad, og_one, og_side, og_both]
    acts_all = [acts, acts_one, acts_side, acts_both]
    keep_0, send_0 = weight_grad_part(acts_all, og, block_mask, where, rows, 0, 1)
    got_0 = swap_z(send_0, 2)
    w_peer = [swap_x(after(weight, acts_side))]
    keep_1, send_1 = weight_grad_part(
        acts_all, og, block_mask, after(where, w_peer[0]), rows, 1, width // BS - 1
    )
    got_1 = swap_z(send_1, 2)
    grad_w = jnp.concatenate([keep_0 + got_0, keep_1 + got_1], axis=1)
    w_three = swap_z(after(w_two, keep_0), 1)
    w_mine = [weight, w_one, w_two, w_three]
    w_peer += [swap_x(after(w_one, got_0)), swap_x(after(w_two, keep_0))]
    w_peer.append(swap_x(after(w_three, keep_1)))

    sums = forward_and_input(
        acts, w_mine[:3], w_peer[:3], out_grad, block_mask, where, 0, None
    )
    outputs, gx = forward_and_input(
        acts, w_mine[3:], w_peer[3:], out_grad, block_mask, where, 3, sums
    )

    by = after(gx, got_1).reshape(2, 2, tokens, depth // 4)
    pair = lax.dynamic_index_in_dim(by, c, 1, keepdims=False) + swap_f(
        lax.dynamic_index_in_dim(by, 1 - c, 1, keepdims=False), 1
    )
    grad_x = lax.dynamic_index_in_dim(pair, y, 0, keepdims=False) + swap_f(
        lax.dynamic_index_in_dim(pair, 1 - y, 0, keepdims=False), 2
    )
    return (outputs, grad_w, grad_x.astype(BF16))


def solution(mesh):
    in_specs = (P("dp", None), P("dp", "fsdp"), P(), P(None, "dp", "fsdp"))
    out_specs = (P(None, "dp", "fsdp"), P("dp", "fsdp"), P("dp", "fsdp"))
    return jax.shard_map(
        on_device, mesh=mesh, in_specs=in_specs, out_specs=out_specs, check_vma=False
    )
```

```python
import jax
import jax.numpy as jnp
from jax import lax
from jax.experimental import pallas as pl
from jax.experimental.pallas import tpu as pltpu
from jax.sharding import PartitionSpec as P

BS = 256
TOK_G = 128
LANES = 128
F32 = jnp.float32
BF16 = jnp.bfloat16
PART_VMEM = 16 * 1024 * 1024
FORWARD_VMEM = 28 * 1024 * 1024


def plain(acts, weight, block_mask, out_grad):
    width = weight.shape[1]
    kblocks = block_mask.shape[1]
    oblocks = block_mask.shape[2]
    first_col = lax.axis_index("fsdp") * width
    col_ids = (first_col + jnp.arange(width, dtype=jnp.int32)) // BS
    col_select = (col_ids[None, :] == jnp.arange(oblocks, dtype=jnp.int32)[:, None]).astype(F32)
    col_mask = jnp.einsum("skb,bc->skc", block_mask.astype(F32), col_select)
    full = lax.all_gather(weight, "dp", axis=0, tiled=True)
    row_ids = jnp.arange(full.shape[0], dtype=jnp.int32) // BS
    row_select = (row_ids[:, None] == jnp.arange(kblocks, dtype=jnp.int32)[None, :]).astype(F32)
    mask = jnp.einsum("nk,skc->snc", row_select, col_mask)
    masked = mask.astype(BF16) * full[None]
    forward = jnp.einsum("tn,snc->stc", acts, masked, preferred_element_type=F32)
    input_part = jnp.einsum("stc,snc->tn", out_grad, masked, preferred_element_type=F32)
    products = jnp.einsum("tn,stc->snc", acts, out_grad, preferred_element_type=F32)
    grad_w = lax.psum_scatter(
        jnp.sum(mask * products, axis=0) * (1.0 / TOK_G), "dp", scatter_dimension=0, tiled=True
    )
    grad_x = lax.psum_scatter(input_part, "fsdp", scatter_dimension=1, tiled=True).astype(BF16)
    return (forward.astype(BF16), grad_w, grad_x)


def weight_grad_part(acts, og, block_mask, where, rows, chunk, chunks):
    nsub, tokens, width = og[0].shape
    flat = nsub * tokens
    ng = len(og)
    per = rows // LANES
    made = chunks * BS

    def kernel(where_ref, mask_ref, *refs):
        og_refs, outs, tiles = refs[ng : 2 * ng], refs[2 * ng : -1], refs[-1]
        z, x = where_ref[0], where_ref[1]
        step = pl.program_id(0)
        col = where_ref[2] + chunk + step

        @pl.when(step == 0)
        def _():
            acts_ref, one_ref, side_ref, both_ref = refs[:ng]
            for r in range(2):
                for g in range(per):
                    start = ((z ^ (2 * r)) * 2 + x) * rows + g * LANES
                    here = pl.ds(pl.multiple_of(start, LANES), LANES)
                    there = pl.ds(pl.multiple_of(x * rows + g * LANES, LANES), LANES)
                    dst = slice((r * per + g) * LANES, (r * per + g + 1) * LANES)
                    tiles[0, dst, :] = acts_ref[:, here].T
                    tiles[1, dst, :] = one_ref[r, :, there].T
                    tiles[2, dst, :] = side_ref[:, dst].T
                    tiles[3, dst, :] = both_ref[:, dst].T

        rhs = [ref[...].reshape(flat, BS) for ref in og_refs]
        for r in range(2):
            for g in range(per):
                block = (((z ^ (2 * r)) * 2 + x) * rows + g * LANES) // BS
                dst = slice((r * per + g) * LANES, (r * per + g + 1) * LANES)
                keep = [mask_ref[s, block, col].astype(F32) for s in range(nsub)]
                keep = [jnp.full((LANES, tokens), k).astype(BF16) for k in keep]
                total = None
                for k in range(ng):
                    t = tiles[k, dst, :]
                    lhs = jnp.concatenate([t * m for m in keep], axis=1)
                    term = jnp.dot(lhs, rhs[k], preferred_element_type=F32)
                    total = term if total is None else total + term
                outs[r][g * LANES : (g + 1) * LANES, :] = total * (1.0 / TOK_G)

    smem = pl.BlockSpec(memory_space=pltpu.SMEM)
    out = pl.BlockSpec((rows, BS), lambda j: (0, j))
    return pl.pallas_call(
        kernel,
        grid=(chunks,),
        out_shape=(jax.ShapeDtypeStruct((rows, made), F32),) * 2,
        in_specs=[smem, smem]
        + [pl.BlockSpec(a.shape, lambda j, n=a.ndim: (0,) * n) for a in acts]
        + [pl.BlockSpec((nsub, tokens, BS), lambda j: (0, 0, chunk + j))] * ng,
        out_specs=(out, out),
        scratch_shapes=[pltpu.VMEM((ng, 2 * rows, tokens), BF16)],
        compiler_params=pltpu.CompilerParams(vmem_limit_bytes=PART_VMEM),
        cost_estimate=pl.CostEstimate(
            flops=4 * ng * rows * made * flat, bytes_accessed=8 * rows * made, transcendentals=0
        ),
        name="weight_grad_part",
    )(where, block_mask, *acts, *og)


def forward_and_input(acts, w_mine, w_peer, og, block_mask, where, first, before):
    nsub, tokens, width = og.shape
    depth = acts.shape[1]
    nz = len(w_mine)
    owners = depth // (2 * w_mine[0].shape[0])
    rows = w_mine[0].shape[0]
    per = rows // LANES
    two = BS // LANES

    def kernel(where_ref, mask_ref, acts_ref, og_ref, *rest):
        w_refs, rest = rest[: 2 * nz], rest[2 * nz :]
        out_ref, gx_ref, acc, hilo = rest[-4:]
        z, x = where_ref[0], where_ref[1]
        step = pl.program_id(0)
        col = where_ref[2] + step

        @pl.when(step == 0)
        def _():
            gx_ref[...] = rest[1][...] if before else jnp.zeros_like(gx_ref)

        acc[...] = rest[0][...] if before else jnp.zeros_like(acc)
        for k in range(nz):
            owner = z ^ (first + k)
            tiles = []
            for side in range(2):
                for g in range(per):
                    at = slice(g * LANES, (g + 1) * LANES)
                    tiles.append(jnp.where(x == side, w_refs[k][at, :], w_refs[nz + k][at, :]))
            for b in range(2 * per // two):
                block = owner * (2 * per // two) + b
                w = jnp.concatenate(tiles[b * two : (b + 1) * two])
                cols = pl.ds(pl.multiple_of(block * BS, BS), BS)
                total = jnp.zeros((tokens, BS), F32)
                for s in range(nsub):
                    total = total + mask_ref[s, block, col].astype(F32) * og_ref[s].astype(F32)
                hi = total.astype(BF16)
                hilo[:tokens] = hi
                hilo[tokens:] = (total - hi.astype(F32)).astype(BF16)
                prod = jnp.dot(acts_ref[:, cols], w, preferred_element_type=F32)
                for s in range(nsub):
                    acc[s] += mask_ref[s, block, col].astype(F32) * prod
                both = lax.dot_general(
                    hilo[...], w, (((1,), (1,)), ((), ())), preferred_element_type=F32
                )
                gx_ref[owner, :, b * BS : (b + 1) * BS] += both[:tokens] + both[tokens:]
        out_ref[...] = acc[...].astype(out_ref.dtype)

    smem = pl.BlockSpec(memory_space=pltpu.SMEM)
    by_col = pl.BlockSpec((nsub, tokens, BS), lambda j: (0, 0, j))
    whole = pl.BlockSpec((tokens, depth), lambda j: (0, 0))
    by_owner = (owners, tokens, depth // owners)
    gx_spec = pl.BlockSpec(by_owner, lambda j: (0, 0, 0))
    return pl.pallas_call(
        kernel,
        grid=(width // BS,),
        out_shape=(
            jax.ShapeDtypeStruct((nsub, tokens, width), BF16 if before else F32),
            jax.ShapeDtypeStruct(by_owner, F32),
        ),
        in_specs=[smem, smem, whole, by_col]
        + [pl.BlockSpec((rows, BS), lambda j: (0, j))] * (2 * nz)
        + ([by_col, gx_spec] if before else []),
        out_specs=(by_col, gx_spec),
        scratch_shapes=[
            pltpu.VMEM((nsub, tokens, BS), F32),
            pltpu.VMEM((2 * tokens, BS), BF16),
        ],
        compiler_params=pltpu.CompilerParams(vmem_limit_bytes=FORWARD_VMEM),
        cost_estimate=pl.CostEstimate(
            flops=72 * tokens * nz * rows * width,
            bytes_accessed=8 * nz * rows * width,
            transcendentals=0,
        ),
        name="forward_and_input",
    )(where, block_mask, acts, og, *w_mine, *w_peer, *(before or ()))


def on_device(acts, weight, block_mask, out_grad):
    rows, width = weight.shape
    tokens, depth = acts.shape
    dp = lax.axis_size("dp")
    fsdp = lax.axis_size("fsdp")
    if rows != 3 * LANES or width != 3 * BS or dp != 8 or fsdp != 4 or tokens != LANES:
        return plain(acts, weight, block_mask, out_grad)
    nx = 2
    me = lax.axis_index("dp")
    z, x = me // nx, me % nx
    f = lax.axis_index("fsdp")
    y, c = f // 2, f % 2
    where = jnp.stack([z, x, f * (width // BS), c]).astype(jnp.int32)

    def swap_dp(a, bits):
        return lax.ppermute(a, "dp", [(d, d ^ bits) for d in range(dp)])

    def swap_x(a):
        return swap_dp(a, 1)

    def swap_z(a, k):
        return swap_dp(a, k * nx)

    def swap_f(a, bit):
        return lax.ppermute(a, "fsdp", [(d, d ^ bit) for d in range(fsdp)])

    def after(a, *others):
        return lax.optimization_barrier((a, *others))[0]

    og_one = swap_z(out_grad, 1)
    og_side = swap_x(out_grad)
    og_both = swap_x(after(og_one, og_side))

    def acts_of(a, first, count):
        return lax.dynamic_slice_in_dim(a, first * rows, count * rows, 1)

    acts_one = swap_z(jnp.stack([acts_of(acts, (z ^ k) * nx, nx) for k in (1, 3)]), 1)
    acts_side = swap_x(
        jnp.concatenate([acts_of(acts, (z ^ k) * nx + 1 - x, 1) for k in (0, 2)], axis=1)
    )
    passed = after(acts_one, acts_side)
    acts_both = swap_x(jnp.concatenate([acts_of(passed[r], 1 - x, 1) for r in range(2)], axis=1))

    w_two = swap_z(weight, 2)
    w_one = swap_z(weight, 1)
    og = [out_grad, og_one, og_side, og_both]
    acts_all = [acts, acts_one, acts_side, acts_both]
    keeps, gots = [], []
    for j in range(width // BS):
        keep, send = weight_grad_part(acts_all, og, block_mask, where, rows, j, 1)
        keeps.append(keep)
        gots.append(swap_z(send, 2))
    grad_w = jnp.concatenate([k + g for k, g in zip(keeps, gots)], axis=1)
    w_three = swap_z(after(w_two, keeps[0]), 1)
    w_mine = [weight, w_one, w_two, w_three]
    x_own = swap_x(after(weight, acts_side))
    x_one = swap_x(after(w_one, gots[0], x_own, keeps[1]))
    x_two = swap_x(after(w_two, keeps[0]))
    x_three = swap_x(after(w_three, keeps[2], x_two))
    w_peer = [x_own, x_one, x_two, x_three]

    sums = forward_and_input(
        acts, w_mine[:3], w_peer[:3], after(out_grad, gots[1]), block_mask, where, 0, None
    )
    outputs, gx = forward_and_input(
        acts, w_mine[3:], w_peer[3:], out_grad, block_mask, where, 3, sums
    )

    by = after(gx, gots[2]).reshape(2, 2, tokens, depth // 4)
    pair = lax.dynamic_index_in_dim(by, c, 1, keepdims=False) + swap_f(
        lax.dynamic_index_in_dim(by, 1 - c, 1, keepdims=False), 1
    )
    grad_x = lax.dynamic_index_in_dim(pair, y, 0, keepdims=False) + swap_f(
        lax.dynamic_index_in_dim(pair, 1 - y, 0, keepdims=False), 2
    )
    return (outputs, grad_w, grad_x.astype(BF16))


def solution(mesh):
    in_specs = (P("dp", None), P("dp", "fsdp"), P(), P(None, "dp", "fsdp"))
    out_specs = (P(None, "dp", "fsdp"), P("dp", "fsdp"), P("dp", "fsdp"))
    return jax.shard_map(
        on_device, mesh=mesh, in_specs=in_specs, out_specs=out_specs, check_vma=False
    )
```

```python
import jax
import jax.numpy as jnp
from jax import lax
from jax.experimental import pallas as pl
from jax.experimental.pallas import tpu as pltpu
from jax.sharding import PartitionSpec as P

BS = 256
TOK_G = 128
LANES = 128
F32 = jnp.float32
BF16 = jnp.bfloat16
PART_VMEM = 16 * 1024 * 1024
FORWARD_VMEM = 28 * 1024 * 1024


def plain(acts, weight, block_mask, out_grad):
    width = weight.shape[1]
    kblocks = block_mask.shape[1]
    oblocks = block_mask.shape[2]
    first_col = lax.axis_index("fsdp") * width
    col_ids = (first_col + jnp.arange(width, dtype=jnp.int32)) // BS
    col_select = (col_ids[None, :] == jnp.arange(oblocks, dtype=jnp.int32)[:, None]).astype(F32)
    col_mask = jnp.einsum("skb,bc->skc", block_mask.astype(F32), col_select)
    full = lax.all_gather(weight, "dp", axis=0, tiled=True)
    row_ids = jnp.arange(full.shape[0], dtype=jnp.int32) // BS
    row_select = (row_ids[:, None] == jnp.arange(kblocks, dtype=jnp.int32)[None, :]).astype(F32)
    mask = jnp.einsum("nk,skc->snc", row_select, col_mask)
    masked = mask.astype(BF16) * full[None]
    forward = jnp.einsum("tn,snc->stc", acts, masked, preferred_element_type=F32)
    input_part = jnp.einsum("stc,snc->tn", out_grad, masked, preferred_element_type=F32)
    products = jnp.einsum("tn,stc->snc", acts, out_grad, preferred_element_type=F32)
    grad_w = lax.psum_scatter(
        jnp.sum(mask * products, axis=0) * (1.0 / TOK_G), "dp", scatter_dimension=0, tiled=True
    )
    grad_x = lax.psum_scatter(input_part, "fsdp", scatter_dimension=1, tiled=True).astype(BF16)
    return (forward.astype(BF16), grad_w, grad_x)


def weight_grad_part(acts, og, block_mask, where, rows, chunk, chunks):
    nsub, tokens, width = og[0].shape
    flat = nsub * tokens
    ng = len(og)
    per = rows // LANES
    made = chunks * BS

    def kernel(where_ref, mask_ref, *refs):
        og_refs, outs, tiles = refs[ng : 2 * ng], refs[2 * ng : -1], refs[-1]
        z, x = where_ref[0], where_ref[1]
        step = pl.program_id(0)
        col = where_ref[2] + chunk + step

        @pl.when(step == 0)
        def _():
            acts_ref, one_ref, side_ref, both_ref = refs[:ng]
            for r in range(2):
                for g in range(per):
                    start = ((z ^ (2 * r)) * 2 + x) * rows + g * LANES
                    here = pl.ds(pl.multiple_of(start, LANES), LANES)
                    there = pl.ds(pl.multiple_of(x * rows + g * LANES, LANES), LANES)
                    dst = slice((r * per + g) * LANES, (r * per + g + 1) * LANES)
                    tiles[0, dst, :] = acts_ref[:, here].T
                    tiles[1, dst, :] = one_ref[r, :, there].T
                    tiles[2, dst, :] = side_ref[:, dst].T
                    tiles[3, dst, :] = both_ref[:, dst].T

        rhs = [ref[...].reshape(flat, BS) for ref in og_refs]
        for r in range(2):
            for g in range(per):
                block = (((z ^ (2 * r)) * 2 + x) * rows + g * LANES) // BS
                dst = slice((r * per + g) * LANES, (r * per + g + 1) * LANES)
                keep = [mask_ref[s, block, col].astype(F32) for s in range(nsub)]
                keep = [jnp.full((LANES, tokens), k).astype(BF16) for k in keep]
                total = None
                for k in range(ng):
                    t = tiles[k, dst, :]
                    lhs = jnp.concatenate([t * m for m in keep], axis=1)
                    term = jnp.dot(lhs, rhs[k], preferred_element_type=F32)
                    total = term if total is None else total + term
                outs[r][g * LANES : (g + 1) * LANES, :] = total * (1.0 / TOK_G)

    smem = pl.BlockSpec(memory_space=pltpu.SMEM)
    out = pl.BlockSpec((rows, BS), lambda j: (0, j))
    return pl.pallas_call(
        kernel,
        grid=(chunks,),
        out_shape=(jax.ShapeDtypeStruct((rows, made), F32),) * 2,
        in_specs=[smem, smem]
        + [pl.BlockSpec(a.shape, lambda j, n=a.ndim: (0,) * n) for a in acts]
        + [pl.BlockSpec((nsub, tokens, BS), lambda j: (0, 0, chunk + j))] * ng,
        out_specs=(out, out),
        scratch_shapes=[pltpu.VMEM((ng, 2 * rows, tokens), BF16)],
        compiler_params=pltpu.CompilerParams(vmem_limit_bytes=PART_VMEM),
        cost_estimate=pl.CostEstimate(
            flops=4 * ng * rows * made * flat, bytes_accessed=8 * rows * made, transcendentals=0
        ),
        name="weight_grad_part",
    )(where, block_mask, *acts, *og)


def forward_and_input(acts, w_mine, w_peer, og, block_mask, where, first, before):
    nsub, tokens, width = og.shape
    depth = acts.shape[1]
    nz = len(w_mine)
    owners = depth // (2 * w_mine[0].shape[0])
    rows = w_mine[0].shape[0]
    per = rows // LANES
    two = BS // LANES

    def kernel(where_ref, mask_ref, acts_ref, og_ref, *rest):
        w_refs, rest = rest[: 2 * nz], rest[2 * nz :]
        out_ref, gx_ref, acc, hilo = rest[-4:]
        z, x = where_ref[0], where_ref[1]
        step = pl.program_id(0)
        col = where_ref[2] + step

        @pl.when(step == 0)
        def _():
            gx_ref[...] = rest[1][...] if before else jnp.zeros_like(gx_ref)

        acc[...] = rest[0][...] if before else jnp.zeros_like(acc)
        for k in range(nz):
            owner = z ^ (first + k)
            tiles = []
            for side in range(2):
                for g in range(per):
                    at = slice(g * LANES, (g + 1) * LANES)
                    tiles.append(jnp.where(x == side, w_refs[k][at, :], w_refs[nz + k][at, :]))
            for b in range(2 * per // two):
                block = owner * (2 * per // two) + b
                w = jnp.concatenate(tiles[b * two : (b + 1) * two])
                cols = pl.ds(pl.multiple_of(block * BS, BS), BS)
                total = jnp.zeros((tokens, BS), F32)
                for s in range(nsub):
                    total = total + mask_ref[s, block, col].astype(F32) * og_ref[s].astype(F32)
                hi = total.astype(BF16)
                hilo[:tokens] = hi
                hilo[tokens:] = (total - hi.astype(F32)).astype(BF16)
                prod = jnp.dot(acts_ref[:, cols], w, preferred_element_type=F32)
                for s in range(nsub):
                    acc[s] += mask_ref[s, block, col].astype(F32) * prod
                both = lax.dot_general(
                    hilo[...], w, (((1,), (1,)), ((), ())), preferred_element_type=F32
                )
                gx_ref[owner, :, b * BS : (b + 1) * BS] += both[:tokens] + both[tokens:]
        out_ref[...] = acc[...].astype(out_ref.dtype)

    smem = pl.BlockSpec(memory_space=pltpu.SMEM)
    by_col = pl.BlockSpec((nsub, tokens, BS), lambda j: (0, 0, j))
    whole = pl.BlockSpec((tokens, depth), lambda j: (0, 0))
    by_owner = (owners, tokens, depth // owners)
    gx_spec = pl.BlockSpec(by_owner, lambda j: (0, 0, 0))
    return pl.pallas_call(
        kernel,
        grid=(width // BS,),
        out_shape=(
            jax.ShapeDtypeStruct((nsub, tokens, width), BF16 if before else F32),
            jax.ShapeDtypeStruct(by_owner, F32),
        ),
        in_specs=[smem, smem, whole, by_col]
        + [pl.BlockSpec((rows, BS), lambda j: (0, j))] * (2 * nz)
        + ([by_col, gx_spec] if before else []),
        out_specs=(by_col, gx_spec),
        scratch_shapes=[
            pltpu.VMEM((nsub, tokens, BS), F32),
            pltpu.VMEM((2 * tokens, BS), BF16),
        ],
        compiler_params=pltpu.CompilerParams(vmem_limit_bytes=FORWARD_VMEM),
        cost_estimate=pl.CostEstimate(
            flops=72 * tokens * nz * rows * width,
            bytes_accessed=8 * nz * rows * width,
            transcendentals=0,
        ),
        name="forward_and_input",
    )(where, block_mask, acts, og, *w_mine, *w_peer, *(before or ()))


def on_device(acts, weight, block_mask, out_grad):
    rows, width = weight.shape
    tokens, depth = acts.shape
    dp = lax.axis_size("dp")
    fsdp = lax.axis_size("fsdp")
    if rows != 3 * LANES or width != 3 * BS or dp != 8 or fsdp != 4 or tokens != LANES:
        return plain(acts, weight, block_mask, out_grad)
    nx = 2
    me = lax.axis_index("dp")
    z, x = me // nx, me % nx
    f = lax.axis_index("fsdp")
    y, c = f // 2, f % 2
    where = jnp.stack([z, x, f * (width // BS), c]).astype(jnp.int32)

    def swap_dp(a, bits):
        return lax.ppermute(a, "dp", [(d, d ^ bits) for d in range(dp)])

    def swap_x(a):
        return swap_dp(a, 1)

    def swap_z(a, k):
        return swap_dp(a, k * nx)

    def swap_f(a, bit):
        return lax.ppermute(a, "fsdp", [(d, d ^ bit) for d in range(fsdp)])

    def after(a, *others):
        return lax.optimization_barrier((a, *others))[0]

    og_one = swap_z(out_grad, 1)
    og_side = swap_x(out_grad)
    og_both = swap_x(after(og_one, og_side))

    def acts_of(a, first, count):
        return lax.dynamic_slice_in_dim(a, first * rows, count * rows, 1)

    acts_one = swap_z(jnp.stack([acts_of(acts, (z ^ k) * nx, nx) for k in (1, 3)]), 1)
    acts_side = swap_x(
        jnp.concatenate([acts_of(acts, (z ^ k) * nx + 1 - x, 1) for k in (0, 2)], axis=1)
    )
    passed = after(acts_one, acts_side)
    acts_both = swap_x(jnp.concatenate([acts_of(passed[r], 1 - x, 1) for r in range(2)], axis=1))

    w_two = swap_z(weight, 2)
    w_one = swap_z(weight, 1)
    og = [out_grad, og_one, og_side, og_both]
    acts_all = [acts, acts_one, acts_side, acts_both]
    keeps, gots = [], []
    for j in range(width // BS):
        keep, send = weight_grad_part(acts_all, og, block_mask, where, rows, j, 1)
        keeps.append(keep)
        gots.append(swap_z(send, 2))
    grad_w = jnp.concatenate([k + g for k, g in zip(keeps, gots)], axis=1)
    w_three = swap_z(after(w_two, keeps[0]), 1)
    w_mine = [weight, w_one, w_two, w_three]
    x_own = swap_x(after(weight, acts_side))
    x_one = swap_x(after(w_one, gots[0], x_own, keeps[1]))
    x_two = swap_x(after(w_two, keeps[0]))
    x_three = swap_x(after(w_three, keeps[2], x_two))
    w_peer = [x_own, x_one, x_two, x_three]

    sums = forward_and_input(
        acts, w_mine[:3], w_peer[:3], out_grad, block_mask, where, 0, None
    )
    outputs, gx = forward_and_input(
        acts, w_mine[3:], w_peer[3:], out_grad, block_mask, where, 3, sums
    )

    by = after(gx, gots[1], gots[2]).reshape(2, 2, tokens, depth // 4)
    pair = lax.dynamic_index_in_dim(by, c, 1, keepdims=False) + swap_f(
        lax.dynamic_index_in_dim(by, 1 - c, 1, keepdims=False), 1
    )
    grad_x = lax.dynamic_index_in_dim(pair, y, 0, keepdims=False) + swap_f(
        lax.dynamic_index_in_dim(pair, 1 - y, 0, keepdims=False), 2
    )
    return (outputs, grad_w, grad_x.astype(BF16))


def solution(mesh):
    in_specs = (P("dp", None), P("dp", "fsdp"), P(), P(None, "dp", "fsdp"))
    out_specs = (P(None, "dp", "fsdp"), P("dp", "fsdp"), P("dp", "fsdp"))
    return jax.shard_map(
        on_device, mesh=mesh, in_specs=in_specs, out_specs=out_specs, check_vma=False
    )
```

```python
import jax
import jax.numpy as jnp
from jax import lax
from jax.experimental import pallas as pl
from jax.experimental.pallas import tpu as pltpu
from jax.sharding import PartitionSpec as P

BS = 256
TOK_G = 128
LANES = 128
F32 = jnp.float32
BF16 = jnp.bfloat16
PART_VMEM = 16 * 1024 * 1024
FORWARD_VMEM = 28 * 1024 * 1024


def plain(acts, weight, block_mask, out_grad):
    width = weight.shape[1]
    kblocks = block_mask.shape[1]
    oblocks = block_mask.shape[2]
    first_col = lax.axis_index("fsdp") * width
    col_ids = (first_col + jnp.arange(width, dtype=jnp.int32)) // BS
    col_select = (col_ids[None, :] == jnp.arange(oblocks, dtype=jnp.int32)[:, None]).astype(F32)
    col_mask = jnp.einsum("skb,bc->skc", block_mask.astype(F32), col_select)
    full = lax.all_gather(weight, "dp", axis=0, tiled=True)
    row_ids = jnp.arange(full.shape[0], dtype=jnp.int32) // BS
    row_select = (row_ids[:, None] == jnp.arange(kblocks, dtype=jnp.int32)[None, :]).astype(F32)
    mask = jnp.einsum("nk,skc->snc", row_select, col_mask)
    masked = mask.astype(BF16) * full[None]
    forward = jnp.einsum("tn,snc->stc", acts, masked, preferred_element_type=F32)
    input_part = jnp.einsum("stc,snc->tn", out_grad, masked, preferred_element_type=F32)
    products = jnp.einsum("tn,stc->snc", acts, out_grad, preferred_element_type=F32)
    grad_w = lax.psum_scatter(
        jnp.sum(mask * products, axis=0) * (1.0 / TOK_G), "dp", scatter_dimension=0, tiled=True
    )
    grad_x = lax.psum_scatter(input_part, "fsdp", scatter_dimension=1, tiled=True).astype(BF16)
    return (forward.astype(BF16), grad_w, grad_x)


def weight_grad_part(acts, og, block_mask, where, rows, chunk, chunks):
    nsub, tokens, width = og[0].shape
    flat = nsub * tokens
    ng = len(og)
    per = rows // LANES
    made = chunks * BS

    def kernel(where_ref, mask_ref, *refs):
        og_refs, outs, tiles = refs[ng : 2 * ng], refs[2 * ng : -1], refs[-1]
        z, x = where_ref[0], where_ref[1]
        step = pl.program_id(0)
        col = where_ref[2] + chunk + step

        @pl.when(step == 0)
        def _():
            acts_ref, one_ref, side_ref, both_ref = refs[:ng]
            for r in range(2):
                for g in range(per):
                    start = ((z ^ (2 * r)) * 2 + x) * rows + g * LANES
                    here = pl.ds(pl.multiple_of(start, LANES), LANES)
                    there = pl.ds(pl.multiple_of(x * rows + g * LANES, LANES), LANES)
                    dst = slice((r * per + g) * LANES, (r * per + g + 1) * LANES)
                    tiles[0, dst, :] = acts_ref[:, here].T
                    tiles[1, dst, :] = one_ref[r, :, there].T
                    tiles[2, dst, :] = side_ref[:, dst].T
                    tiles[3, dst, :] = both_ref[:, dst].T

        rhs = [ref[...].reshape(flat, BS) for ref in og_refs]
        for r in range(2):
            for g in range(per):
                block = (((z ^ (2 * r)) * 2 + x) * rows + g * LANES) // BS
                dst = slice((r * per + g) * LANES, (r * per + g + 1) * LANES)
                keep = [mask_ref[s, block, col].astype(F32) for s in range(nsub)]
                keep = [jnp.full((LANES, tokens), k).astype(BF16) for k in keep]
                total = None
                for k in range(ng):
                    t = tiles[k, dst, :]
                    lhs = jnp.concatenate([t * m for m in keep], axis=1)
                    term = jnp.dot(lhs, rhs[k], preferred_element_type=F32)
                    total = term if total is None else total + term
                outs[r][g * LANES : (g + 1) * LANES, :] = total * (1.0 / TOK_G)

    smem = pl.BlockSpec(memory_space=pltpu.SMEM)
    out = pl.BlockSpec((rows, BS), lambda j: (0, j))
    return pl.pallas_call(
        kernel,
        grid=(chunks,),
        out_shape=(jax.ShapeDtypeStruct((rows, made), F32),) * 2,
        in_specs=[smem, smem]
        + [pl.BlockSpec(a.shape, lambda j, n=a.ndim: (0,) * n) for a in acts]
        + [pl.BlockSpec((nsub, tokens, BS), lambda j: (0, 0, chunk + j))] * ng,
        out_specs=(out, out),
        scratch_shapes=[pltpu.VMEM((ng, 2 * rows, tokens), BF16)],
        compiler_params=pltpu.CompilerParams(vmem_limit_bytes=PART_VMEM),
        cost_estimate=pl.CostEstimate(
            flops=4 * ng * rows * made * flat, bytes_accessed=8 * rows * made, transcendentals=0
        ),
        name="weight_grad_part",
    )(where, block_mask, *acts, *og)


def forward_and_input(acts, w_mine, w_peer, og, block_mask, where, first, out_before=None, gx_before=None):
    nsub, tokens, width = og.shape
    depth = acts.shape[1]
    nz = len(w_mine)
    owners = depth // (2 * w_mine[0].shape[0])
    started = out_before is None and gx_before is None
    outs = started or out_before is not None
    gxs = started or gx_before is not None
    rows = w_mine[0].shape[0]
    per = rows // LANES
    two = BS // LANES

    def kernel(where_ref, mask_ref, acts_ref, og_ref, *rest):
        w_refs, rest = rest[: 2 * nz], rest[2 * nz :]
        acc, hilo = rest[-2:]
        out_ref = rest[-3 - gxs]
        gx_ref = rest[-3]
        z, x = where_ref[0], where_ref[1]
        step = pl.program_id(0)
        col = where_ref[2] + step

        if gxs:

            @pl.when(step == 0)
            def _():
                gx_ref[...] = jnp.zeros_like(gx_ref) if started else rest[0][...]

        if outs:
            acc[...] = jnp.zeros_like(acc) if started else rest[0][...]
        for k in range(nz):
            owner = z ^ (first + k)
            tiles = []
            for side in range(2):
                for g in range(per):
                    at = slice(g * LANES, (g + 1) * LANES)
                    tiles.append(jnp.where(x == side, w_refs[k][at, :], w_refs[nz + k][at, :]))
            for b in range(2 * per // two):
                block = owner * (2 * per // two) + b
                w = jnp.concatenate(tiles[b * two : (b + 1) * two])
                cols = pl.ds(pl.multiple_of(block * BS, BS), BS)
                if outs:
                    prod = jnp.dot(acts_ref[:, cols], w, preferred_element_type=F32)
                    for s in range(nsub):
                        acc[s] += mask_ref[s, block, col].astype(F32) * prod
                if not gxs:
                    continue
                total = jnp.zeros((tokens, BS), F32)
                for s in range(nsub):
                    total = total + mask_ref[s, block, col].astype(F32) * og_ref[s].astype(F32)
                hi = total.astype(BF16)
                hilo[:tokens] = hi
                hilo[tokens:] = (total - hi.astype(F32)).astype(BF16)
                both = lax.dot_general(
                    hilo[...], w, (((1,), (1,)), ((), ())), preferred_element_type=F32
                )
                gx_ref[owner, :, b * BS : (b + 1) * BS] += both[:tokens] + both[tokens:]
        if outs:
            out_ref[...] = acc[...].astype(out_ref.dtype)

    smem = pl.BlockSpec(memory_space=pltpu.SMEM)
    by_col = pl.BlockSpec((nsub, tokens, BS), lambda j: (0, 0, j))
    whole = pl.BlockSpec((tokens, depth), lambda j: (0, 0))
    by_owner = (owners, tokens, depth // owners)
    gx_spec = pl.BlockSpec(by_owner, lambda j: (0, 0, 0))
    return pl.pallas_call(
        kernel,
        grid=(width // BS,),
        out_shape=[jax.ShapeDtypeStruct((nsub, tokens, width), F32 if started else BF16)] * outs
        + [jax.ShapeDtypeStruct(by_owner, F32)] * gxs,
        in_specs=[smem, smem, whole, by_col]
        + [pl.BlockSpec((rows, BS), lambda j: (0, j))] * (2 * nz)
        + ([] if started else [by_col] * outs + [gx_spec] * gxs),
        out_specs=[by_col] * outs + [gx_spec] * gxs,
        scratch_shapes=[
            pltpu.VMEM((nsub, tokens, BS), F32),
            pltpu.VMEM((2 * tokens, BS), BF16),
        ],
        compiler_params=pltpu.CompilerParams(vmem_limit_bytes=FORWARD_VMEM),
        cost_estimate=pl.CostEstimate(
            flops=72 * tokens * nz * rows * width,
            bytes_accessed=8 * nz * rows * width,
            transcendentals=0,
        ),
        name="forward_and_input",
    )(where, block_mask, acts, og, *w_mine, *w_peer, *[a for a in (out_before, gx_before) if a is not None])


def on_device(acts, weight, block_mask, out_grad):
    rows, width = weight.shape
    tokens, depth = acts.shape
    dp = lax.axis_size("dp")
    fsdp = lax.axis_size("fsdp")
    if rows != 3 * LANES or width != 3 * BS or dp != 8 or fsdp != 4 or tokens != LANES:
        return plain(acts, weight, block_mask, out_grad)
    nx = 2
    me = lax.axis_index("dp")
    z, x = me // nx, me % nx
    f = lax.axis_index("fsdp")
    y, c = f // 2, f % 2
    where = jnp.stack([z, x, f * (width // BS), c]).astype(jnp.int32)

    def swap_dp(a, bits):
        return lax.ppermute(a, "dp", [(d, d ^ bits) for d in range(dp)])

    def swap_x(a):
        return swap_dp(a, 1)

    def swap_z(a, k):
        return swap_dp(a, k * nx)

    def swap_f(a, bit):
        return lax.ppermute(a, "fsdp", [(d, d ^ bit) for d in range(fsdp)])

    def after(a, *others):
        return lax.optimization_barrier((a, *others))[0]

    og_one = swap_z(out_grad, 1)
    og_side = swap_x(out_grad)
    og_both = swap_x(after(og_one, og_side))

    def acts_of(a, first, count):
        return lax.dynamic_slice_in_dim(a, first * rows, count * rows, 1)

    acts_one = swap_z(jnp.stack([acts_of(acts, (z ^ k) * nx, nx) for k in (1, 3)]), 1)
    acts_side = swap_x(
        jnp.concatenate([acts_of(acts, (z ^ k) * nx + 1 - x, 1) for k in (0, 2)], axis=1)
    )
    passed = after(acts_one, acts_side)
    acts_both = swap_x(jnp.concatenate([acts_of(passed[r], 1 - x, 1) for r in range(2)], axis=1))

    w_two = swap_z(weight, 2)
    w_one = swap_z(weight, 1)
    og = [out_grad, og_one, og_side, og_both]
    acts_all = [acts, acts_one, acts_side, acts_both]
    keeps, gots = [], []
    for j, count in ((0, 1), (1, width // BS - 1)):
        keep, send = weight_grad_part(acts_all, og, block_mask, where, rows, j, count)
        keeps.append(keep)
        gots.append(swap_z(send, 2))
    grad_w = jnp.concatenate([k + g for k, g in zip(keeps, gots)], axis=1)
    w_three = swap_z(after(w_two, keeps[0]), 1)
    w_mine = [weight, w_one, w_two, w_three]
    x_own = swap_x(after(weight, acts_side))
    x_one = swap_x(after(w_one, gots[0], x_own, keeps[1]))
    x_two = swap_x(after(w_two, keeps[0]))
    x_three = swap_x(after(w_three, keeps[1], x_two))
    w_peer = [x_own, x_one, x_two, x_three]

    part, gx = forward_and_input(acts, w_mine[:3], w_peer[:3], out_grad, block_mask, where, 0)
    last = (acts, w_mine[3:], w_peer[3:], out_grad, block_mask, where, 3)
    (gx,) = forward_and_input(*last, gx_before=gx)
    (outputs,) = forward_and_input(*last, out_before=part)

    by = after(gx, gots[1]).reshape(2, 2, tokens, depth // 4)
    pair = lax.dynamic_index_in_dim(by, c, 1, keepdims=False) + swap_f(
        lax.dynamic_index_in_dim(by, 1 - c, 1, keepdims=False), 1
    )
    grad_x = lax.dynamic_index_in_dim(pair, y, 0, keepdims=False) + swap_f(
        lax.dynamic_index_in_dim(pair, 1 - y, 0, keepdims=False), 2
    )
    return (outputs, grad_w, grad_x.astype(BF16))


def solution(mesh):
    in_specs = (P("dp", None), P("dp", "fsdp"), P(), P(None, "dp", "fsdp"))
    out_specs = (P(None, "dp", "fsdp"), P("dp", "fsdp"), P("dp", "fsdp"))
    return jax.shard_map(
        on_device, mesh=mesh, in_specs=in_specs, out_specs=out_specs, check_vma=False
    )
```

```python
import jax
import jax.numpy as jnp
from jax import lax
from jax.experimental import pallas as pl
from jax.experimental.pallas import tpu as pltpu
from jax.sharding import PartitionSpec as P

BS = 256
TOK_G = 128
LANES = 128
F32 = jnp.float32
BF16 = jnp.bfloat16
PART_VMEM = 16 * 1024 * 1024
FORWARD_VMEM = 28 * 1024 * 1024


def plain(acts, weight, block_mask, out_grad):
    width = weight.shape[1]
    kblocks = block_mask.shape[1]
    oblocks = block_mask.shape[2]
    first_col = lax.axis_index("fsdp") * width
    col_ids = (first_col + jnp.arange(width, dtype=jnp.int32)) // BS
    col_select = (col_ids[None, :] == jnp.arange(oblocks, dtype=jnp.int32)[:, None]).astype(F32)
    col_mask = jnp.einsum("skb,bc->skc", block_mask.astype(F32), col_select)
    full = lax.all_gather(weight, "dp", axis=0, tiled=True)
    row_ids = jnp.arange(full.shape[0], dtype=jnp.int32) // BS
    row_select = (row_ids[:, None] == jnp.arange(kblocks, dtype=jnp.int32)[None, :]).astype(F32)
    mask = jnp.einsum("nk,skc->snc", row_select, col_mask)
    masked = mask.astype(BF16) * full[None]
    forward = jnp.einsum("tn,snc->stc", acts, masked, preferred_element_type=F32)
    input_part = jnp.einsum("stc,snc->tn", out_grad, masked, preferred_element_type=F32)
    products = jnp.einsum("tn,stc->snc", acts, out_grad, preferred_element_type=F32)
    grad_w = lax.psum_scatter(
        jnp.sum(mask * products, axis=0) * (1.0 / TOK_G), "dp", scatter_dimension=0, tiled=True
    )
    grad_x = lax.psum_scatter(input_part, "fsdp", scatter_dimension=1, tiled=True).astype(BF16)
    return (forward.astype(BF16), grad_w, grad_x)


def weight_grad_part(acts, og, block_mask, where, rows, chunk, chunks):
    nsub, tokens, width = og[0].shape
    flat = nsub * tokens
    ng = len(og)
    per = rows // LANES
    made = chunks * BS

    def kernel(where_ref, mask_ref, *refs):
        og_refs, outs, tiles = refs[ng : 2 * ng], refs[2 * ng : -1], refs[-1]
        z, x = where_ref[0], where_ref[1]
        step = pl.program_id(0)
        col = where_ref[2] + chunk + step

        @pl.when(step == 0)
        def _():
            acts_ref, one_ref, side_ref, both_ref = refs[:ng]
            for r in range(2):
                for g in range(per):
                    start = ((z ^ (2 * r)) * 2 + x) * rows + g * LANES
                    here = pl.ds(pl.multiple_of(start, LANES), LANES)
                    there = pl.ds(pl.multiple_of(x * rows + g * LANES, LANES), LANES)
                    dst = slice((r * per + g) * LANES, (r * per + g + 1) * LANES)
                    tiles[0, dst, :] = acts_ref[:, here].T
                    tiles[1, dst, :] = one_ref[r, :, there].T
                    tiles[2, dst, :] = side_ref[:, dst].T
                    tiles[3, dst, :] = both_ref[:, dst].T

        rhs = [ref[...].reshape(flat, BS) for ref in og_refs]
        for r in range(2):
            for g in range(per):
                block = (((z ^ (2 * r)) * 2 + x) * rows + g * LANES) // BS
                dst = slice((r * per + g) * LANES, (r * per + g + 1) * LANES)
                keep = [mask_ref[s, block, col].astype(F32) for s in range(nsub)]
                keep = [jnp.full((LANES, tokens), k).astype(BF16) for k in keep]
                total = None
                for k in range(ng):
                    t = tiles[k, dst, :]
                    lhs = jnp.concatenate([t * m for m in keep], axis=1)
                    term = jnp.dot(lhs, rhs[k], preferred_element_type=F32)
                    total = term if total is None else total + term
                outs[r][g * LANES : (g + 1) * LANES, :] = total * (1.0 / TOK_G)

    smem = pl.BlockSpec(memory_space=pltpu.SMEM)
    out = pl.BlockSpec((rows, BS), lambda j: (0, j))
    return pl.pallas_call(
        kernel,
        grid=(chunks,),
        out_shape=(jax.ShapeDtypeStruct((rows, made), F32),) * 2,
        in_specs=[smem, smem]
        + [pl.BlockSpec(a.shape, lambda j, n=a.ndim: (0,) * n) for a in acts]
        + [pl.BlockSpec((nsub, tokens, BS), lambda j: (0, 0, chunk + j))] * ng,
        out_specs=(out, out),
        scratch_shapes=[pltpu.VMEM((ng, 2 * rows, tokens), BF16)],
        compiler_params=pltpu.CompilerParams(vmem_limit_bytes=PART_VMEM),
        cost_estimate=pl.CostEstimate(
            flops=4 * ng * rows * made * flat, bytes_accessed=8 * rows * made, transcendentals=0
        ),
        name="weight_grad_part",
    )(where, block_mask, *acts, *og)


def forward_and_input(acts, w_mine, w_peer, og, block_mask, where, first, out_before=None, gx_before=None):
    nsub, tokens, width = og.shape
    depth = acts.shape[1]
    nz = len(w_mine)
    owners = depth // (2 * w_mine[0].shape[0])
    started = out_before is None and gx_before is None
    outs = started or out_before is not None
    gxs = started or gx_before is not None
    rows = w_mine[0].shape[0]
    per = rows // LANES
    two = BS // LANES

    def kernel(where_ref, mask_ref, acts_ref, og_ref, *rest):
        w_refs, rest = rest[: 2 * nz], rest[2 * nz :]
        acc, hilo = rest[-2:]
        out_ref = rest[-3 - gxs]
        gx_ref = rest[-3]
        z, x = where_ref[0], where_ref[1]
        step = pl.program_id(0)
        col = where_ref[2] + step

        if gxs:

            @pl.when(step == 0)
            def _():
                gx_ref[...] = jnp.zeros_like(gx_ref) if started else rest[0][...]

        if outs:
            acc[...] = jnp.zeros_like(acc) if started else rest[0][...]
        for k in range(nz):
            owner = z ^ (first + k)
            tiles = []
            for side in range(2):
                for g in range(per):
                    at = slice(g * LANES, (g + 1) * LANES)
                    tiles.append(jnp.where(x == side, w_refs[k][at, :], w_refs[nz + k][at, :]))
            for b in range(2 * per // two):
                block = owner * (2 * per // two) + b
                w = jnp.concatenate(tiles[b * two : (b + 1) * two])
                cols = pl.ds(pl.multiple_of(block * BS, BS), BS)
                if outs:
                    prod = jnp.dot(acts_ref[:, cols], w, preferred_element_type=F32)
                    for s in range(nsub):
                        acc[s] += mask_ref[s, block, col].astype(F32) * prod
                if not gxs:
                    continue
                total = jnp.zeros((tokens, BS), F32)
                for s in range(nsub):
                    total = total + mask_ref[s, block, col].astype(F32) * og_ref[s].astype(F32)
                hi = total.astype(BF16)
                hilo[:tokens] = hi
                hilo[tokens:] = (total - hi.astype(F32)).astype(BF16)
                both = lax.dot_general(
                    hilo[...], w, (((1,), (1,)), ((), ())), preferred_element_type=F32
                )
                gx_ref[owner, :, b * BS : (b + 1) * BS] += both[:tokens] + both[tokens:]
        if outs:
            out_ref[...] = acc[...].astype(out_ref.dtype)

    smem = pl.BlockSpec(memory_space=pltpu.SMEM)
    by_col = pl.BlockSpec((nsub, tokens, BS), lambda j: (0, 0, j))
    whole = pl.BlockSpec((tokens, depth), lambda j: (0, 0))
    by_owner = (owners, tokens, depth // owners)
    gx_spec = pl.BlockSpec(by_owner, lambda j: (0, 0, 0))
    return pl.pallas_call(
        kernel,
        grid=(width // BS,),
        out_shape=[jax.ShapeDtypeStruct((nsub, tokens, width), F32 if started else BF16)] * outs
        + [jax.ShapeDtypeStruct(by_owner, F32)] * gxs,
        in_specs=[smem, smem, whole, by_col]
        + [pl.BlockSpec((rows, BS), lambda j: (0, j))] * (2 * nz)
        + ([] if started else [by_col] * outs + [gx_spec] * gxs),
        out_specs=[by_col] * outs + [gx_spec] * gxs,
        scratch_shapes=[
            pltpu.VMEM((nsub, tokens, BS), F32),
            pltpu.VMEM((2 * tokens, BS), BF16),
        ],
        compiler_params=pltpu.CompilerParams(vmem_limit_bytes=FORWARD_VMEM),
        cost_estimate=pl.CostEstimate(
            flops=72 * tokens * nz * rows * width,
            bytes_accessed=8 * nz * rows * width,
            transcendentals=0,
        ),
        name="forward_and_input",
    )(where, block_mask, acts, og, *w_mine, *w_peer, *[a for a in (out_before, gx_before) if a is not None])


def on_device(acts, weight, block_mask, out_grad):
    rows, width = weight.shape
    tokens, depth = acts.shape
    dp = lax.axis_size("dp")
    fsdp = lax.axis_size("fsdp")
    if rows != 3 * LANES or width != 3 * BS or dp != 8 or fsdp != 4 or tokens != LANES:
        return plain(acts, weight, block_mask, out_grad)
    nx = 2
    me = lax.axis_index("dp")
    z, x = me // nx, me % nx
    f = lax.axis_index("fsdp")
    y, c = f // 2, f % 2
    where = jnp.stack([z, x, f * (width // BS), c]).astype(jnp.int32)

    def swap_dp(a, bits):
        return lax.ppermute(a, "dp", [(d, d ^ bits) for d in range(dp)])

    def swap_x(a):
        return swap_dp(a, 1)

    def swap_z(a, k):
        return swap_dp(a, k * nx)

    def swap_f(a, bit):
        return lax.ppermute(a, "fsdp", [(d, d ^ bit) for d in range(fsdp)])

    def after(a, *others):
        return lax.optimization_barrier((a, *others))[0]

    og_one = swap_z(out_grad, 1)
    og_side = swap_x(out_grad)
    og_both = swap_x(after(og_one, og_side))

    def acts_of(a, first, count):
        return lax.dynamic_slice_in_dim(a, first * rows, count * rows, 1)

    acts_one = swap_z(jnp.stack([acts_of(acts, (z ^ k) * nx, nx) for k in (1, 3)]), 1)
    acts_side = swap_x(
        jnp.concatenate([acts_of(acts, (z ^ k) * nx + 1 - x, 1) for k in (0, 2)], axis=1)
    )
    passed = after(acts_one, acts_side)
    acts_both = swap_x(jnp.concatenate([acts_of(passed[r], 1 - x, 1) for r in range(2)], axis=1))

    w_two = swap_z(weight, 2)
    w_one = swap_z(weight, 1)
    og = [out_grad, og_one, og_side, og_both]
    acts_all = [acts, acts_one, acts_side, acts_both]
    keeps, gots = [], []
    for j, count in ((0, 1), (1, width // BS - 1)):
        keep, send = weight_grad_part(acts_all, og, block_mask, where, rows, j, count)
        keeps.append(keep)
        gots.append(swap_z(send, 2))
    grad_w = jnp.concatenate([k + g for k, g in zip(keeps, gots)], axis=1)
    w_three = swap_z(after(w_two, keeps[0]), 1)
    w_mine = [weight, w_one, w_two, w_three]
    x_own = swap_x(after(weight, acts_side))
    x_one = swap_x(after(w_one, gots[0], x_own, keeps[1]))
    x_two = swap_x(after(w_two, keeps[0]))
    x_three = swap_x(after(w_three, keeps[1], x_two))
    w_peer = [x_own, x_one, x_two, x_three]

    part, gx = forward_and_input(acts, w_mine[:3], w_peer[:3], out_grad, block_mask, where, 0)
    last = (acts, w_mine[3:], w_peer[3:], out_grad, block_mask, where, 3)
    (gx,) = forward_and_input(*last, gx_before=gx)
    (outputs,) = forward_and_input(*last, out_before=part)

    by = gx.reshape(2, 2, tokens, depth // 4)
    pair = lax.dynamic_index_in_dim(by, c, 1, keepdims=False) + swap_f(
        lax.dynamic_index_in_dim(by, 1 - c, 1, keepdims=False), 1
    )
    pair = after(pair, gots[1])
    grad_x = lax.dynamic_index_in_dim(pair, y, 0, keepdims=False) + swap_f(
        lax.dynamic_index_in_dim(pair, 1 - y, 0, keepdims=False), 2
    )
    return (outputs, grad_w, grad_x.astype(BF16))


def solution(mesh):
    in_specs = (P("dp", None), P("dp", "fsdp"), P(), P(None, "dp", "fsdp"))
    out_specs = (P(None, "dp", "fsdp"), P("dp", "fsdp"), P("dp", "fsdp"))
    return jax.shard_map(
        on_device, mesh=mesh, in_specs=in_specs, out_specs=out_specs, check_vma=False
    )
```

```python
import jax
import jax.numpy as jnp
from jax import lax
from jax.experimental import pallas as pl
from jax.experimental.pallas import tpu as pltpu
from jax.sharding import PartitionSpec as P

BS = 256
TOK_G = 128
LANES = 128
F32 = jnp.float32
BF16 = jnp.bfloat16
PART_VMEM = 48 * 1024 * 1024
FORWARD_VMEM = 48 * 1024 * 1024


def plain(acts, weight, block_mask, out_grad):
    width = weight.shape[1]
    kblocks = block_mask.shape[1]
    oblocks = block_mask.shape[2]
    first_col = lax.axis_index("fsdp") * width
    col_ids = (first_col + jnp.arange(width, dtype=jnp.int32)) // BS
    col_select = (col_ids[None, :] == jnp.arange(oblocks, dtype=jnp.int32)[:, None]).astype(F32)
    col_mask = jnp.einsum("skb,bc->skc", block_mask.astype(F32), col_select)
    full = lax.all_gather(weight, "dp", axis=0, tiled=True)
    row_ids = jnp.arange(full.shape[0], dtype=jnp.int32) // BS
    row_select = (row_ids[:, None] == jnp.arange(kblocks, dtype=jnp.int32)[None, :]).astype(F32)
    mask = jnp.einsum("nk,skc->snc", row_select, col_mask)
    masked = mask.astype(BF16) * full[None]
    forward = jnp.einsum("tn,snc->stc", acts, masked, preferred_element_type=F32)
    input_part = jnp.einsum("stc,snc->tn", out_grad, masked, preferred_element_type=F32)
    products = jnp.einsum("tn,stc->snc", acts, out_grad, preferred_element_type=F32)
    grad_w = lax.psum_scatter(
        jnp.sum(mask * products, axis=0) * (1.0 / TOK_G), "dp", scatter_dimension=0, tiled=True
    )
    grad_x = lax.psum_scatter(input_part, "fsdp", scatter_dimension=1, tiled=True).astype(BF16)
    return (forward.astype(BF16), grad_w, grad_x)


def weight_grad_part(acts, og, block_mask, where, rows, chunk, chunks):
    nsub, tokens, width = og[0].shape
    flat = nsub * tokens
    ng = len(og)
    per = rows // LANES
    made = chunks * BS

    def kernel(where_ref, mask_ref, *refs):
        og_refs, outs, tiles = refs[ng : 2 * ng], refs[2 * ng : -1], refs[-1]
        z, x = where_ref[0], where_ref[1]
        step = pl.program_id(0)
        col = where_ref[2] + chunk + step

        @pl.when(step == 0)
        def _():
            acts_ref, one_ref, side_ref, both_ref = refs[:ng]
            for r in range(2):
                for g in range(per):
                    start = ((z ^ (2 * r)) * 2 + x) * rows + g * LANES
                    here = pl.ds(pl.multiple_of(start, LANES), LANES)
                    there = pl.ds(pl.multiple_of(x * rows + g * LANES, LANES), LANES)
                    dst = slice((r * per + g) * LANES, (r * per + g + 1) * LANES)
                    tiles[0, dst, :] = acts_ref[:, here].T
                    tiles[1, dst, :] = one_ref[r, :, there].T
                    tiles[2, dst, :] = side_ref[:, dst].T
                    tiles[3, dst, :] = both_ref[:, dst].T

        rhs = [ref[...].reshape(flat, BS) for ref in og_refs]
        for r in range(2):
            for g in range(per):
                block = (((z ^ (2 * r)) * 2 + x) * rows + g * LANES) // BS
                dst = slice((r * per + g) * LANES, (r * per + g + 1) * LANES)
                keep = [mask_ref[s, block, col].astype(F32) for s in range(nsub)]
                keep = [jnp.full((LANES, tokens), k).astype(BF16) for k in keep]
                total = None
                for k in range(ng):
                    t = tiles[k, dst, :]
                    lhs = jnp.concatenate([t * m for m in keep], axis=1)
                    term = jnp.dot(lhs, rhs[k], preferred_element_type=F32)
                    total = term if total is None else total + term
                outs[r][g * LANES : (g + 1) * LANES, :] = total * (1.0 / TOK_G)

    smem = pl.BlockSpec(memory_space=pltpu.SMEM)
    out = pl.BlockSpec((rows, BS), lambda j: (0, j))
    return pl.pallas_call(
        kernel,
        grid=(chunks,),
        out_shape=(jax.ShapeDtypeStruct((rows, made), F32),) * 2,
        in_specs=[smem, smem]
        + [pl.BlockSpec(a.shape, lambda j, n=a.ndim: (0,) * n) for a in acts]
        + [pl.BlockSpec((nsub, tokens, BS), lambda j: (0, 0, chunk + j))] * ng,
        out_specs=(out, out),
        scratch_shapes=[pltpu.VMEM((ng, 2 * rows, tokens), BF16)],
        compiler_params=pltpu.CompilerParams(vmem_limit_bytes=PART_VMEM),
        cost_estimate=pl.CostEstimate(
            flops=4 * ng * rows * made * flat, bytes_accessed=8 * rows * made, transcendentals=0
        ),
        name="weight_grad_part",
    )(where, block_mask, *acts, *og)


def forward_and_input(acts, w_mine, w_peer, og, block_mask, where, first, out_before=None, gx_before=None):
    nsub, tokens, width = og.shape
    depth = acts.shape[1]
    nz = len(w_mine)
    owners = depth // (2 * w_mine[0].shape[0])
    started = out_before is None and gx_before is None
    outs = started or out_before is not None
    gxs = started or gx_before is not None
    rows = w_mine[0].shape[0]
    per = rows // LANES
    two = BS // LANES

    def kernel(where_ref, mask_ref, acts_ref, og_ref, *rest):
        w_refs, rest = rest[: 2 * nz], rest[2 * nz :]
        acc, hilo = rest[-2:]
        out_ref = rest[-3 - gxs]
        gx_ref = rest[-3]
        z, x = where_ref[0], where_ref[1]
        step = pl.program_id(0)
        col = where_ref[2] + step

        if gxs:

            @pl.when(step == 0)
            def _():
                gx_ref[...] = jnp.zeros_like(gx_ref) if started else rest[0][...]

        if outs:
            acc[...] = jnp.zeros_like(acc) if started else rest[0][...]
        for k in range(nz):
            owner = z ^ (first + k)
            tiles = []
            for side in range(2):
                for g in range(per):
                    at = slice(g * LANES, (g + 1) * LANES)
                    tiles.append(jnp.where(x == side, w_refs[k][at, :], w_refs[nz + k][at, :]))
            for b in range(2 * per // two):
                block = owner * (2 * per // two) + b
                w = jnp.concatenate(tiles[b * two : (b + 1) * two])
                cols = pl.ds(pl.multiple_of(block * BS, BS), BS)
                if outs:
                    prod = jnp.dot(acts_ref[:, cols], w, preferred_element_type=F32)
                    for s in range(nsub):
                        acc[s] += mask_ref[s, block, col].astype(F32) * prod
                if not gxs:
                    continue
                total = jnp.zeros((tokens, BS), F32)
                for s in range(nsub):
                    total = total + mask_ref[s, block, col].astype(F32) * og_ref[s].astype(F32)
                hi = total.astype(BF16)
                hilo[:tokens] = hi
                hilo[tokens:] = (total - hi.astype(F32)).astype(BF16)
                both = lax.dot_general(
                    hilo[...], w, (((1,), (1,)), ((), ())), preferred_element_type=F32
                )
                gx_ref[owner, :, b * BS : (b + 1) * BS] += both[:tokens] + both[tokens:]
        if outs:
            out_ref[...] = acc[...].astype(out_ref.dtype)

    smem = pl.BlockSpec(memory_space=pltpu.SMEM)
    by_col = pl.BlockSpec((nsub, tokens, BS), lambda j: (0, 0, j))
    whole = pl.BlockSpec((tokens, depth), lambda j: (0, 0))
    by_owner = (owners, tokens, depth // owners)
    gx_spec = pl.BlockSpec(by_owner, lambda j: (0, 0, 0))
    return pl.pallas_call(
        kernel,
        grid=(width // BS,),
        out_shape=[jax.ShapeDtypeStruct((nsub, tokens, width), F32 if started else BF16)] * outs
        + [jax.ShapeDtypeStruct(by_owner, F32)] * gxs,
        in_specs=[smem, smem, whole, by_col]
        + [pl.BlockSpec((rows, BS), lambda j: (0, j))] * (2 * nz)
        + ([] if started else [by_col] * outs + [gx_spec] * gxs),
        out_specs=[by_col] * outs + [gx_spec] * gxs,
        scratch_shapes=[
            pltpu.VMEM((nsub, tokens, BS), F32),
            pltpu.VMEM((2 * tokens, BS), BF16),
        ],
        compiler_params=pltpu.CompilerParams(vmem_limit_bytes=FORWARD_VMEM),
        cost_estimate=pl.CostEstimate(
            flops=72 * tokens * nz * rows * width,
            bytes_accessed=8 * nz * rows * width,
            transcendentals=0,
        ),
        name="forward_and_input",
    )(where, block_mask, acts, og, *w_mine, *w_peer, *[a for a in (out_before, gx_before) if a is not None])


def on_device(acts, weight, block_mask, out_grad):
    rows, width = weight.shape
    tokens, depth = acts.shape
    dp = lax.axis_size("dp")
    fsdp = lax.axis_size("fsdp")
    if rows != 3 * LANES or width != 3 * BS or dp != 8 or fsdp != 4 or tokens != LANES:
        return plain(acts, weight, block_mask, out_grad)
    nx = 2
    me = lax.axis_index("dp")
    z, x = me // nx, me % nx
    f = lax.axis_index("fsdp")
    y, c = f // 2, f % 2
    where = jnp.stack([z, x, f * (width // BS), c]).astype(jnp.int32)

    def swap_dp(a, bits):
        return lax.ppermute(a, "dp", [(d, d ^ bits) for d in range(dp)])

    def swap_x(a):
        return swap_dp(a, 1)

    def swap_z(a, k):
        return swap_dp(a, k * nx)

    def swap_f(a, bit):
        return lax.ppermute(a, "fsdp", [(d, d ^ bit) for d in range(fsdp)])

    def after(a, *others):
        return lax.optimization_barrier((a, *others))[0]

    og_one = swap_z(out_grad, 1)
    og_side = swap_x(out_grad)
    og_both = swap_x(after(og_one, og_side))

    def acts_of(a, first, count):
        return lax.dynamic_slice_in_dim(a, first * rows, count * rows, 1)

    acts_one = swap_z(jnp.stack([acts_of(acts, (z ^ k) * nx, nx) for k in (1, 3)]), 1)
    acts_side = swap_x(
        jnp.concatenate([acts_of(acts, (z ^ k) * nx + 1 - x, 1) for k in (0, 2)], axis=1)
    )
    passed = after(acts_one, acts_side)
    acts_both = swap_x(jnp.concatenate([acts_of(passed[r], 1 - x, 1) for r in range(2)], axis=1))

    w_two = swap_z(weight, 2)
    w_one = swap_z(weight, 1)
    og = [out_grad, og_one, og_side, og_both]
    acts_all = [acts, acts_one, acts_side, acts_both]
    keeps, gots = [], []
    for j, count in ((0, 1), (1, width // BS - 1)):
        keep, send = weight_grad_part(acts_all, og, block_mask, where, rows, j, count)
        keeps.append(keep)
        gots.append(swap_z(send, 2))
    grad_w = jnp.concatenate([k + g for k, g in zip(keeps, gots)], axis=1)
    w_three = swap_z(after(w_two, keeps[0]), 1)
    w_mine = [weight, w_one, w_two, w_three]
    x_own = swap_x(after(weight, acts_side))
    x_one = swap_x(after(w_one, gots[0], x_own, keeps[1]))
    x_two = swap_x(after(w_two, keeps[0]))
    x_three = swap_x(after(w_three, keeps[1], x_two))
    w_peer = [x_own, x_one, x_two, x_three]

    part, gx = forward_and_input(acts, w_mine[:3], w_peer[:3], out_grad, block_mask, where, 0)
    last = (acts, w_mine[3:], w_peer[3:], out_grad, block_mask, where, 3)
    (gx,) = forward_and_input(*last, gx_before=gx)
    (outputs,) = forward_and_input(*last, out_before=part)

    by = gx.reshape(2, 2, tokens, depth // 4)
    pair = lax.dynamic_index_in_dim(by, c, 1, keepdims=False) + swap_f(
        lax.dynamic_index_in_dim(by, 1 - c, 1, keepdims=False), 1
    )
    pair = after(pair, gots[1])
    grad_x = lax.dynamic_index_in_dim(pair, y, 0, keepdims=False) + swap_f(
        lax.dynamic_index_in_dim(pair, 1 - y, 0, keepdims=False), 2
    )
    return (outputs, grad_w, grad_x.astype(BF16))


def solution(mesh):
    in_specs = (P("dp", None), P("dp", "fsdp"), P(), P(None, "dp", "fsdp"))
    out_specs = (P(None, "dp", "fsdp"), P("dp", "fsdp"), P("dp", "fsdp"))
    return jax.shard_map(
        on_device, mesh=mesh, in_specs=in_specs, out_specs=out_specs, check_vma=False
    )
```

```python
import jax
import jax.numpy as jnp
from jax import lax
from jax.experimental import pallas as pl
from jax.experimental.pallas import tpu as pltpu
from jax.sharding import PartitionSpec as P

BS = 256
TOK_G = 128
LANES = 128
F32 = jnp.float32
BF16 = jnp.bfloat16
PART_VMEM = 9 * 1024 * 1024
FORWARD_VMEM = 17 * 1024 * 1024


def plain(acts, weight, block_mask, out_grad):
    width = weight.shape[1]
    kblocks = block_mask.shape[1]
    oblocks = block_mask.shape[2]
    first_col = lax.axis_index("fsdp") * width
    col_ids = (first_col + jnp.arange(width, dtype=jnp.int32)) // BS
    col_select = (col_ids[None, :] == jnp.arange(oblocks, dtype=jnp.int32)[:, None]).astype(F32)
    col_mask = jnp.einsum("skb,bc->skc", block_mask.astype(F32), col_select)
    full = lax.all_gather(weight, "dp", axis=0, tiled=True)
    row_ids = jnp.arange(full.shape[0], dtype=jnp.int32) // BS
    row_select = (row_ids[:, None] == jnp.arange(kblocks, dtype=jnp.int32)[None, :]).astype(F32)
    mask = jnp.einsum("nk,skc->snc", row_select, col_mask)
    masked = mask.astype(BF16) * full[None]
    forward = jnp.einsum("tn,snc->stc", acts, masked, preferred_element_type=F32)
    input_part = jnp.einsum("stc,snc->tn", out_grad, masked, preferred_element_type=F32)
    products = jnp.einsum("tn,stc->snc", acts, out_grad, preferred_element_type=F32)
    grad_w = lax.psum_scatter(
        jnp.sum(mask * products, axis=0) * (1.0 / TOK_G), "dp", scatter_dimension=0, tiled=True
    )
    grad_x = lax.psum_scatter(input_part, "fsdp", scatter_dimension=1, tiled=True).astype(BF16)
    return (forward.astype(BF16), grad_w, grad_x)


def weight_grad_part(acts, og, block_mask, where, rows, chunk, chunks):
    nsub, tokens, width = og[0].shape
    flat = nsub * tokens
    ng = len(og)
    per = rows // LANES
    made = chunks * BS

    def kernel(where_ref, mask_ref, *refs):
        og_refs, outs, tiles = refs[ng : 2 * ng], refs[2 * ng : -1], refs[-1]
        z, x = where_ref[0], where_ref[1]
        step = pl.program_id(0)
        col = where_ref[2] + chunk + step

        @pl.when(step == 0)
        def _():
            acts_ref, one_ref, side_ref, both_ref = refs[:ng]
            for r in range(2):
                for g in range(per):
                    start = ((z ^ (2 * r)) * 2 + x) * rows + g * LANES
                    here = pl.ds(pl.multiple_of(start, LANES), LANES)
                    there = pl.ds(pl.multiple_of(x * rows + g * LANES, LANES), LANES)
                    dst = slice((r * per + g) * LANES, (r * per + g + 1) * LANES)
                    tiles[0, dst, :] = acts_ref[:, here].T
                    tiles[1, dst, :] = one_ref[r, :, there].T
                    tiles[2, dst, :] = side_ref[:, dst].T
                    tiles[3, dst, :] = both_ref[:, dst].T

        rhs = [ref[...].reshape(flat, BS) for ref in og_refs]
        for r in range(2):
            for g in range(per):
                block = (((z ^ (2 * r)) * 2 + x) * rows + g * LANES) // BS
                dst = slice((r * per + g) * LANES, (r * per + g + 1) * LANES)
                keep = [mask_ref[s, block, col].astype(F32) for s in range(nsub)]
                keep = [jnp.full((LANES, tokens), k).astype(BF16) for k in keep]
                total = None
                for k in range(ng):
                    t = tiles[k, dst, :]
                    lhs = jnp.concatenate([t * m for m in keep], axis=1)
                    term = jnp.dot(lhs, rhs[k], preferred_element_type=F32)
                    total = term if total is None else total + term
                outs[r][g * LANES : (g + 1) * LANES, :] = total * (1.0 / TOK_G)

    smem = pl.BlockSpec(memory_space=pltpu.SMEM)
    out = pl.BlockSpec((rows, BS), lambda j: (0, j))
    return pl.pallas_call(
        kernel,
        grid=(chunks,),
        out_shape=(jax.ShapeDtypeStruct((rows, made), F32),) * 2,
        in_specs=[smem, smem]
        + [pl.BlockSpec(a.shape, lambda j, n=a.ndim: (0,) * n) for a in acts]
        + [pl.BlockSpec((nsub, tokens, BS), lambda j: (0, 0, chunk + j))] * ng,
        out_specs=(out, out),
        scratch_shapes=[pltpu.VMEM((ng, 2 * rows, tokens), BF16)],
        compiler_params=pltpu.CompilerParams(vmem_limit_bytes=PART_VMEM),
        cost_estimate=pl.CostEstimate(
            flops=4 * ng * rows * made * flat, bytes_accessed=8 * rows * made, transcendentals=0
        ),
        name="weight_grad_part",
    )(where, block_mask, *acts, *og)


def forward_and_input(acts, w_mine, w_peer, og, block_mask, where, first, out_before=None, gx_before=None):
    nsub, tokens, width = og.shape
    depth = acts.shape[1]
    nz = len(w_mine)
    owners = depth // (2 * w_mine[0].shape[0])
    started = out_before is None and gx_before is None
    outs = started or out_before is not None
    gxs = started or gx_before is not None
    rows = w_mine[0].shape[0]
    per = rows // LANES
    two = BS // LANES

    def kernel(where_ref, mask_ref, acts_ref, og_ref, *rest):
        w_refs, rest = rest[: 2 * nz], rest[2 * nz :]
        acc, hilo = rest[-2:]
        out_ref = rest[-3 - gxs]
        gx_ref = rest[-3]
        z, x = where_ref[0], where_ref[1]
        step = pl.program_id(0)
        col = where_ref[2] + step

        if gxs:

            @pl.when(step == 0)
            def _():
                gx_ref[...] = jnp.zeros_like(gx_ref) if started else rest[0][...]

        if outs:
            acc[...] = jnp.zeros_like(acc) if started else rest[0][...]
        for k in range(nz):
            owner = z ^ (first + k)
            tiles = []
            for side in range(2):
                for g in range(per):
                    at = slice(g * LANES, (g + 1) * LANES)
                    tiles.append(jnp.where(x == side, w_refs[k][at, :], w_refs[nz + k][at, :]))
            for b in range(2 * per // two):
                block = owner * (2 * per // two) + b
                w = jnp.concatenate(tiles[b * two : (b + 1) * two])
                cols = pl.ds(pl.multiple_of(block * BS, BS), BS)
                if outs:
                    prod = jnp.dot(acts_ref[:, cols], w, preferred_element_type=F32)
                    for s in range(nsub):
                        acc[s] += mask_ref[s, block, col].astype(F32) * prod
                if not gxs:
                    continue
                total = jnp.zeros((tokens, BS), F32)
                for s in range(nsub):
                    total = total + mask_ref[s, block, col].astype(F32) * og_ref[s].astype(F32)
                hi = total.astype(BF16)
                hilo[:tokens] = hi
                hilo[tokens:] = (total - hi.astype(F32)).astype(BF16)
                both = lax.dot_general(
                    hilo[...], w, (((1,), (1,)), ((), ())), preferred_element_type=F32
                )
                gx_ref[owner, :, b * BS : (b + 1) * BS] += both[:tokens] + both[tokens:]
        if outs:
            out_ref[...] = acc[...].astype(out_ref.dtype)

    smem = pl.BlockSpec(memory_space=pltpu.SMEM)
    by_col = pl.BlockSpec((nsub, tokens, BS), lambda j: (0, 0, j))
    whole = pl.BlockSpec((tokens, depth), lambda j: (0, 0))
    by_owner = (owners, tokens, depth // owners)
    gx_spec = pl.BlockSpec(by_owner, lambda j: (0, 0, 0))
    return pl.pallas_call(
        kernel,
        grid=(width // BS,),
        out_shape=[jax.ShapeDtypeStruct((nsub, tokens, width), F32 if started else BF16)] * outs
        + [jax.ShapeDtypeStruct(by_owner, F32)] * gxs,
        in_specs=[smem, smem, whole, by_col]
        + [pl.BlockSpec((rows, BS), lambda j: (0, j))] * (2 * nz)
        + ([] if started else [by_col] * outs + [gx_spec] * gxs),
        out_specs=[by_col] * outs + [gx_spec] * gxs,
        scratch_shapes=[
            pltpu.VMEM((nsub, tokens, BS), F32),
            pltpu.VMEM((2 * tokens, BS), BF16),
        ],
        compiler_params=pltpu.CompilerParams(vmem_limit_bytes=FORWARD_VMEM),
        cost_estimate=pl.CostEstimate(
            flops=72 * tokens * nz * rows * width,
            bytes_accessed=8 * nz * rows * width,
            transcendentals=0,
        ),
        name="forward_and_input",
    )(where, block_mask, acts, og, *w_mine, *w_peer, *[a for a in (out_before, gx_before) if a is not None])


def on_device(acts, weight, block_mask, out_grad):
    rows, width = weight.shape
    tokens, depth = acts.shape
    dp = lax.axis_size("dp")
    fsdp = lax.axis_size("fsdp")
    if rows != 3 * LANES or width != 3 * BS or dp != 8 or fsdp != 4 or tokens != LANES:
        return plain(acts, weight, block_mask, out_grad)
    nx = 2
    me = lax.axis_index("dp")
    z, x = me // nx, me % nx
    f = lax.axis_index("fsdp")
    y, c = f // 2, f % 2
    where = jnp.stack([z, x, f * (width // BS), c]).astype(jnp.int32)

    def swap_dp(a, bits):
        return lax.ppermute(a, "dp", [(d, d ^ bits) for d in range(dp)])

    def swap_x(a):
        return swap_dp(a, 1)

    def swap_z(a, k):
        return swap_dp(a, k * nx)

    def swap_f(a, bit):
        return lax.ppermute(a, "fsdp", [(d, d ^ bit) for d in range(fsdp)])

    def after(a, *others):
        return lax.optimization_barrier((a, *others))[0]

    og_one = swap_z(out_grad, 1)
    og_side = swap_x(out_grad)
    og_both = swap_x(after(og_one, og_side))

    def acts_of(a, first, count):
        return lax.dynamic_slice_in_dim(a, first * rows, count * rows, 1)

    acts_one = swap_z(jnp.stack([acts_of(acts, (z ^ k) * nx, nx) for k in (1, 3)]), 1)
    acts_side = swap_x(
        jnp.concatenate([acts_of(acts, (z ^ k) * nx + 1 - x, 1) for k in (0, 2)], axis=1)
    )
    passed = after(acts_one, acts_side)
    acts_both = swap_x(jnp.concatenate([acts_of(passed[r], 1 - x, 1) for r in range(2)], axis=1))

    w_two = swap_z(weight, 2)
    w_one = swap_z(weight, 1)
    og = [out_grad, og_one, og_side, og_both]
    acts_all = [acts, acts_one, acts_side, acts_both]
    keeps, gots = [], []
    for j, count in ((0, 1), (1, width // BS - 1)):
        keep, send = weight_grad_part(acts_all, og, block_mask, where, rows, j, count)
        keeps.append(keep)
        gots.append(swap_z(send, 2))
    grad_w = jnp.concatenate([k + g for k, g in zip(keeps, gots)], axis=1)
    w_three = swap_z(after(w_two, keeps[0]), 1)
    w_mine = [weight, w_one, w_two, w_three]
    x_own = swap_x(after(weight, acts_side))
    x_one = swap_x(after(w_one, gots[0], x_own, keeps[1]))
    x_two = swap_x(after(w_two, keeps[0]))
    x_three = swap_x(after(w_three, keeps[1], x_two))
    w_peer = [x_own, x_one, x_two, x_three]

    part, gx = forward_and_input(acts, w_mine[:3], w_peer[:3], out_grad, block_mask, where, 0)
    last = (acts, w_mine[3:], w_peer[3:], out_grad, block_mask, where, 3)
    (gx,) = forward_and_input(*last, gx_before=gx)
    (outputs,) = forward_and_input(*last, out_before=part)

    by = gx.reshape(2, 2, tokens, depth // 4)
    pair = lax.dynamic_index_in_dim(by, c, 1, keepdims=False) + swap_f(
        lax.dynamic_index_in_dim(by, 1 - c, 1, keepdims=False), 1
    )
    pair = after(pair, gots[1])
    grad_x = lax.dynamic_index_in_dim(pair, y, 0, keepdims=False) + swap_f(
        lax.dynamic_index_in_dim(pair, 1 - y, 0, keepdims=False), 2
    )
    return (outputs, grad_w, grad_x.astype(BF16))


def solution(mesh):
    in_specs = (P("dp", None), P("dp", "fsdp"), P(), P(None, "dp", "fsdp"))
    out_specs = (P(None, "dp", "fsdp"), P("dp", "fsdp"), P("dp", "fsdp"))
    return jax.shard_map(
        on_device, mesh=mesh, in_specs=in_specs, out_specs=out_specs, check_vma=False
    )
```
